32 devices in a mesh: dp: 8 (over z, y), tensor: 4 (over x, core).
Axes of the slice: x: 2, y: 2, z: 4, core: 2. Of those that a mesh axis runs over, the one named last changes fastest.
Arguments:
- tokens: bfloat16 [8192, 768], P('dp'), may hold values from -6 to 6
- segment_ids: int32 [16, 512], P('dp'), may hold values from 0 to 3, never falling along the last dimension, each value on 1 to 256 neighbouring positions
- qkv_weight: bfloat16 [768, 3, 12, 64], P(None, None, 'tensor'), may hold values from -0.21875 to 0.21875
- qkv_bias: bfloat16 [2, 12, 64], P(None, 'tensor'), may hold values from -3 to 3
- output_weight: bfloat16 [12, 64, 768], P('tensor'), may hold values from -1.25 to 1.25
- output_bias: bfloat16 [768], replicated, may hold values from -2 to 2
- first_gain: bfloat16 [768], replicated, may hold values from 0.5 to 1.5
- first_shift: bfloat16 [768], replicated, may hold values from -2 to 2
- up_weight: bfloat16 [768, 3072], P(None, 'tensor'), may hold values from -0.21875 to 0.21875
- up_bias: bfloat16 [48, 64], P('tensor'), may hold values from -3 to 3
- down_weight: bfloat16 [3072, 768], P('tensor'), may hold values from -0.109375 to 0.109375
- down_bias: bfloat16 [768], replicated, may hold values from -2 to 2
- second_gain: bfloat16 [768], replicated, may hold values from 0.5 to 1.5
- second_shift: bfloat16 [768], replicated, may hold values from -2 to 2
- cotangent: bfloat16 [8192, 768], P('dp'), may hold values from -6 to 6
Outputs:
- layer_out: bfloat16 [8192, 768], P(('dp', 'tensor'))
- tokens_grad: bfloat16 [8192, 768], P(('dp', 'tensor'))
- qkv_weight_grad: float32 [768, 3, 12, 64], P('dp', None, 'tensor')
- qkv_bias_grad: float32 [2, 12, 64], P(None, 'tensor', 'dp')
- output_weight_grad: float32 [12, 64, 768], P('tensor', None, 'dp')
- output_bias_grad: float32 [768], P('dp')
- first_gain_grad: float32 [768], P('dp')
- first_shift_grad: float32 [768], P('dp')
- up_weight_grad: float32 [768, 3072], P('dp', 'tensor')
- up_bias_grad: float32 [48, 64], P('tensor', 'dp')
- down_weight_grad: float32 [3072, 768], P('tensor', 'dp')
- down_bias_grad: float32 [768], P('dp')
- second_gain_grad: float32 [768], P('dp')
- second_shift_grad: float32 [768], P('dp')
The draws below stay inside these ranges and needn't reach their ends.
Inputs may be any that keep to these rules, and one draw needn't show every extreme that they name: `segment_ids`: along each row of 512 tokens the ids never fall; each id covers 1 to 256 tokens of its row.
All inputs are finite; a program needn't handle non-finite values.
Results may differ from the reference program's by a relative error of at most 0.02.
The reference program's roundings to bfloat16 on the way count: a program that leaves them out, or rounds other values in their place, can miss the bound.
Values may be sent and summed in bfloat16 or wider, within the bound.
A program may use at most 128 MiB of HBM per device.

```python
import math
import jax
import jax.numpy as jnp
import numpy as np
from jax import lax

D = 768
HEADS = 12
HEAD = 64
FF = 3072
SEQ = 512
PAIRS = 4
ROWS = 16
TOKENS = 8192
N_TENSOR = 4


def spiked(values, own_key, source, target, parts, factor):
    def block_of(axis_at):
        return (jnp.arange(values.shape[axis_at]) // (values.shape[axis_at] // parts)).reshape((-1,) + (1,) * (values.ndim - 1 - axis_at))

    one_side = jax.random.permutation(own_key, parts)[block_of(target)]
    second = (block_of(target) + parts // 2) % parts
    return jnp.where((block_of(source) == one_side) | (block_of(source) == second), factor * values, values)


def block_levels(stream_key, shape, cuts, low, largest):
    gain, own = 1.0, jax.random.fold_in(stream_key, 6)
    for axis_at, parts in cuts:
        heights = jnp.exp(jax.random.uniform(jax.random.fold_in(own, axis_at), (parts,), jnp.float32, low / len(cuts), largest / len(cuts)))
        gain = gain * jnp.repeat(heights, shape[axis_at] // parts).reshape([-1 if axis == axis_at else 1 for axis in range(len(shape))])
    return gain


def length_profile(number_of, total, bound, slope):
    loads = [(1 << 20) // math.isqrt(grade ** slope) + 1 for grade in range(2, number_of + 1)]
    spare, holding = total - bound - (number_of - 1), [1] * (number_of - 1)
    while spare > 0:
        candidates = [i for i in range(number_of - 1) if holding[i] < bound]
        pool, left = sum([loads[i] for i in candidates]), spare
        for i in candidates:
            extra = min(bound - holding[i], max(1, left * loads[i] // pool), spare)
            holding[i] = holding[i] + extra
            spare = spare - extra
    return np.array([bound] + holding)


def uneven_parts(key, amount, total, bound, lean):
    if amount == 2:
        one = jax.random.randint(key, (), max(1, total - bound), min(bound, total - 1) + 1)
        return jnp.stack([one, total - one])
    sizes = jnp.asarray(length_profile(amount, total, bound, lean), jnp.int32)
    pairs = (amount - 1) // 2
    donor, sink = sizes[1:1 + 2 * pairs:2], sizes[2:2 + 2 * pairs:2]
    slack = jnp.minimum(donor - 1, bound - sink)
    passed = jax.random.randint(jax.random.fold_in(key, 1), (pairs,), 0, 1 << 20) % (slack + 1)
    sizes = sizes.at[1:1 + 2 * pairs:2].set(donor - passed).at[2:2 + 2 * pairs:2].set(sink + passed)
    return sizes[jax.random.permutation(jax.random.fold_in(key, 2), amount)]


def noise(stream_key, dims, scale, reach, pieces=(), kind=jnp.bfloat16):
    drawn = jax.random.normal(stream_key, dims, jnp.float32) * scale
    if len(pieces) > 0:
        drawn = block_levels(stream_key, dims, pieces, -0.22, 0.18) * drawn
    return jnp.clip(drawn, min=-reach, max=reach).astype(kind)


def heavy_noise(rng, extent, scale, reach, split, heavy, kind=jnp.bfloat16):
    entries = scale * jax.random.normal(rng, extent, jnp.float32)
    if split:
        entries = entries * block_levels(rng, extent, split, -0.22, 0.18)
    return jnp.clip(spiked(entries, jax.random.fold_in(rng, 3), *heavy), -reach, reach).astype(kind)


def setup_inputs(seed: int = 0) -> dict:
    arg_keys = jax.random.split(jax.random.key(seed), 16)
    return {
        "tokens": heavy_noise(arg_keys[0], (TOKENS, D), 1.0, 6.0, ((0, 8),), (0, 1, 8, 2.0)),
        "segment_ids": jax.vmap(lambda own: jnp.searchsorted(jnp.cumsum(uneven_parts(own, PAIRS, SEQ, SEQ // 2, 1)), jnp.arange(SEQ), side="right"))(jax.random.split(arg_keys[1], ROWS)).reshape((ROWS, SEQ)).astype(jnp.int32),
        "qkv_weight": noise(arg_keys[2], (D, 3, HEADS, HEAD), D ** -0.5, 0.21875, ((2, 4),)),
        "qkv_bias": noise(arg_keys[3], (2, HEADS, HEAD), 0.5, 3.0, ((1, 4),)),
        "output_weight": noise(arg_keys[4], (HEADS, HEAD, D), (D // 32) ** -0.5, 1.25, ((0, 4),)),
        "output_bias": noise(arg_keys[5], (D,), 0.3, 2.0),
        "first_gain": jnp.clip(1.0 + 0.1 * jax.random.normal(arg_keys[6], (D,), jnp.float32), 0.5, 1.5).astype(jnp.bfloat16),
        "first_shift": noise(arg_keys[7], (D,), 0.3, 2.0),
        "up_weight": noise(arg_keys[8], (D, FF), D ** -0.5, 0.21875, ((1, 4),)),
        "up_bias": noise(arg_keys[9], (FF // HEAD, HEAD), 0.5, 3.0, ((0, 4),)),
        "down_weight": noise(arg_keys[10], (FF, D), FF ** -0.5, 0.109375, ((0, 4),)),
        "down_bias": noise(arg_keys[11], (D,), 0.3, 2.0),
        "second_gain": jnp.clip(1.0 + 0.1 * jax.random.normal(arg_keys[12], (D,), jnp.float32), 0.5, 1.5).astype(jnp.bfloat16),
        "second_shift": noise(arg_keys[13], (D,), 0.3, 2.0),
        "cotangent": heavy_noise(arg_keys[14], (TOKENS, D), 1.0, 6.0, ((0, 8),), (0, 1, 8, 2.0)),
    }


@jax.custom_vjp
def low(v):
    return lax.optimization_barrier(v.astype(jnp.bfloat16)).astype(jnp.float32)

@jax.custom_vjp
def low_back(v):
    return v

def low_keep(v):
    return (low(v), None)

def low_pass(kept, grad):
    return (grad,)

def back_keep(v):
    return (v, None)

def back_low(kept, grad):
    return (low(grad),)
low.defvjp(low_keep, low_pass)
low_back.defvjp(back_keep, back_low)
HIGH = lax.Precision.HIGHEST
EPS = 1e-12

def normalize(rows_in, gain_vec, shift_vec):
    center = rows_in - lax.optimization_barrier(jnp.mean(rows_in, axis=-1, keepdims=True))
    spread = lax.optimization_barrier(jnp.mean(center * center, axis=-1, keepdims=True))
    return center * lax.rsqrt(spread + EPS) * gain_vec + shift_vec

def group_terms(left_mat, right_mat):
    left_parts = left_mat.reshape(left_mat.shape[0], N_TENSOR, left_mat.shape[1] // N_TENSOR)
    right_parts = right_mat.reshape(N_TENSOR, left_parts.shape[2], right_mat.shape[-1])
    group_out = jnp.einsum('tnc,ncd->tnd', left_parts, right_parts, precision=HIGH)
    return lax.optimization_barrier(jnp.sum(low_back(low(group_out)), axis=1))

def layer(tokens_f, seg_rows, params):
    qkv_w, qkv_b, out_w, out_b, gain_first, shift_first, up_w, up_b, down_w, down_b, gain_second, shift_second = params
    tok_count = tokens_f.shape[0]
    row_count = tok_count // SEQ
    mixed_proj = low_back(jnp.dot(tokens_f, qkv_w.reshape(D, 3 * D), precision=HIGH)).reshape(tok_count, 3, D)
    queries = low(mixed_proj[:, 0] + qkv_b[0].reshape(D))
    keys_low = low(mixed_proj[:, 1])
    values_low = low(mixed_proj[:, 2] + qkv_b[1].reshape(D))
    head_shape = (row_count, SEQ, HEADS, HEAD)
    scores = jnp.einsum('rqhd,rkhd->rhqk', queries.reshape(head_shape), keys_low.reshape(head_shape), precision=HIGH) * HEAD ** (-0.5)
    scores = low_back(scores)
    same_doc = seg_rows[:, :, None] == seg_rows[:, None, :]
    scores = jnp.where(same_doc[:, None], scores, -1e+30)
    attn_probs = low(jax.nn.softmax(scores, axis=-1))
    context = jnp.einsum('rhqk,rkhd->rqhd', attn_probs, values_low.reshape(head_shape), precision=HIGH).reshape(tok_count, D)
    context = low_back(low(context))
    first_in = tokens_f + group_terms(context, out_w.reshape(D, D)) + out_b
    first_out = normalize(first_in, gain_first, shift_first)
    hidden = low_back(jnp.dot(low(first_out), up_w, precision=HIGH)) + up_b.reshape(FF)
    active = low(jax.nn.gelu(hidden, approximate=False))
    second_in = first_out + group_terms(active, down_w) + down_b
    return normalize(second_in, gain_second, shift_second)

def reference(tokens, segment_ids, qkv_weight, qkv_bias, output_weight, output_bias, first_gain, first_shift, up_weight, up_bias, down_weight, down_bias, second_gain, second_shift, cotangent):
    params = (qkv_weight.astype(jnp.float32), qkv_bias.astype(jnp.float32), output_weight.astype(jnp.float32), output_bias.astype(jnp.float32), first_gain.astype(jnp.float32), first_shift.astype(jnp.float32), up_weight.astype(jnp.float32), up_bias.astype(jnp.float32), down_weight.astype(jnp.float32), down_bias.astype(jnp.float32), second_gain.astype(jnp.float32), second_shift.astype(jnp.float32))
    block_rows = math.gcd(ROWS, 8)
    block_count = ROWS // block_rows
    tok_blocks = tokens.astype(jnp.float32).reshape(block_count, block_rows * SEQ, D)
    seg_blocks = segment_ids.reshape(block_count, block_rows, SEQ)
    cot_blocks = cotangent.astype(jnp.float32).reshape(block_count, block_rows * SEQ, D)

    def one_block(totals, block_item):
        tok_b, seg_b, cot_b = block_item
        result, pull_back = jax.vjp(lambda tok_in, par_in: layer(tok_in, seg_b, par_in), tok_b, params)
        d_tok, d_par = pull_back(cot_b)
        return (jax.tree.map(jnp.add, totals, d_par), (result.astype(jnp.bfloat16), d_tok.astype(jnp.bfloat16)))
    zero_grads = jax.tree.map(jnp.zeros_like, params)
    weight_grads, (block_outs, block_dtok) = lax.scan(one_block, zero_grads, (tok_blocks, seg_blocks, cot_blocks))
    return (block_outs.reshape(TOKENS, D), block_dtok.reshape(TOKENS, D), weight_grads[0], weight_grads[1], weight_grads[2], weight_grads[3], weight_grads[4], weight_grads[5], weight_grads[6], weight_grads[7], weight_grads[8], weight_grads[9], weight_grads[10], weight_grads[11])
```

```python
import jax
import jax.numpy as jnp
from jax import lax
from jax.experimental import pallas as pl
from jax.experimental.pallas import tpu as pltpu
from jax.sharding import PartitionSpec as P

HEAD = 64
SEQ = 512
EPS = 1e-12
SCALE = HEAD ** (-0.5)
BF = jnp.bfloat16
F32 = jnp.float32
MESH_ID = pl.DeviceIdType.MESH
NAMES = ("dp", "tensor")
PIECES = (
    ("d0", 256),
    ("d1", 256),
    ("d2", 256),
    ("u0", 256),
    ("u1", 256),
    ("u2", 256),
    ("o", 128),
    ("q", 384),
    ("r", 256),
)


def dot(left, right, left_dim, right_dim):
    return lax.dot_general(
        left, right, (((left_dim,), (right_dim,)), ((), ())), preferred_element_type=F32
    )


def mean_of(values):
    return jnp.mean(values, axis=-1, keepdims=True)


def row_sum(values):
    return jnp.sum(values, axis=0, keepdims=True)


def scratch_plan(rows, half, fused):
    plan = {
        "tok": ((rows, 2, 2, 128, 768), BF),
        "cot": ((rows, 2, 128, 768), BF),
        "wq": ((5, 128, 768), BF),
        "wo": ((4, 256, 768), BF),
        "wu": ((768, 768), BF),
        "wd": ((768, 768), BF),
        "mix": ((rows, 512, 640), BF),
        "bias": ((512, 512), F32),
        "prob": ((rows, 3, 512, 512), F32),
        "ctx": ((rows, 512, 256), BF),
        "cs": ((rows, 2, 384, 128), BF),
        "cr": ((rows, 4, 384, 128), BF),
        "n1": ((rows, 256, 768), F32),
        "r1": ((rows, 256, 1), F32),
        "fo": ((rows, 256, 768), F32),
        "flow": ((rows, 2, 2, 128, 768), BF),
        "act": ((rows, 2, 256, 768), BF),
        "gp": ((rows, 2, 256, 768), F32),
        "p2": ((rows, 2, 2, 128, 768), BF),
        "p2r": ((rows, 2, 128, 768), BF),
        "x2": ((rows, 2, 128, 768), BF),
        "x2r": ((rows, 2, 128, 768), BF),
        "ds": ((rows, 256, 768), F32),
        "dsl": ((rows, 2, 2, 128, 768), BF),
        "dhl": ((rows, 2, 256, 768), BF),
        "p3": ((rows, 2, 2, 128, 768), BF),
        "p3r": ((rows, 2, 128, 768), BF),
        "x3": ((rows, 2, 128, 768), BF),
        "x3r": ((rows, 2, 128, 768), BF),
        "dfi": ((rows, 256, 768), F32),
        "dal": ((rows, 2, 2, 128, 768), BF),
        "dctx": ((512, 256), BF),
        "dsc": ((3, 512, 512), BF),
        "dmx": ((rows, 512, 640), BF),
        "p4": ((rows, 2, 2, 128, 768), BF),
        "p4r": ((rows, 2, 128, 768), BF),
        "x4": ((2, 128, 768), BF),
        "x4r": ((2, 128, 768), BF),
        "vs": ((8, 768), F32),
        "vm": ((8, 768), F32),
    }
    if fused:
        plan["vy"] = ((8, 768), F32)
        plan["vt"] = ((8, 768), F32)
        plan["vz"] = ((half - 1, 8, 768), F32)
        share = 768 // (2 * half)
        for name, width in PIECES:
            plan["g_" + name] = ((half, 2, share, width), BF)
            plan["a_" + name] = ((half, share, width), BF)
            plan["s_" + name] = ((half - 1, share, width), BF)
            plan["b_" + name] = ((half - 1, share, width), BF)
            plan["t_" + name] = ((share, width), F32)
    return plan


LOCAL_COPIES = 24
REMOTE_COPIES = 128


def layer_kernel(rows, n_dp, fused, names, *refs):
    half = n_dp // 2
    tok_h, cot_h, wq_h, wo_h, wu_h, wd_h, seg, vec = refs[:8]
    n_out = 14 if fused else 4
    outs = refs[8 : 8 + n_out]
    buf = dict(zip(names, refs[8 + n_out : 8 + n_out + len(names)]))
    local_sem, send_sem, recv_sem = refs[8 + n_out + len(names) :]

    dp = lax.axis_index("dp")
    me = lax.axis_index("tensor")
    chip = me // 2
    core = lax.rem(me, 2)
    mate = (dp, chip * 2 + (1 - core))
    over = (dp, (1 - chip) * 2 + core)
    over_mate = (dp, (1 - chip) * 2 + (1 - core))
    zed = dp // 2
    why = lax.rem(dp, 2)

    def row_partner(step):
        return (lax.rem(zed + step, half) * 2 + why, me)

    counts = {"local": 0, "remote": 0}
    pending = []

    def fetch(src, dst):
        copy = pltpu.make_async_copy(src, dst, local_sem.at[counts["local"]])
        counts["local"] += 1
        copy.start()
        return copy

    def remote(src, dst, device):
        at = counts["remote"]
        counts["remote"] += 1
        return pltpu.make_async_remote_copy(
            src_ref=src,
            dst_ref=dst,
            send_sem=send_sem.at[at],
            recv_sem=recv_sem.at[at],
            device_id=device,
            device_id_type=MESH_ID,
        )

    def send(src, dst, device):
        copy = remote(src, dst, device)
        copy.start()
        pending.append(copy)
        return copy

    got_tok = [
        [fetch(tok_h.at[r, :, h], buf["tok"].at[r, h]) for h in range(2)] for r in range(rows)
    ]
    got_wq = [
        fetch(wq_h.at[:, 0:128], buf["wq"].at[0:3]),
        fetch(wq_h.at[0, 128:192], buf["wq"].at[3, 0:64]),
        fetch(wq_h.at[1, 128:192], buf["wq"].at[3, 64:128]),
        fetch(wq_h.at[2, 128:192], buf["wq"].at[4, 0:64]),
    ]
    got_wo = fetch(wo_h, buf["wo"].at[me, 0:192])
    got_wu = fetch(wu_h, buf["wu"])
    got_wd = fetch(wd_h, buf["wd"])
    got_cot = fetch(cot_h.at[:, core], buf["cot"])

    partners = [mate, over, over_mate]
    if fused:
        partners.append((zed * 2 + (1 - why), me))
        partners += [row_partner(step) for step in range(1, half)]
    barrier = pltpu.get_barrier_semaphore()
    for device in partners:
        pl.semaphore_signal(barrier, inc=1, device_id=device, device_id_type=MESH_ID)
    buf["wq"][4, 64:128] = jnp.zeros((64, 768), BF)
    buf["vs"][...] = jnp.zeros((8, 768), F32)
    pl.semaphore_wait(barrier, len(partners))

    got_wo.wait()
    own_wo = buf["wo"].at[me, 0:192]
    wo_mate = send(own_wo, own_wo, mate)
    wo_over = send(own_wo, own_wo, over)

    lane = lax.broadcasted_iota(jnp.int32, (256, 128), 1)
    low_half = lane < 64
    lane_row = lax.broadcasted_iota(jnp.int32, (512, 128), 1) < 64

    ctx_copies = []

    def attention(r):
        for copy in got_tok[r]:
            copy.wait()
        if r == 0:
            for copy in got_wq:
                copy.wait()
        mixed = dot(
            buf["tok"][r].reshape(512, 768), buf["wq"][...].reshape(640, 768), 1, 1
        ) + vec[0:1, 0:640]
        q_low = mixed[:, 0:128].astype(BF).astype(F32) * SCALE
        buf["mix"][r, :, 0:128] = q_low.astype(BF)
        buf["mix"][r, :, 128:384] = mixed[:, 128:384].astype(BF)
        tail = mixed[:, 384:512].astype(BF).astype(F32)
        buf["mix"][r, :, 384:512] = jnp.where(lane_row, tail * SCALE, tail).astype(BF)
        buf["mix"][r, :, 512:640] = mixed[:, 512:640].astype(BF)

        ids = seg[r : r + 1, :].astype(F32)
        ids = jnp.concatenate(
            [ids[:, 0:128], ids[:, 256:384], ids[:, 128:256], ids[:, 384:512]], axis=1
        )
        column = jnp.broadcast_to(ids, (128, 512)).T
        buf["bias"][...] = jnp.where(column[:, 0:1] == ids, 0.0, -1e30)

        k_a = buf["mix"][r, :, 128:256]
        v_a = buf["mix"][r, :, 256:384]
        k_b = pltpu.roll(buf["mix"][r, :, 384:512].astype(F32), 64, 1).astype(BF)
        v_b = buf["mix"][r, :, 512:640]
        v_b_up = pltpu.roll(v_b.astype(F32), 64, 1).astype(BF)
        for h in range(2):
            at = pl.ds(h * 256, 256)
            q_a = buf["mix"][r, at, 0:128]
            q_b = buf["mix"][r, at, 384:512]
            zero = jnp.zeros_like(q_a)
            parts = []
            for head in range(3):
                query = jnp.where(low_half, q_b if head == 2 else q_a, zero)
                if head == 1:
                    query = jnp.where(low_half, zero, q_a)
                scores = dot(query, k_b if head == 2 else k_a, 1, 1) + buf["bias"][at, :]
                top = jnp.max(scores, axis=-1, keepdims=True)
                expo = jnp.exp(scores - top)
                probs = expo * (1.0 / jnp.sum(expo, axis=-1, keepdims=True))
                buf["prob"][r, head, at, :] = probs
                value = v_a if head < 2 else (v_b if h == 0 else v_b_up)
                parts.append(dot(probs.astype(BF), value, 1, 0))
            buf["ctx"][r, at, 0:128] = jnp.where(low_half, parts[0], parts[1]).astype(BF)
            buf["ctx"][r, at, 128:256] = parts[2].astype(BF)
        for part in range(2):
            here = [
                buf["ctx"][r, h * 256 + part * 128 : h * 256 + part * 128 + 128, :]
                for h in range(2)
            ]
            buf["cs"][r, part, 0:128] = here[0][:, 0:128]
            buf["cs"][r, part, 128:256] = here[1][:, 0:128]
            buf["cs"][r, part, 256:384] = jnp.where(
                lane[0:128] < 64, here[0][:, 128:256], here[1][:, 128:256]
            )
        ctx_copies.append(
            [
                send(buf["cs"].at[r, core], buf["cr"].at[r, me], over),
                send(buf["cs"].at[r, 1 - core], buf["cr"].at[r, me], over_mate),
                send(buf["cs"].at[r, 1 - core], buf["cr"].at[r, me], mate),
            ]
        )
        buf["cr"][r, me] = buf["cs"][r, core]

    flow_copies = {}

    def first_norm(r):
        for copy in ctx_copies[r]:
            copy.wait_recv()
        total = None
        for group in range(4):
            packed = buf["cr"][r, group, 256:384]
            zero = jnp.zeros_like(packed)
            keep = lane[0:128] < 64
            left = jnp.concatenate(
                [
                    buf["cr"][r, group, 0:256],
                    jnp.concatenate(
                        [jnp.where(keep, packed, zero), jnp.where(keep, zero, packed)], axis=0
                    ),
                ],
                axis=1,
            )
            term = dot(left, buf["wo"][group], 1, 0).astype(BF).astype(F32)
            total = term if total is None else total + term
        first_in = buf["tok"][r, :, core].reshape(256, 768).astype(F32) + total + vec[1:2, :]
        center = first_in - mean_of(first_in)
        scale = lax.rsqrt(mean_of(center * center) + EPS)
        unit = center * scale
        buf["n1"][r] = unit
        buf["r1"][r] = scale
        first_out = unit * vec[2:3, :] + vec[3:4, :]
        buf["fo"][r] = first_out
        first_low = first_out.astype(BF)
        for h in range(2):
            buf["flow"][r, h, core] = first_low[h * 128 : h * 128 + 128]
            own = buf["flow"].at[r, h, core]
            flow_copies[r, h] = send(own, own, mate)

    pair_copies = {}
    cross_copies = {}

    def ffn_forward(r, h):
        flow_copies[r, h].wait_recv()
        rows_in = buf["flow"][r, h].reshape(256, 768)
        for part in range(3):
            at = pl.ds(part * 256, 256)
            hidden = dot(rows_in, buf["wu"][:, at], 1, 0) + vec[4:5, at]
            phi = 0.5 * (1.0 + lax.erf(hidden * 0.7071067811865476))
            buf["act"][r, h, :, at] = (hidden * phi).astype(BF)
            buf["gp"][r, h, :, at] = (
                phi + hidden * jnp.exp(-0.5 * hidden * hidden) * 0.3989422804014327
            )
        terms = dot(buf["act"][r, h], buf["wd"][...], 1, 0).astype(BF)
        buf["p2"][r, h] = terms.reshape(2, 128, 768)
        pair_copies[2, r, h] = send(buf["p2"].at[r, h, 1 - core], buf["p2r"].at[r, h], mate)

    def exchange(stage, r, h):
        pair_copies[stage, r, h].wait_recv()
        own = buf["p%d" % stage][r, h, core].astype(F32)
        other = buf["p%dr" % stage][r, h].astype(F32)
        buf["x%d" % stage][r, h] = (own + other).astype(BF)
        cross_copies[stage, r, h] = send(
            buf["x%d" % stage].at[r, h], buf["x%dr" % stage].at[r, h], over
        )

    def crossed(stage, r, h):
        cross_copies[stage, r, h].wait_recv()
        return buf["x%d" % stage][r, h].astype(F32) + buf["x%dr" % stage][r, h].astype(F32)

    dsl_copies = {}

    def second_norm(r, h):
        total = crossed(2, r, h)
        at = pl.ds(h * 128, 128)
        second_in = buf["fo"][r, at, :] + total + vec[5:6, :]
        center = second_in - mean_of(second_in)
        scale = lax.rsqrt(mean_of(center * center) + EPS)
        unit = center * scale

        @pl.when(chip == r)
        def _():
            layer = unit * vec[6:7, :] + vec[7:8, :]
            outs[0][at, :] = layer.astype(BF)

        grad = buf["cot"][r, h].astype(F32)
        scaled = grad * vec[6:7, :]
        d_second = scale * (scaled - mean_of(scaled) - unit * mean_of(scaled * unit))
        buf["ds"][r, at, :] = d_second
        buf["dsl"][r, h, core] = d_second.astype(BF)
        own = buf["dsl"].at[r, h, core]
        dsl_copies[r, h] = send(own, own, mate)
        buf["vs"][0:1, :] += row_sum(grad * unit)
        buf["vs"][1:2, :] += row_sum(grad)
        buf["vs"][2:3, :] += row_sum(d_second)

    def ffn_backward(r, h):
        dsl_copies[r, h].wait_recv()
        rows_in = buf["dsl"][r, h].reshape(256, 768)
        for part in range(3):
            at = pl.ds(part * 256, 256)
            d_hidden = dot(rows_in, buf["wd"][at, :], 1, 1) * buf["gp"][r, h, :, at]
            buf["vs"][6:7, at] += row_sum(d_hidden)
            buf["dhl"][r, h, :, at] = d_hidden.astype(BF)
        terms = dot(buf["dhl"][r, h], buf["wu"][...], 1, 1).astype(BF)
        buf["p3"][r, h] = terms.reshape(2, 128, 768)
        pair_copies[3, r, h] = send(buf["p3"].at[r, h, 1 - core], buf["p3r"].at[r, h], mate)

    dal_copies = {}

    def first_norm_back(r, h):
        total = crossed(3, r, h)
        at = pl.ds(h * 128, 128)
        d_first = buf["ds"][r, at, :] + total
        unit = buf["n1"][r, at, :]
        scaled = d_first * vec[2:3, :]
        d_in = buf["r1"][r, at, :] * (scaled - mean_of(scaled) - unit * mean_of(scaled * unit))
        buf["dfi"][r, at, :] = d_in
        buf["dal"][r, h, core] = d_in.astype(BF)
        own = buf["dal"].at[r, h, core]
        dal_copies[r, h] = send(own, own, mate)
        buf["vs"][3:4, :] += row_sum(d_first * unit)
        buf["vs"][4:5, :] += row_sum(d_first)
        buf["vs"][5:6, :] += row_sum(d_in)

    out_parts = []

    def attention_back(r):
        for h in range(2):
            dal_copies[r, h].wait_recv()
        buf["dctx"][...] = dot(
            buf["dal"][r].reshape(512, 768), buf["wo"][me], 1, 1
        ).astype(BF)
        q_a = buf["mix"][r, :, 0:128]
        k_a = buf["mix"][r, :, 128:256]
        v_a = buf["mix"][r, :, 256:384]
        qk_b = buf["mix"][r, :, 384:512]
        qk_roll = pltpu.roll(qk_b.astype(F32), 64, 1).astype(BF)
        v_b = buf["mix"][r, :, 512:640]
        d_q, d_k, d_v = [], [], []
        for head in range(3):
            tile = pl.ds((head // 2) * 128, 128)
            value = v_a if head < 2 else v_b
            for h in range(2):
                at = pl.ds(h * 256, 256)
                d_rows = buf["dctx"][at, tile]
                if head == 0:
                    d_rows = jnp.where(low_half, d_rows, jnp.zeros_like(d_rows))
                if head == 1:
                    d_rows = jnp.where(low_half, jnp.zeros_like(d_rows), d_rows)
                probs = buf["prob"][r, head, at, :]
                weighted = probs * dot(d_rows, value, 1, 1)
                inner = jnp.sum(weighted, axis=-1, keepdims=True)
                buf["dsc"][head, at, :] = (weighted - probs * inner).astype(BF)
            d_scores = buf["dsc"][head]
            d_q.append(dot(d_scores, k_a if head < 2 else qk_roll, 1, 0))
            d_k.append(dot(d_scores, q_a if head < 2 else qk_roll, 0, 0))
            d_v.append(dot(buf["prob"][r, head].astype(BF), buf["dctx"][:, tile], 0, 0))
        tiles = [
            jnp.where(lane_row, d_q[0], d_q[1]) * SCALE,
            jnp.where(lane_row, d_k[0], d_k[1]),
            jnp.where(lane_row, d_v[0], d_v[1]),
            jnp.where(lane_row, d_q[2] * SCALE, d_k[2]),
            jnp.where(lane_row, d_v[2], 0.0),
        ]
        for at, tile in enumerate(tiles):
            lanes = pl.ds(at * 128, 128)
            buf["dmx"][r, :, lanes] = tile.astype(BF)
            if at != 1:
                buf["vs"][7:8, lanes] += row_sum(tile)

    tok_copies = []

    def token_terms(r, h):
        terms = dot(
            buf["dmx"][r, h * 256 : h * 256 + 256, :], buf["wq"][...].reshape(640, 768), 1, 0
        )
        buf["p4"][r, h] = terms.astype(BF).reshape(2, 128, 768)
        pair_copies[4, r, h] = send(buf["p4"].at[r, h, 1 - core], buf["p4r"].at[r, h], mate)

    cross4 = [remote(buf["x4"].at[h], buf["x4r"].at[h], over) for h in range(2)]

    def token_cross(r, h):
        pair_copies[4, r, h].wait_recv()

        @pl.when(chip != r)
        def _():
            own = buf["p4"][r, h, core].astype(F32)
            other = buf["p4r"][r, h].astype(F32)
            buf["x4"][h] = (own + other).astype(BF)
            cross4[h].start()

    def token_finish(h):
        cross4[h].wait_recv()
        own = buf["p4"][chip, h, core].astype(F32)
        other = buf["p4r"][chip, h].astype(F32)
        pair = (own + other).astype(BF).astype(F32)
        total = pair + buf["x4r"][h].astype(F32)
        result = buf["dfi"][chip, pl.ds(h * 128, 128), :] + total
        outs[1][h * 128 : h * 128 + 128, :] = result.astype(BF)

    first_copies = {}
    second_copies = {}
    starts = {}
    column = 0
    for name, width in PIECES:
        starts[name] = column
        column += width

    def reduce_start(name, grad):
        width = dict(PIECES)[name]
        if not fused:
            outs[2][:, starts[name] : starts[name] + width] = grad
            return
        stage = buf["g_" + name]
        stage[...] = grad.astype(BF).reshape(stage.shape)
        first_copies[name] = send(
            stage.at[:, 1 - why], buf["a_" + name], (zed * 2 + (1 - why), me)
        )

    def reduce_middle(name):
        if not fused:
            return
        first_copies[name].wait_recv()
        stage, came = buf["g_" + name], buf["a_" + name]
        copies = []
        for step in range(1, half):
            target = lax.rem(zed + step, half)
            both = stage[target, why].astype(F32) + came[target].astype(F32)
            buf["s_" + name][step - 1] = both.astype(BF)
            copies.append(
                send(
                    buf["s_" + name].at[step - 1],
                    buf["b_" + name].at[step - 1],
                    row_partner(step),
                )
            )
        second_copies[name] = copies
        buf["t_" + name][...] = stage[zed, why].astype(F32) + came[zed].astype(F32)

    def reduce_finish(name):
        if not fused:
            return
        total = buf["t_" + name][...]
        for step, copy in enumerate(second_copies[name]):
            copy.wait_recv()
            total = total + buf["b_" + name][step].astype(F32)
        if name[0] == "d":
            outs[10][:, starts[name] : starts[name] + 256] = total
        elif name[0] == "u":
            at = starts[name] - starts["u0"]
            outs[8][:, at : at + 256] = total
        elif name == "o":
            outs[4][0:128, :] = total.T
        elif name == "q":
            for kind in range(3):
                outs[2][kind * 192 : kind * 192 + 128, :] = total[
                    :, kind * 128 : kind * 128 + 128
                ].T
        else:
            for at in range(4):
                flipped = total[:, (at // 2) * 128 : (at // 2) * 128 + 128].T
                piece = flipped[(at % 2) * 64 : (at % 2) * 64 + 64]
                if at < 3:
                    outs[2][at * 192 + 128 : at * 192 + 192, :] = piece
                else:
                    outs[4][128:192, :] = piece

    def down_grad(part):
        at = pl.ds(part * 256, 256)
        return dot(
            buf["dsl"][...].reshape(rows * 512, 768),
            buf["act"][:, :, :, at].reshape(rows * 512, 256),
            0,
            0,
        )

    def up_grad(part):
        at = pl.ds(part * 256, 256)
        return dot(
            buf["flow"][...].reshape(rows * 512, 768),
            buf["dhl"][:, :, :, at].reshape(rows * 512, 256),
            0,
            0,
        )

    def out_grad_first():
        return dot(
            buf["dal"][...].reshape(rows * 512, 768),
            buf["ctx"][:, :, 0:128].reshape(rows * 512, 128),
            0,
            0,
        )

    def out_grad_second():
        sides = []
        for h in range(2):
            sides.append(
                dot(
                    buf["dal"][:, h].reshape(rows * 256, 768),
                    buf["ctx"][:, h * 256 : h * 256 + 256, 128:256].reshape(rows * 256, 128),
                    0,
                    0,
                )
            )
        return pltpu.roll(sides[0], 64, 1) + sides[1]

    def qkv_grad(low, high):
        return dot(
            buf["tok"][...].reshape(rows * 512, 768),
            buf["dmx"][:, :, low:high].reshape(rows * 512, high - low),
            0,
            0,
        )

    attention(0)
    wo_over.wait_recv()
    theirs = buf["wo"].at[(1 - chip) * 2 + core, 0:192]
    wo_far = send(theirs, theirs, mate)
    attention(1)
    wo_mate.wait_recv()
    wo_far.wait_recv()
    for group in range(4):
        buf["wo"][group, 192:256] = buf["wo"][group, 128:192]
    first_norm(0)
    got_wu.wait()
    got_wd.wait()
    got_cot.wait()
    ffn_forward(0, 0)
    ffn_forward(0, 1)
    exchange(2, 0, 0)
    first_norm(1)
    exchange(2, 0, 1)
    ffn_forward(1, 0)
    ffn_forward(1, 1)
    exchange(2, 1, 0)
    second_norm(0, 0)
    exchange(2, 1, 1)
    ffn_backward(0, 0)
    second_norm(0, 1)
    exchange(3, 0, 0)
    ffn_backward(0, 1)
    second_norm(1, 0)
    exchange(3, 0, 1)
    ffn_backward(1, 0)
    second_norm(1, 1)
    exchange(3, 1, 0)
    ffn_backward(1, 1)
    reduce_start("d0", down_grad(0))
    exchange(3, 1, 1)
    reduce_start("u0", up_grad(0))
    reduce_start("d1", down_grad(1))
    first_norm_back(0, 0)
    reduce_start("u1", up_grad(1))
    reduce_start("d2", down_grad(2))
    reduce_middle("d0")
    first_norm_back(0, 1)
    reduce_start("u2", up_grad(2))
    reduce_middle("u0")
    attention_back(0)
    reduce_middle("d1")
    token_terms(0, 0)
    token_terms(0, 1)
    token_cross(0, 0)
    first_norm_back(1, 0)
    token_cross(0, 1)
    reduce_middle("u1")
    first_norm_back(1, 1)
    attention_back(1)
    token_terms(1, 0)
    token_terms(1, 1)
    reduce_start("o", out_grad_first())
    token_cross(1, 0)
    reduce_start("q", qkv_grad(0, 384))
    token_cross(1, 1)
    tail = qkv_grad(384, 640)
    merged = jnp.concatenate(
        [
            tail[:, 0:128],
            jnp.where(
                lax.broadcasted_iota(jnp.int32, (768, 128), 1) < 64,
                tail[:, 128:256],
                out_grad_second(),
            ),
        ],
        axis=1,
    )
    reduce_start("r", merged)

    vec_mate = send(buf["vs"], buf["vm"], mate)
    reduce_middle("d2")
    reduce_middle("u2")
    vec_mate.wait_recv()
    shared = lax.broadcasted_iota(jnp.int32, (8, 768), 0) < 6
    small = buf["vs"][...] + jnp.where(shared, buf["vm"][...], 0.0)
    if fused:
        buf["vt"][...] = small
        vec_row = send(buf["vt"], buf["vy"], (zed * 2 + (1 - why), me))
    else:
        outs[3][...] = small
    for name in ("d0", "u0", "d1", "u1"):
        reduce_finish(name)
    reduce_middle("o")
    reduce_middle("q")
    reduce_middle("r")
    if fused:
        vec_row.wait_recv()
        vec_row.wait_send()
        pending[:] = [copy for copy in pending if copy is not vec_row]
        small = small + buf["vy"][...]
        buf["vt"][...] = small
        vec_far = [send(buf["vt"], buf["vz"].at[s - 1], row_partner(s)) for s in range(1, half)]
    token_finish(0)
    token_finish(1)
    for name in ("d2", "u2", "o"):
        reduce_finish(name)
    if fused:
        for step, copy in enumerate(vec_far):
            copy.wait_recv()
            small = small + buf["vz"][step]
        share = 768 // n_dp
        turned = pltpu.roll(small, 768 - dp * share, 1)
        for row, at in ((5, 5), (3, 6), (4, 7), (2, 11), (0, 12), (1, 13)):
            outs[at][...] = turned[row : row + 1, 0:share]
        wide = HEAD // n_dp
        lanes = lax.broadcasted_iota(jnp.int32, (8, 768), 1)
        depth = lax.broadcasted_iota(jnp.int32, (8, 768), 0)
        spread = jnp.where(lax.rem(lanes, HEAD) == depth + dp * wide, small[6:7, :], 0.0)
        group = lax.broadcasted_iota(jnp.int32, (768, 128), 0) // HEAD
        pick = (group == lax.broadcasted_iota(jnp.int32, (768, 128), 1)).astype(F32)
        outs[9][...] = jnp.dot(spread, pick, precision=lax.Precision.HIGHEST)[0:wide, 0:12]
        group = lanes // HEAD
        where = jnp.where(
            depth < 4,
            lax.rem(depth, 2) * 4 + depth // 2,
            jnp.where(depth == 4, 6, 8),
        )
        spread = jnp.where((group == where) & (depth < 6), small[7:8, :], 0.0)
        inside = lax.rem(lax.broadcasted_iota(jnp.int32, (768, 128), 0), HEAD)
        pick = (inside == lax.broadcasted_iota(jnp.int32, (768, 128), 1) + dp * wide).astype(F32)
        heads = jnp.dot(spread, pick, precision=lax.Precision.HIGHEST)
        for head in range(3):
            outs[3][head] = heads[head * 2 : head * 2 + 2, 0:wide]
    reduce_finish("q")
    reduce_finish("r")
    for copy in pending + cross4:
        copy.wait_send()


def body(
    tokens,
    segment_ids,
    qkv_weight,
    qkv_bias,
    output_weight,
    output_bias,
    first_gain,
    first_shift,
    up_weight,
    up_bias,
    down_weight,
    down_bias,
    second_gain,
    second_shift,
    cotangent,
):
    rows = tokens.shape[0] // SEQ
    n_dp = lax.axis_size("dp")
    share = 768 // n_dp
    fused = share % 16 == 0 and n_dp % 2 == 0
    split = (rows, 2, 2, 128, 768)
    pad = jnp.zeros((64,), BF)
    bias_q = qkv_bias[0].reshape(192)
    bias_v = qkv_bias[1].reshape(192)
    vectors = jnp.stack(
        [
            jnp.concatenate(
                [bias_q[:128], pad, pad, bias_v[:128], bias_q[128:], pad, bias_v[128:], pad, pad, pad]
            ),
            output_bias,
            first_gain,
            first_shift,
            up_bias.reshape(768),
            down_bias,
            second_gain,
            second_shift,
        ]
    ).astype(F32)
    plan = scratch_plan(rows, n_dp // 2, fused)
    shape = jax.ShapeDtypeStruct
    outs = [shape((256, 768), BF), shape((256, 768), BF)]
    if fused:
        wide = HEAD // n_dp
        vector = shape((1, share), F32)
        outs += [
            shape((576, share), F32),
            shape((3, 2, wide), F32),
            shape((192, share), F32),
            vector,
            vector,
            vector,
            shape((share, 768), F32),
            shape((wide, 12), F32),
            shape((share, 768), F32),
            vector,
            vector,
            vector,
        ]
    else:
        outs += [shape((768, 2304), F32), shape((8, 768), F32)]
    whole = pl.BlockSpec(memory_space=pltpu.VMEM)
    anywhere = pl.BlockSpec(memory_space=pl.ANY)

    def kernel(*refs):
        layer_kernel(rows, n_dp, fused, list(plan), *refs)

    got = pl.pallas_call(
        kernel,
        out_shape=outs,
        in_specs=[anywhere] * 6 + [whole] * 2,
        out_specs=[whole] * len(outs),
        scratch_shapes=[pltpu.VMEM(dims, kind) for dims, kind in plan.values()]
        + [
            pltpu.SemaphoreType.DMA((LOCAL_COPIES,)),
            pltpu.SemaphoreType.DMA((REMOTE_COPIES,)),
            pltpu.SemaphoreType.DMA((REMOTE_COPIES,)),
        ],
        compiler_params=pltpu.CompilerParams(
            collective_id=0, has_side_effects=True, vmem_limit_bytes=62 * 1024 * 1024
        ),
    )(
        tokens.reshape(split),
        cotangent.reshape(split),
        qkv_weight.transpose(1, 2, 3, 0).reshape(3, 192, 768),
        output_weight.reshape(192, 768),
        up_weight,
        down_weight,
        segment_ids,
        vectors,
    )
    if not fused:
        got = finish_plain(n_dp, *got)
    return (
        got[0],
        got[1],
        got[2].reshape(3, 3, HEAD, share).transpose(3, 0, 1, 2),
        got[3].transpose(1, 0, 2),
        got[4].reshape(3, HEAD, share),
        got[5].reshape(share),
        got[6].reshape(share),
        got[7].reshape(share),
        got[8],
        got[9].T,
        got[10].T,
        got[11].reshape(share),
        got[12].reshape(share),
        got[13].reshape(share),
    )


def finish_plain(n_dp, layer, tokens_grad, grads, small):
    share = 768 // n_dp
    grads = lax.psum_scatter(grads, "dp", scatter_dimension=0, tiled=True)
    small = lax.psum(small, "dp")
    dp = lax.axis_index("dp")
    wide = HEAD // n_dp
    turned = lax.dynamic_slice_in_dim(small, dp * share, share, 1)
    up_bias = lax.dynamic_slice_in_dim(small[6].reshape(12, HEAD), dp * wide, wide, 1)
    row = small[7]
    sums = jnp.stack(
        [row[0:64], row[256:320], row[64:128], row[320:384], row[384:448], row[512:576]]
    )
    sums = lax.dynamic_slice_in_dim(sums, dp * wide, wide, 1)
    down, up = grads[:, 0:768], grads[:, 768:1536]
    out_a, main, tail = grads[:, 1536:1664], grads[:, 1664:2048], grads[:, 2048:2304]
    qkv = jnp.concatenate(
        [
            main[:, 0:128],
            tail[:, 0:64],
            main[:, 128:256],
            tail[:, 64:128],
            main[:, 256:384],
            tail[:, 128:192],
        ],
        axis=1,
    )
    out = jnp.concatenate([out_a, tail[:, 192:256]], axis=1)
    return [
        layer,
        tokens_grad,
        qkv.T,
        sums.reshape(3, 2, wide),
        out.T,
        turned[5],
        turned[3],
        turned[4],
        up,
        up_bias.T,
        down,
        turned[2],
        turned[0],
        turned[1],
    ]


def solution(mesh):
    placed = (
        P("dp", None),
        P("dp", None),
        P(None, None, "tensor", None),
        P(None, "tensor", None),
        P("tensor", None, None),
        P(),
        P(),
        P(),
        P(None, "tensor"),
        P("tensor", None),
        P("tensor", None),
        P(),
        P(),
        P(),
        P("dp", None),
    )
    return jax.shard_map(
        body,
        mesh=mesh,
        in_specs=placed,
        out_specs=(
            P(("dp", "tensor"), None),
            P(("dp", "tensor"), None),
            P("dp", None, "tensor", None),
            P(None, "tensor", "dp"),
            P("tensor", None, "dp"),
            P("dp"),
            P("dp"),
            P("dp"),
            P("dp", "tensor"),
            P("tensor", "dp"),
            P("tensor", "dp"),
            P("dp"),
            P("dp"),
            P("dp"),
        ),
        check_vma=False,
    )
```

```python
import jax
import jax.numpy as jnp
from jax import lax
from jax.experimental import pallas as pl
from jax.experimental.pallas import tpu as pltpu
from jax.sharding import PartitionSpec as P

HEAD = 64
SEQ = 512
EPS = 1e-12
SCALE = HEAD ** (-0.5)
BF = jnp.bfloat16
F32 = jnp.float32
MESH_ID = pl.DeviceIdType.MESH
NAMES = ("dp", "tensor")
PIECES = (
    ("d0", 256),
    ("d1", 256),
    ("d2", 256),
    ("u0", 256),
    ("u1", 256),
    ("u2", 256),
    ("o", 128),
    ("q", 384),
    ("r", 128),
    ("s", 128),
)
DEPTH_FIRST = ("d1", "u2")


def dot(left, right, left_dim, right_dim):
    return lax.dot_general(
        left, right, (((left_dim,), (right_dim,)), ((), ())), preferred_element_type=F32
    )


def mean_of(values):
    return jnp.mean(values, axis=-1, keepdims=True)


def row_sum(values):
    return jnp.sum(values, axis=0, keepdims=True)


def scratch_plan(rows, share, fused, results):
    plan = {
        "seg": ((rows, SEQ), jnp.int32),
        "bqv": ((3, 2, HEAD), BF),
        "bup": ((12, HEAD), BF),
        "vec": ((8, 768), F32),
        "tok": ((rows, 2, 2, 128, 768), BF),
        "cot": ((rows, 2, 128, 768), BF),
        "wq": ((5, 128, 768), BF),
        "wo": ((4, 256, 768), BF),
        "wu": ((768, 768), BF),
        "wd": ((768, 768), BF),
        "mix": ((rows, 512, 640), BF),
        "bias": ((rows, 512, 512), F32),
        "mixr": ((rows, 512, 128), BF),
        "prob": ((rows, 3, 512, 512), F32),
        "ctx": ((rows, 512, 256), BF),
        "cs": ((rows, 2, 2, 192, 128), BF),
        "cr": ((rows, 2, 4, 192, 128), BF),
        "n1": ((rows, 256, 768), F32),
        "r1": ((rows, 256, 1), F32),
        "fo": ((rows, 256, 768), F32),
        "flow": ((rows, 2, 2, 128, 768), BF),
        "act": ((rows, 2, 256, 768), BF),
        "gp": ((rows, 2, 256, 768), F32),
        "p2": ((rows, 2, 2, 128, 768), BF),
        "p2r": ((rows, 2, 128, 768), BF),
        "x2": ((rows, 2, 128, 768), BF),
        "x2r": ((rows, 2, 128, 768), BF),
        "ds": ((rows, 256, 768), F32),
        "dsl": ((rows, 2, 2, 128, 768), BF),
        "dhl": ((rows, 2, 256, 768), BF),
        "p3": ((rows, 2, 2, 128, 768), BF),
        "p3r": ((rows, 2, 128, 768), BF),
        "x3": ((rows, 2, 128, 768), BF),
        "x3r": ((rows, 2, 128, 768), BF),
        "dfi": ((rows, 256, 768), F32),
        "dal": ((rows, 2, 2, 128, 768), BF),
        "dctx": ((512, 256), BF),
        "dsc": ((3, 512, 512), BF),
        "dmx": ((rows, 512, 640), BF),
        "p4": ((rows, 2, 2, 128, 768), BF),
        "p4r": ((rows, 2, 128, 768), BF),
        "x4": ((2, 128, 768), BF),
        "x4r": ((2, 128, 768), BF),
        "vs": ((8, 768), F32),
        "vm": ((8, 768), F32),
    }
    for at in range(6):
        plan["e%d" % at] = ((6, 128), BF)
    for at, result in enumerate(results):
        plan["y%d" % at] = (result.shape, result.dtype)
    if fused:
        for name in ("vt", "vy", "vu", "vz", "vw", "vx"):
            plan[name] = ((8, 768), F32)
        for name, width in PIECES:
            plan["g_" + name] = ((2, 2, 2, share, width), BF)
            plan["a_" + name] = ((2, 2, share, width), BF)
            plan["s_" + name] = ((2, share, width), BF)
            plan["b_" + name] = ((2, share, width), BF)
            plan["v_" + name] = ((share, width), BF)
            plan["c_" + name] = ((share, width), BF)
    return plan


INPUTS = 15
LOCAL_COPIES = 40
REMOTE_COPIES = 128


def layer_kernel(rows, n_dp, fused, names, *refs):
    tok_h, cot_h, wq_h, wo_h, wu_h, wd_h, seg_h = refs[:7]
    small_h = refs[7:INPUTS]
    n_out = 14 if fused else 4
    results = refs[INPUTS : INPUTS + n_out]
    buf = dict(zip(names, refs[INPUTS + n_out : INPUTS + n_out + len(names)]))
    outs = [buf["y%d" % at] for at in range(n_out)]
    seg, vec = buf["seg"], buf["vec"]
    local_sem, send_sem, recv_sem = refs[INPUTS + n_out + len(names) :]

    dp = lax.axis_index("dp")
    me = lax.axis_index("tensor")
    chip = me // 2
    core = lax.rem(me, 2)
    mate = (dp, chip * 2 + (1 - core))
    over = (dp, (1 - chip) * 2 + core)
    over_mate = (dp, (1 - chip) * 2 + (1 - core))
    why = lax.rem(dp, 2)
    near = lax.rem(dp // 2, 2)
    far = dp // 4
    side = (dp + 1 - 2 * why, me)
    next_near = (dp + 2 - 4 * near, me)
    next_far = (dp + 4 - 8 * far, me)

    counts = {"local": 0, "remote": 0}
    pending = []
    stored = []

    def fetch(src, dst):
        copy = pltpu.make_async_copy(src, dst, local_sem.at[counts["local"]])
        counts["local"] += 1
        copy.start()
        return copy

    def remote(src, dst, device):
        at = counts["remote"]
        counts["remote"] += 1
        return pltpu.make_async_remote_copy(
            src_ref=src,
            dst_ref=dst,
            send_sem=send_sem.at[at],
            recv_sem=recv_sem.at[at],
            device_id=device,
            device_id_type=MESH_ID,
        )

    arrived = []

    def once(copy):
        new = not any(copy is other for other in arrived)
        if new:
            arrived.append(copy)
        return new

    def arrive(copy):
        if once(copy):
            copy.wait_recv()

    def loaded(copy):
        if once(copy):
            copy.wait()

    def send(src, dst, device):
        copy = remote(src, dst, device)
        copy.start()
        pending.append(copy)
        return copy

    partners = [mate, over, over_mate]
    if fused:
        partners += [side, next_near, next_far]
    barrier = pltpu.get_barrier_semaphore()
    for device in partners:
        pl.semaphore_signal(barrier, inc=1, device_id=device, device_id_type=MESH_ID)
    got_tok = [
        [fetch(tok_h.at[r, :, h], buf["tok"].at[r, h]) for h in range(2)] for r in range(rows)
    ]
    got_wq = [
        fetch(wq_h.at[:, 0:128], buf["wq"].at[0:3]),
        fetch(wq_h.at[0, 128:192], buf["wq"].at[3, 0:64]),
        fetch(wq_h.at[1, 128:192], buf["wq"].at[3, 64:128]),
        fetch(wq_h.at[2, 128:192], buf["wq"].at[4, 0:64]),
    ]
    got_small = [fetch(seg_h, buf["seg"]), fetch(small_h[0], buf["bqv"])]
    got_small.append(fetch(small_h[1], buf["bup"]))
    got_small += [fetch(small_h[2 + at], buf["e%d" % at]) for at in range(6)]
    got_wo = fetch(wo_h, buf["wo"].at[me, 0:192])
    got_wu = fetch(wu_h, buf["wu"])
    got_wd = fetch(wd_h, buf["wd"])
    got_cot = fetch(cot_h.at[:, core], buf["cot"])

    buf["wq"][4, 64:128] = jnp.zeros((64, 768), BF)
    buf["vs"][...] = jnp.zeros((8, 768), F32)
    for copy in got_small:
        copy.wait()
    bias = [[buf["bqv"][head, kind : kind + 1, :].astype(F32) for kind in range(2)] for head in range(3)]
    none = jnp.zeros((1, HEAD), F32)
    none2 = jnp.zeros((1, 128), F32)
    for at, pair in enumerate(
        (
            (bias[0][0], bias[1][0]),
            (none, none),
            (bias[0][1], bias[1][1]),
            (bias[2][0], none),
            (bias[2][1], none),
        )
    ):
        vec[0:1, at * 128 : at * 128 + 128] = jnp.concatenate(pair, axis=1)
    vec[0:1, 640:768] = none2
    for at in range(6):
        pair = buf["bup"][2 * at : 2 * at + 2, :].astype(F32)
        vec[4:5, at * 128 : at * 128 + 128] = jnp.concatenate([pair[0:1], pair[1:2]], axis=1)
    for at, row in enumerate((1, 2, 3, 5, 6, 7)):
        short = buf["e%d" % at][...].astype(F32)
        for part in range(6):
            vec[row : row + 1, part * 128 : part * 128 + 128] = short[part : part + 1]

    lane = lax.broadcasted_iota(jnp.int32, (256, 128), 1)
    low_half = lane < 64
    lane_row = lax.broadcasted_iota(jnp.int32, (512, 128), 1) < 64

    ctx_copies = {}

    def project(r):
        for copy in got_tok[r]:
            copy.wait()
        for copy in got_wq:
            loaded(copy)
        mixed = dot(
            buf["tok"][r].reshape(512, 768), buf["wq"][...].reshape(640, 768), 1, 1
        ) + vec[0:1, 0:640]
        q_low = mixed[:, 0:128].astype(BF).astype(F32) * SCALE
        buf["mix"][r, :, 0:128] = q_low.astype(BF)
        buf["mix"][r, :, 128:384] = mixed[:, 128:384].astype(BF)
        tail = mixed[:, 384:512].astype(BF).astype(F32)
        tail = jnp.where(lane_row, tail * SCALE, tail)
        buf["mix"][r, :, 384:512] = tail.astype(BF)
        buf["mixr"][r] = pltpu.roll(tail, 64, 1).astype(BF)
        buf["mix"][r, :, 512:640] = mixed[:, 512:640].astype(BF)

        ids = seg[r : r + 1, :].astype(F32)
        ids = jnp.concatenate(
            [ids[:, 0:128], ids[:, 256:384], ids[:, 128:256], ids[:, 384:512]], axis=1
        )
        column = jnp.broadcast_to(ids, (128, 512)).T
        buf["bias"][r] = jnp.where(column[:, 0:1] == ids, 0.0, -1e30)

    def attend(r, h):
        at = pl.ds(h * 256, 256)
        q_a = buf["mix"][r, at, 0:128]
        q_b = buf["mix"][r, at, 384:512]
        zero = jnp.zeros_like(q_a)
        parts = []
        for head in range(3):
            if head == 1:
                query = jnp.where(low_half, zero, q_a)
            else:
                query = jnp.where(low_half, q_b if head == 2 else q_a, zero)
            key = buf["mixr"][r] if head == 2 else buf["mix"][r, :, 128:256]
            value = buf["mix"][r, :, 512:640] if head == 2 else buf["mix"][r, :, 256:384]
            scores = dot(query, key, 1, 1) + buf["bias"][r, at, :]
            top = jnp.max(scores, axis=-1, keepdims=True)
            expo = jnp.exp(scores - top)
            probs = expo * (1.0 / jnp.sum(expo, axis=-1, keepdims=True))
            buf["prob"][r, head, at, :] = probs
            parts.append(dot(probs.astype(BF), value, 1, 0))
        both = jnp.where(low_half, parts[0], parts[1]).astype(BF)
        buf["ctx"][r, at, 0:128] = both
        buf["ctx"][r, at, 128:256] = parts[2].astype(BF)
        for part in range(2):
            first = part * 128
            buf["cs"][r, h, part, 0:128] = both[first : first + 128]
            buf["cs"][r, h, part, 128:192] = jnp.where(
                lane[0:64] < 64,
                parts[2][first : first + 64],
                pltpu.roll(parts[2][first + 64 : first + 128], 64, 1),
            ).astype(BF)

    def send_context(r, h):
        there = buf["cr"].at[r, h, me]
        ctx_copies[r, h] = [
            send(buf["cs"].at[r, h, core], there, over),
            send(buf["cs"].at[r, h, 1 - core], there, over_mate),
            send(buf["cs"].at[r, h, 1 - core], there, mate),
        ]
        buf["cr"][r, h, me] = buf["cs"][r, h, core]

    weight_copies = {}

    def send_weight():
        weight_copies["over"] = send(wo_h, buf["wo"].at[me, 0:192], over)
        weight_copies["mate"] = send(wo_h, buf["wo"].at[me, 0:192], mate)

    def forward_weight():
        weight_copies["over"].wait_recv()
        theirs = buf["wo"].at[(1 - chip) * 2 + core, 0:192]
        weight_copies["far"] = send(theirs, theirs, mate)

    def complete_weight():
        got_wo.wait()
        weight_copies["mate"].wait_recv()
        weight_copies["far"].wait_recv()
        for group in range(4):
            buf["wo"][group, 192:256] = buf["wo"][group, 128:192]

    flow_copies = {}

    def first_norm(r, h):
        for copy in ctx_copies[r, h]:
            copy.wait_recv()
        total = None
        for group in range(4):
            packed = buf["cr"][r, h, group, 128:192]
            zero = jnp.zeros_like(packed)
            keep = lane[0:64] < 64
            left = jnp.concatenate(
                [
                    buf["cr"][r, h, group, 0:128],
                    jnp.concatenate(
                        [jnp.where(keep, packed, zero), jnp.where(keep, zero, packed)], axis=0
                    ),
                ],
                axis=1,
            )
            term = dot(left, buf["wo"][group], 1, 0).astype(BF).astype(F32)
            total = term if total is None else total + term
        at = pl.ds(h * 128, 128)
        first_in = buf["tok"][r, h, core].astype(F32) + total + vec[1:2, :]
        center = first_in - mean_of(first_in)
        scale = lax.rsqrt(mean_of(center * center) + EPS)
        unit = center * scale
        buf["n1"][r, at, :] = unit
        buf["r1"][r, at, :] = scale
        first_out = unit * vec[2:3, :] + vec[3:4, :]
        buf["fo"][r, at, :] = first_out
        buf["flow"][r, h, core] = first_out.astype(BF)
        own = buf["flow"].at[r, h, core]
        flow_copies[r, h] = send(own, own, mate)

    pair_copies = {}
    cross_copies = {}

    def ffn_forward(r, h):
        flow_copies[r, h].wait_recv()
        loaded(got_wu)
        loaded(got_wd)
        rows_in = buf["flow"][r, h].reshape(256, 768)
        for part in range(3):
            at = pl.ds(part * 256, 256)
            hidden = dot(rows_in, buf["wu"][:, at], 1, 0) + vec[4:5, at]
            phi = 0.5 * (1.0 + lax.erf(hidden * 0.7071067811865476))
            buf["act"][r, h, :, at] = (hidden * phi).astype(BF)
            buf["gp"][r, h, :, at] = (
                phi + hidden * jnp.exp(-0.5 * hidden * hidden) * 0.3989422804014327
            )
        terms = dot(buf["act"][r, h], buf["wd"][...], 1, 0).astype(BF)
        buf["p2"][r, h] = terms.reshape(2, 128, 768)
        pair_copies[2, r, h] = send(buf["p2"].at[r, h, 1 - core], buf["p2r"].at[r, h], mate)

    def exchange(stage, r, h):
        pair_copies[stage, r, h].wait_recv()
        own = buf["p%d" % stage][r, h, core].astype(F32)
        other = buf["p%dr" % stage][r, h].astype(F32)
        buf["x%d" % stage][r, h] = (own + other).astype(BF)
        cross_copies[stage, r, h] = send(
            buf["x%d" % stage].at[r, h], buf["x%dr" % stage].at[r, h], over
        )

    def crossed(stage, r, h):
        cross_copies[stage, r, h].wait_recv()
        return buf["x%d" % stage][r, h].astype(F32) + buf["x%dr" % stage][r, h].astype(F32)

    dsl_copies = {}

    def second_norm(r, h):
        loaded(got_cot)
        total = crossed(2, r, h)
        at = pl.ds(h * 128, 128)
        second_in = buf["fo"][r, at, :] + total + vec[5:6, :]
        center = second_in - mean_of(second_in)
        scale = lax.rsqrt(mean_of(center * center) + EPS)
        unit = center * scale

        @pl.when(chip == r)
        def _():
            layer = unit * vec[6:7, :] + vec[7:8, :]
            outs[0][at, :] = layer.astype(BF)

        grad = buf["cot"][r, h].astype(F32)
        scaled = grad * vec[6:7, :]
        d_second = scale * (scaled - mean_of(scaled) - unit * mean_of(scaled * unit))
        buf["ds"][r, at, :] = d_second
        buf["dsl"][r, h, core] = d_second.astype(BF)
        own = buf["dsl"].at[r, h, core]
        dsl_copies[r, h] = send(own, own, mate)
        buf["vs"][0:1, :] += row_sum(grad * unit)
        buf["vs"][1:2, :] += row_sum(grad)
        buf["vs"][2:3, :] += row_sum(d_second)
        finished.append("layer")
        if finished.count("layer") == 2 * rows:
            emit(0)

    def ffn_backward(r, h):
        arrive(dsl_copies[r, h])
        rows_in = buf["dsl"][r, h].reshape(256, 768)
        for part in range(3):
            at = pl.ds(part * 256, 256)
            d_hidden = dot(rows_in, buf["wd"][at, :], 1, 1) * buf["gp"][r, h, :, at]
            buf["vs"][6:7, at] += row_sum(d_hidden)
            buf["dhl"][r, h, :, at] = d_hidden.astype(BF)
        terms = dot(buf["dhl"][r, h], buf["wu"][...], 1, 1).astype(BF)
        buf["p3"][r, h] = terms.reshape(2, 128, 768)
        pair_copies[3, r, h] = send(buf["p3"].at[r, h, 1 - core], buf["p3r"].at[r, h], mate)

    dal_copies = {}

    def first_norm_back(r, h):
        total = crossed(3, r, h)
        at = pl.ds(h * 128, 128)
        d_first = buf["ds"][r, at, :] + total
        unit = buf["n1"][r, at, :]
        scaled = d_first * vec[2:3, :]
        d_in = buf["r1"][r, at, :] * (scaled - mean_of(scaled) - unit * mean_of(scaled * unit))
        buf["dfi"][r, at, :] = d_in
        buf["dal"][r, h, core] = d_in.astype(BF)
        own = buf["dal"].at[r, h, core]
        dal_copies[r, h] = send(own, own, mate)
        buf["vs"][3:4, :] += row_sum(d_first * unit)
        buf["vs"][4:5, :] += row_sum(d_first)
        buf["vs"][5:6, :] += row_sum(d_in)

    out_parts = []

    def attention_back(r):
        for h in range(2):
            arrive(dal_copies[r, h])
        buf["dctx"][...] = dot(
            buf["dal"][r].reshape(512, 768), buf["wo"][me], 1, 1
        ).astype(BF)
        q_a = buf["mix"][r, :, 0:128]
        k_a = buf["mix"][r, :, 128:256]
        v_a = buf["mix"][r, :, 256:384]
        qk_roll = buf["mixr"][r]
        v_b = buf["mix"][r, :, 512:640]
        d_q, d_k, d_v = [], [], []
        for head in range(3):
            tile = pl.ds((head // 2) * 128, 128)
            value = v_a if head < 2 else v_b
            for h in range(2):
                at = pl.ds(h * 256, 256)
                d_rows = buf["dctx"][at, tile]
                if head == 0:
                    d_rows = jnp.where(low_half, d_rows, jnp.zeros_like(d_rows))
                if head == 1:
                    d_rows = jnp.where(low_half, jnp.zeros_like(d_rows), d_rows)
                probs = buf["prob"][r, head, at, :]
                weighted = probs * dot(d_rows, value, 1, 1)
                inner = jnp.sum(weighted, axis=-1, keepdims=True)
                buf["dsc"][head, at, :] = (weighted - probs * inner).astype(BF)
            d_scores = buf["dsc"][head]
            d_q.append(dot(d_scores, k_a if head < 2 else qk_roll, 1, 0))
            d_k.append(dot(d_scores, q_a if head < 2 else qk_roll, 0, 0))
            d_v.append(dot(buf["prob"][r, head].astype(BF), buf["dctx"][:, tile], 0, 0))
        tiles = [
            jnp.where(lane_row, d_q[0], d_q[1]) * SCALE,
            jnp.where(lane_row, d_k[0], d_k[1]),
            jnp.where(lane_row, d_v[0], d_v[1]),
            jnp.where(lane_row, d_q[2] * SCALE, d_k[2]),
            jnp.where(lane_row, d_v[2], 0.0),
        ]
        for at, tile in enumerate(tiles):
            lanes = pl.ds(at * 128, 128)
            buf["dmx"][r, :, lanes] = tile.astype(BF)
            if at != 1:
                buf["vs"][7:8, lanes] += row_sum(tile)

    tok_copies = []

    def token_terms(r, h):
        terms = dot(
            buf["dmx"][r, h * 256 : h * 256 + 256, :], buf["wq"][...].reshape(640, 768), 1, 0
        )
        buf["p4"][r, h] = terms.astype(BF).reshape(2, 128, 768)
        pair_copies[4, r, h] = send(buf["p4"].at[r, h, 1 - core], buf["p4r"].at[r, h], mate)

    cross4 = [remote(buf["x4"].at[h], buf["x4r"].at[h], over) for h in range(2)]

    def token_cross(r, h):
        pair_copies[4, r, h].wait_recv()

        @pl.when(chip != r)
        def _():
            own = buf["p4"][r, h, core].astype(F32)
            other = buf["p4r"][r, h].astype(F32)
            buf["x4"][h] = (own + other).astype(BF)
            cross4[h].start()

    def token_finish(h):
        cross4[h].wait_recv()
        own = buf["p4"][chip, h, core].astype(F32)
        other = buf["p4r"][chip, h].astype(F32)
        pair = (own + other).astype(BF).astype(F32)
        total = pair + buf["x4r"][h].astype(F32)
        result = buf["dfi"][chip, pl.ds(h * 128, 128), :] + total
        outs[1][h * 128 : h * 128 + 128, :] = result.astype(BF)
        finished.append("token")
        if finished.count("token") == 2:
            emit(1)

    steps = {}
    starts = {}
    column = 0
    for name, width in PIECES:
        starts[name] = column
        column += width
    finished = []

    def piece(name):
        return [buf[kind + name] for kind in ("g_", "a_", "s_", "b_", "v_", "c_")]

    def reduce_start(name):
        grad = gradient(name)
        width = dict(PIECES)[name]
        if not fused:
            outs[2][:, starts[name] : starts[name] + width] = grad
            finished.append(name)
            if len(set(finished) & set(starts)) == len(PIECES):
                emit(2)
            return
        stage, came = piece(name)[:2]
        stage[...] = grad.astype(BF).reshape(stage.shape)
        if name in DEPTH_FIRST:
            steps[name] = send(stage.at[:, 1 - near], came, next_near)
        else:
            steps[name] = send(stage.at[:, :, 1 - why], came, side)

    def reduce_first(name):
        if not fused:
            return
        steps[name].wait_recv()
        stage, came, out, into = piece(name)[:4]
        for at in range(2):
            if name in DEPTH_FIRST:
                total = stage[1 - far, near, at].astype(F32) + came[1 - far, at].astype(F32)
            else:
                total = stage[at, 1 - near, why].astype(F32) + came[at, 1 - near].astype(F32)
            out[at] = total.astype(BF)
        steps[name] = send(out, into, next_far if name in DEPTH_FIRST else next_near)

    def reduce_second(name):
        if not fused:
            return
        steps[name].wait_recv()
        stage, came, _, into, out, last = piece(name)
        if name in DEPTH_FIRST:
            total = stage[far, near, 1 - why].astype(F32) + came[far, 1 - why].astype(F32)
            total = total + into[1 - why].astype(F32)
        else:
            total = stage[1 - far, near, why].astype(F32) + came[1 - far, near].astype(F32)
            total = total + into[1 - far].astype(F32)
        out[...] = total.astype(BF)
        steps[name] = send(out, last, side if name in DEPTH_FIRST else next_far)

    def emit(*which):
        for at in which:
            stored.append(fetch(outs[at], results[at]))

    def reduce_finish(name):
        if not fused:
            return
        steps[name].wait_recv()
        stage, came, _, into, _, last = piece(name)
        total = stage[far, near, why].astype(F32)
        if name in DEPTH_FIRST:
            total = total + came[far, why].astype(F32) + into[why].astype(F32)
        else:
            total = total + came[far, near].astype(F32) + into[far].astype(F32)
        total = total + last[...].astype(F32)
        if name[0] == "d":
            outs[10][:, starts[name] : starts[name] + 256] = total
        elif name[0] == "u":
            at = starts[name] - starts["u0"]
            outs[8][:, at : at + 256] = total
        elif name == "o":
            outs[4][0:128, :] = total.T
        elif name == "q":
            for kind in range(3):
                outs[2][kind * 192 : kind * 192 + 128, :] = total[
                    :, kind * 128 : kind * 128 + 128
                ].T
        elif name == "r":
            flipped = total.T
            outs[2][128:192, :] = flipped[0:64]
            outs[2][320:384, :] = flipped[64:128]
        else:
            flipped = total.T
            outs[2][512:576, :] = flipped[0:64]
            outs[4][128:192, :] = flipped[64:128]
        before = set(finished)
        finished.append(name)
        for group, at in (("d0 d1 d2", 10), ("u0 u1 u2", 8), ("q r s", 2), ("o s", 4)):
            wanted = set(group.split())
            if wanted <= set(finished) and not wanted <= before:
                emit(at)

    def down_grad(part):
        for r in range(rows):
            for h in range(2):
                arrive(dsl_copies[r, h])
        at = pl.ds(part * 256, 256)
        return dot(
            buf["dsl"][...].reshape(rows * 512, 768),
            buf["act"][:, :, :, at].reshape(rows * 512, 256),
            0,
            0,
        )

    def up_grad(part):
        at = pl.ds(part * 256, 256)
        return dot(
            buf["flow"][...].reshape(rows * 512, 768),
            buf["dhl"][:, :, :, at].reshape(rows * 512, 256),
            0,
            0,
        )

    def all_back():
        for r in range(rows):
            for h in range(2):
                arrive(dal_copies[r, h])

    def out_grad_first():
        all_back()
        return dot(
            buf["dal"][...].reshape(rows * 512, 768),
            buf["ctx"][:, :, 0:128].reshape(rows * 512, 128),
            0,
            0,
        )

    def out_grad_second():
        all_back()
        turned = dot(
            buf["dal"][...].reshape(rows * 512, 768),
            buf["ctx"][:, :, 128:256].reshape(rows * 512, 128),
            0,
            0,
        )
        return pltpu.roll(turned, 64, 1)

    def qkv_grad(low, high):
        return dot(
            buf["tok"][...].reshape(rows * 512, 768),
            buf["dmx"][:, :, low:high].reshape(rows * 512, high - low),
            0,
            0,
        )

    def gradient(name):
        if name[0] == "d":
            return down_grad(int(name[1]))
        if name[0] == "u":
            return up_grad(int(name[1]))
        if name == "o":
            return out_grad_first()
        if name == "q":
            return qkv_grad(0, 384)
        if name == "r":
            return qkv_grad(384, 512)
        first = lax.broadcasted_iota(jnp.int32, (768, 128), 1) < 64
        return jnp.where(first, qkv_grad(512, 640), out_grad_second())

    small_copies = {}

    def small_mate():
        small_copies["mate"] = send(buf["vs"], buf["vm"], mate)

    def small_side():
        small_copies["mate"].wait_recv()
        shared = lax.broadcasted_iota(jnp.int32, (8, 768), 0) < 6
        small = buf["vs"][...] + jnp.where(shared, buf["vm"][...], 0.0)
        if not fused:
            outs[3][...] = small
            emit(3)
            return
        buf["vt"][...] = small
        small_copies["side"] = send(buf["vt"], buf["vy"], side)

    def small_near():
        if not fused:
            return
        small_copies["side"].wait_recv()
        buf["vu"][...] = buf["vt"][...] + buf["vy"][...]
        small_copies["near"] = send(buf["vu"], buf["vz"], next_near)

    def small_far():
        if not fused:
            return
        small_copies["near"].wait_recv()
        buf["vw"][...] = buf["vu"][...] + buf["vz"][...]
        small_copies["far"] = send(buf["vw"], buf["vx"], next_far)

    def small_finish():
        if not fused:
            return
        small_copies["far"].wait_recv()
        small = buf["vw"][...] + buf["vx"][...]
        share = 768 // n_dp
        turned = pltpu.roll(small, 768 - dp * share, 1)
        for row, at in ((5, 5), (3, 6), (4, 7), (2, 11), (0, 12), (1, 13)):
            outs[at][...] = turned[row : row + 1, 0:share]
        wide = HEAD // n_dp
        lanes = lax.broadcasted_iota(jnp.int32, (8, 768), 1)
        depth = lax.broadcasted_iota(jnp.int32, (8, 768), 0)
        spread = jnp.where(lax.rem(lanes, HEAD) == depth + dp * wide, small[6:7, :], 0.0)
        group = lax.broadcasted_iota(jnp.int32, (768, 128), 0) // HEAD
        pick = (group == lax.broadcasted_iota(jnp.int32, (768, 128), 1)).astype(F32)
        outs[9][...] = jnp.dot(spread, pick, precision=lax.Precision.HIGHEST)[0:wide, 0:12]
        group = lanes // HEAD
        where = jnp.where(
            depth < 4,
            lax.rem(depth, 2) * 4 + depth // 2,
            jnp.where(depth == 4, 6, 8),
        )
        spread = jnp.where((group == where) & (depth < 6), small[7:8, :], 0.0)
        inside = lax.rem(lax.broadcasted_iota(jnp.int32, (768, 128), 0), HEAD)
        pick = (inside == lax.broadcasted_iota(jnp.int32, (768, 128), 1) + dp * wide).astype(F32)
        heads = jnp.dot(spread, pick, precision=lax.Precision.HIGHEST)
        for head in range(3):
            outs[3][head] = heads[head * 2 : head * 2 + 2, 0:wide]
        emit(3, 5, 6, 7, 9, 11, 12, 13)

    project(1)
    attend(1, 1)
    project(0)
    pl.semaphore_wait(barrier, len(partners))
    send_weight()
    attend(0, 1)
    send_context(1, 1)
    attend(1, 0)
    send_context(1, 0)
    attend(0, 0)
    send_context(0, 0)
    send_context(0, 1)
    forward_weight()
    complete_weight()
    first_norm(1, 1)
    ffn_forward(1, 1)
    first_norm(1, 0)
    first_norm(0, 0)
    exchange(2, 1, 1)
    ffn_forward(1, 0)
    first_norm(0, 1)
    ffn_forward(0, 0)
    exchange(2, 1, 0)
    ffn_forward(0, 1)
    exchange(2, 0, 0)
    exchange(2, 0, 1)
    second_norm(1, 1)
    ffn_backward(1, 1)
    exchange(3, 1, 1)
    second_norm(1, 0)
    ffn_backward(1, 0)
    second_norm(0, 0)
    exchange(3, 1, 0)
    ffn_backward(0, 0)
    second_norm(0, 1)
    exchange(3, 0, 0)
    reduce_start("d1")
    reduce_start("d0")
    reduce_start("d2")
    ffn_backward(0, 1)
    reduce_start("u1")
    reduce_start("u0")
    exchange(3, 0, 1)
    reduce_start("u2")
    first_norm_back(1, 1)
    first_norm_back(1, 0)
    reduce_first("d1")
    reduce_first("d0")
    attention_back(1)
    first_norm_back(0, 0)
    reduce_first("d2")
    token_terms(1, 1)
    reduce_first("u2")
    token_terms(1, 0)
    token_cross(1, 1)
    token_cross(1, 0)
    first_norm_back(0, 1)
    reduce_first("u1")
    reduce_second("d0")
    reduce_start("o")
    attention_back(0)
    reduce_start("q")
    reduce_second("d2")
    reduce_first("u0")
    token_terms(0, 0)
    small_mate()
    reduce_start("s")
    reduce_second("u1")
    reduce_second("d1")
    token_terms(0, 1)
    token_cross(0, 0)
    reduce_second("u2")
    small_side()
    reduce_start("r")
    reduce_first("o")
    token_cross(0, 1)
    reduce_finish("d0")
    reduce_finish("d2")
    reduce_second("u0")
    reduce_first("q")
    token_finish(0)
    reduce_second("o")
    reduce_finish("u1")
    reduce_first("s")
    reduce_finish("d1")
    reduce_finish("u0")
    reduce_finish("u2")
    token_finish(1)
    small_near()
    reduce_second("q")
    reduce_first("r")
    reduce_second("s")
    reduce_finish("o")
    small_far()
    reduce_second("r")
    reduce_finish("q")
    reduce_finish("s")
    small_finish()
    reduce_finish("r")
    for copy in pending + cross4:
        copy.wait_send()
    for copy in stored:
        copy.wait()


def body(
    tokens,
    segment_ids,
    qkv_weight,
    qkv_bias,
    output_weight,
    output_bias,
    first_gain,
    first_shift,
    up_weight,
    up_bias,
    down_weight,
    down_bias,
    second_gain,
    second_shift,
    cotangent,
):
    rows = tokens.shape[0] // SEQ
    n_dp = lax.axis_size("dp")
    share = 768 // n_dp
    fused = n_dp == 8
    split = (rows, 2, 2, 128, 768)
    shape = jax.ShapeDtypeStruct
    outs = [shape((256, 768), BF), shape((256, 768), BF)]
    if fused:
        wide = HEAD // n_dp
        vector = shape((1, share), F32)
        outs += [
            shape((576, share), F32),
            shape((3, 2, wide), F32),
            shape((192, share), F32),
            vector,
            vector,
            vector,
            shape((share, 768), F32),
            shape((wide, 12), F32),
            shape((share, 768), F32),
            vector,
            vector,
            vector,
        ]
    else:
        outs += [shape((768, 2304), F32), shape((8, 768), F32)]
    plan = scratch_plan(rows, share, fused, outs)
    anywhere = pl.BlockSpec(memory_space=pl.ANY)

    def kernel(*refs):
        layer_kernel(rows, n_dp, fused, list(plan), *refs)

    got = pl.pallas_call(
        kernel,
        out_shape=outs,
        in_specs=[anywhere] * INPUTS,
        out_specs=[anywhere] * len(outs),
        scratch_shapes=[pltpu.VMEM(dims, kind) for dims, kind in plan.values()]
        + [
            pltpu.SemaphoreType.DMA((LOCAL_COPIES,)),
            pltpu.SemaphoreType.DMA((REMOTE_COPIES,)),
            pltpu.SemaphoreType.DMA((REMOTE_COPIES,)),
        ],
        compiler_params=pltpu.CompilerParams(
            collective_id=0, has_side_effects=True, vmem_limit_bytes=62 * 1024 * 1024
        ),
    )(
        tokens.reshape(split),
        cotangent.reshape(split),
        qkv_weight.transpose(1, 2, 3, 0).reshape(3, 192, 768),
        output_weight.reshape(192, 768),
        up_weight,
        down_weight,
        segment_ids,
        qkv_bias.transpose(1, 0, 2),
        up_bias,
        *(
            vector.reshape(6, 128)
            for vector in (
                output_bias,
                first_gain,
                first_shift,
                down_bias,
                second_gain,
                second_shift,
            )
        ),
    )
    if fused:
        got = hand_over(got)
    else:
        got = finish_plain(n_dp, *got)
    return (
        got[0],
        got[1],
        got[2].reshape(3, 3, HEAD, share).transpose(3, 0, 1, 2),
        got[3].transpose(1, 0, 2),
        got[4].reshape(3, HEAD, share),
        got[5].reshape(share),
        got[6].reshape(share),
        got[7].reshape(share),
        got[8],
        got[9].T,
        got[10].T,
        got[11].reshape(share),
        got[12].reshape(share),
        got[13].reshape(share),
    )


def hand_over(arrays):
    count = len(arrays)

    def kernel(*refs):
        source, result, held = (refs[at * count : at * count + count] for at in range(3))
        sem = refs[3 * count]
        inward = [
            pltpu.make_async_copy(source[at], held[at], sem.at[at]) for at in range(count)
        ]
        outward = [
            pltpu.make_async_copy(held[at], result[at], sem.at[count + at]) for at in range(count)
        ]
        for copy in inward:
            copy.start()
        for before, after in zip(inward, outward):
            before.wait()
            after.start()
        for copy in outward:
            copy.wait()

    anywhere = pl.BlockSpec(memory_space=pl.ANY)
    return pl.pallas_call(
        kernel,
        out_shape=[jax.ShapeDtypeStruct(a.shape, a.dtype) for a in arrays],
        in_specs=[anywhere] * count,
        out_specs=[anywhere] * count,
        scratch_shapes=[pltpu.VMEM(a.shape, a.dtype) for a in arrays]
        + [pltpu.SemaphoreType.DMA((2 * count,))],
    )(*arrays)


def finish_plain(n_dp, layer, tokens_grad, grads, small):
    share = 768 // n_dp
    grads = lax.psum_scatter(grads, "dp", scatter_dimension=0, tiled=True)
    small = lax.psum(small, "dp")
    dp = lax.axis_index("dp")
    wide = HEAD // n_dp
    turned = lax.dynamic_slice_in_dim(small, dp * share, share, 1)
    up_bias = lax.dynamic_slice_in_dim(small[6].reshape(12, HEAD), dp * wide, wide, 1)
    row = small[7]
    sums = jnp.stack(
        [row[0:64], row[256:320], row[64:128], row[320:384], row[384:448], row[512:576]]
    )
    sums = lax.dynamic_slice_in_dim(sums, dp * wide, wide, 1)
    down, up = grads[:, 0:768], grads[:, 768:1536]
    out_a, main, tail = grads[:, 1536:1664], grads[:, 1664:2048], grads[:, 2048:2304]
    qkv = jnp.concatenate(
        [
            main[:, 0:128],
            tail[:, 0:64],
            main[:, 128:256],
            tail[:, 64:128],
            main[:, 256:384],
            tail[:, 128:192],
        ],
        axis=1,
    )
    out = jnp.concatenate([out_a, tail[:, 192:256]], axis=1)
    return [
        layer,
        tokens_grad,
        qkv.T,
        sums.reshape(3, 2, wide),
        out.T,
        turned[5],
        turned[3],
        turned[4],
        up,
        up_bias.T,
        down,
        turned[2],
        turned[0],
        turned[1],
    ]


def solution(mesh):
    placed = (
        P("dp", None),
        P("dp", None),
        P(None, None, "tensor", None),
        P(None, "tensor", None),
        P("tensor", None, None),
        P(),
        P(),
        P(),
        P(None, "tensor"),
        P("tensor", None),
        P("tensor", None),
        P(),
        P(),
        P(),
        P("dp", None),
    )
    return jax.shard_map(
        body,
        mesh=mesh,
        in_specs=placed,
        out_specs=(
            P(("dp", "tensor"), None),
            P(("dp", "tensor"), None),
            P("dp", None, "tensor", None),
            P(None, "tensor", "dp"),
            P("tensor", None, "dp"),
            P("dp"),
            P("dp"),
            P("dp"),
            P("dp", "tensor"),
            P("tensor", "dp"),
            P("tensor", "dp"),
            P("dp"),
            P("dp"),
            P("dp"),
        ),
        check_vma=False,
    )
```

```python
from types import SimpleNamespace

import jax
import jax.numpy as jnp
from jax import lax
from jax.experimental import pallas as pl
from jax.experimental.pallas import tpu as pltpu
from jax.sharding import PartitionSpec as P

HEAD = 64
SEQ = 512
EPS = 1e-12
SCALE = HEAD ** (-0.5)
BF = jnp.bfloat16
F32 = jnp.float32
MESH_ID = pl.DeviceIdType.MESH
NAMES = ("dp", "tensor")
D0, D1, D2, U0, U1, U2, OUT, QK, V, QK2, V2 = range(11)
WIDTHS = (256, 256, 256, 256, 256, 256, 128, 256, 128, 128, 128)
DEPTH_FIRST = (D0, U2)


def dot(left, right, left_dim, right_dim):
    return lax.dot_general(
        left, right, (((left_dim,), (right_dim,)), ((), ())), preferred_element_type=F32
    )


def mean_of(values):
    return jnp.mean(values, axis=-1, keepdims=True)


def row_sum(values):
    return jnp.sum(values, axis=0, keepdims=True)


def scratch_plan(rows, share, fused, results):
    plan = dict(
        seg=((rows, SEQ), jnp.int32),
        bqv=((3, 2, HEAD), BF),
        bup=((12, HEAD), BF),
        vec=((8, 768), F32),
        tok=((rows, 2, 2, 128, 768), BF),
        cot=((rows, 2, 128, 768), BF),
        wq=((5, 128, 768), BF),
        wo=((4, 256, 768), BF),
        wu=((768, 768), BF),
        wd=((768, 768), BF),
        mix=((rows, 512, 640), BF),
        bias=((rows, 512, 512), F32),
        mixr=((rows, 512, 128), BF),
        prob=((rows, 3, 512, 512), F32),
        ctx=((rows, 512, 256), BF),
        cs=((rows, 2, 2, 192, 128), BF),
        cr=((rows, 2, 4, 192, 128), BF),
        n1=((rows, 256, 768), F32),
        r1=((rows, 256, 1), F32),
        fo=((rows, 256, 768), F32),
        flow=((rows, 2, 2, 128, 768), BF),
        act=((rows, 2, 256, 768), BF),
        gp=((rows, 2, 256, 768), F32),
        ds=((rows, 256, 768), F32),
        dsl=((rows, 2, 2, 128, 768), BF),
        dhl=((rows, 2, 256, 768), BF),
        dfi=((rows, 256, 768), F32),
        dal=((rows, 2, 2, 128, 768), BF),
        dctx=((512, 256), BF),
        dsc=((3, 512, 512), BF),
        dmx=((rows, 512, 640), BF),
        x4=((2, 128, 768), BF),
        x4r=((2, 128, 768), BF),
        vs=((8, 768), F32),
        vm=((8, 768), F32),
    )
    plan.update(
        pair=[((rows, 2, 2, 128, 768), BF)] * 3,
        paired=[((rows, 2, 128, 768), BF)] * 3,
        cross=[((rows, 2, 128, 768), BF)] * 2,
        crossed=[((rows, 2, 128, 768), BF)] * 2,
        given=[((6, 128), BF)] * 6,
        outs=[(result.shape, result.dtype) for result in results],
    )
    if fused:
        plan.update(
            small=[((8, 768), F32)] * 6,
            pieces=[
                [
                    ((2, 2, 2, share, width), BF),
                    ((2, 2, share, width), BF),
                    ((2, share, width), BF),
                    ((2, share, width), BF),
                    ((share, width), BF),
                    ((share, width), BF),
                ]
                for width in WIDTHS
            ],
        )
    return plan


def is_buffer(node):
    return isinstance(node, tuple)


INPUTS = 15
OVER, CORNER, PAIR, ROWS, CROSS = range(5)
FIRST_ROW = 0
LOCAL_COPIES = 21
REMOTE_COPIES = 60


def layer_kernel(rows, n_dp, fused, tree, *refs):
    tok_h, cot_h, wq_h, wo_h, wu_h, wd_h, seg_h = refs[:7]
    small_h = refs[7:INPUTS]
    n_out = 14 if fused else 4
    results = refs[INPUTS : INPUTS + n_out]
    held = tree.num_leaves
    buf = SimpleNamespace(
        **jax.tree.unflatten(tree, refs[INPUTS + n_out : INPUTS + n_out + held])
    )
    outs, seg, vec = buf.outs, buf.seg, buf.vec
    local_sem, send_sem, recv_sem = refs[INPUTS + n_out + held :]

    dp = lax.axis_index("dp")
    me = lax.axis_index("tensor")
    chip = me // 2
    core = lax.rem(me, 2)
    mate = (dp, chip * 2 + (1 - core))
    over = (dp, (1 - chip) * 2 + core)
    over_mate = (dp, (1 - chip) * 2 + (1 - core))
    why = lax.rem(dp, 2)
    near = lax.rem(dp // 2, 2)
    far = dp // 4
    side = (dp + 1 - 2 * why, me)
    next_near = (dp + 2 - 4 * near, me)
    next_far = (dp + 4 - 8 * far, me)

    fetched = []
    stored, token_rows, layer_rows = [], [], []

    def fetch(src, dst, at=None):
        if at is None:
            at = len(fetched)
            fetched.append(at)
        copy = pltpu.make_async_copy(src, dst, local_sem.at[at])
        copy.start()
        return copy

    keys = {}
    latest = {}

    def remote(src, dst, device, key):
        at = keys.setdefault(key, len(keys))
        copy = pltpu.make_async_remote_copy(
            src_ref=src,
            dst_ref=dst,
            send_sem=send_sem.at[at],
            recv_sem=recv_sem.at[at],
            device_id=device,
            device_id_type=MESH_ID,
        )
        if key in latest:
            latest[key].wait_send()
        latest[key] = copy
        return copy

    arrived = []

    def once(copy):
        new = not any(copy is other for other in arrived)
        if new:
            arrived.append(copy)
        return new

    def arrive(copy):
        if once(copy):
            copy.wait_recv()

    def loaded(copy):
        if once(copy):
            copy.wait()

    def send(src, dst, device, key):
        copy = remote(src, dst, device, key)
        copy.start()
        return copy

    partners = [mate, over, over_mate]
    if fused:
        partners += [side, next_near, next_far]
    barrier = pltpu.get_barrier_semaphore()
    for device in partners:
        pl.semaphore_signal(barrier, inc=1, device_id=device, device_id_type=MESH_ID)
    got_tok = [None] * rows

    def fetch_row(r):
        got_tok[r] = [fetch(tok_h.at[r, :, h], buf.tok.at[r, h]) for h in range(2)]

    lane = lax.broadcasted_iota(jnp.int32, (256, 128), 1)
    low_half = lane < 64
    lane_row = lax.broadcasted_iota(jnp.int32, (512, 128), 1) < 64
    later = SimpleNamespace()

    def fetch_all():
        fetch_row(FIRST_ROW)
        later.wq = [
            fetch(wq_h.at[:, 0:128], buf.wq.at[0:3]),
            fetch(wq_h.at[0, 128:192], buf.wq.at[3, 0:64]),
            fetch(wq_h.at[1, 128:192], buf.wq.at[3, 64:128]),
            fetch(wq_h.at[2, 128:192], buf.wq.at[4, 0:64]),
        ]
        later.small = [fetch(seg_h, buf.seg), fetch(small_h[0], buf.bqv)]
        later.small.append(fetch(small_h[1], buf.bup))
        later.small += [fetch(small_h[2 + at], buf.given[at]) for at in range(6)]
        for r in range(rows):
            if r != FIRST_ROW:
                fetch_row(r)
        later.wo = fetch(wo_h, buf.wo.at[me, 0:192])
        later.wu = fetch(wu_h, buf.wu)
        later.wd = fetch(wd_h, buf.wd)
        later.cot = fetch(cot_h.at[:, core], buf.cot)

    def prepare():
        fetch_all()
        buf.wq[4, 64:128] = jnp.zeros((64, 768), BF)
        buf.vs[...] = jnp.zeros((8, 768), F32)
        for copy in later.small:
            copy.wait()
        bias = [[buf.bqv[head, kind : kind + 1, :].astype(F32) for kind in range(2)] for head in range(3)]
        none = jnp.zeros((1, HEAD), F32)
        none2 = jnp.zeros((1, 128), F32)
        for at, pair in enumerate(
            (
                (bias[0][0], bias[1][0]),
                (none, none),
                (bias[0][1], bias[1][1]),
                (bias[2][0], none),
                (bias[2][1], none),
            )
        ):
            vec[0:1, at * 128 : at * 128 + 128] = jnp.concatenate(pair, axis=1)
        vec[0:1, 640:768] = none2
        for at in range(6):
            pair = buf.bup[2 * at : 2 * at + 2, :].astype(F32)
            vec[4:5, at * 128 : at * 128 + 128] = jnp.concatenate([pair[0:1], pair[1:2]], axis=1)
        for at, row in enumerate((1, 2, 3, 5, 6, 7)):
            short = buf.given[at][...].astype(F32)
            for part in range(6):
                vec[row : row + 1, part * 128 : part * 128 + 128] = short[part : part + 1]

    ctx_copies = {}

    def project(r):
        for copy in got_tok[r]:
            copy.wait()
        for copy in later.wq:
            loaded(copy)
        mixed = dot(
            buf.tok[r].reshape(512, 768), buf.wq[...].reshape(640, 768), 1, 1
        ) + vec[0:1, 0:640]
        q_low = mixed[:, 0:128].astype(BF).astype(F32) * SCALE
        buf.mix[r, :, 0:128] = q_low.astype(BF)
        buf.mix[r, :, 128:384] = mixed[:, 128:384].astype(BF)
        tail = mixed[:, 384:512].astype(BF).astype(F32)
        tail = jnp.where(lane_row, tail * SCALE, tail)
        buf.mix[r, :, 384:512] = tail.astype(BF)
        buf.mixr[r] = pltpu.roll(tail, 64, 1).astype(BF)
        buf.mix[r, :, 512:640] = mixed[:, 512:640].astype(BF)

        ids = seg[r : r + 1, :].astype(F32)
        ids = jnp.concatenate(
            [ids[:, 0:128], ids[:, 256:384], ids[:, 128:256], ids[:, 384:512]], axis=1
        )
        column = jnp.broadcast_to(ids, (128, 512)).T
        buf.bias[r] = jnp.where(column[:, 0:1] == ids, 0.0, -1e30)

    def attend(r, h):
        at = pl.ds(h * 256, 256)
        q_a = buf.mix[r, at, 0:128]
        q_b = buf.mix[r, at, 384:512]
        zero = jnp.zeros_like(q_a)
        parts = []
        for head in range(3):
            if head == 1:
                query = jnp.where(low_half, zero, q_a)
            else:
                query = jnp.where(low_half, q_b if head == 2 else q_a, zero)
            key = buf.mixr[r] if head == 2 else buf.mix[r, :, 128:256]
            value = buf.mix[r, :, 512:640] if head == 2 else buf.mix[r, :, 256:384]
            scores = dot(query, key, 1, 1) + buf.bias[r, at, :]
            top = jnp.max(scores, axis=-1, keepdims=True)
            expo = jnp.exp(scores - top)
            probs = expo * (1.0 / jnp.sum(expo, axis=-1, keepdims=True))
            buf.prob[r, head, at, :] = probs
            parts.append(dot(probs.astype(BF), value, 1, 0))
        both = jnp.where(low_half, parts[0], parts[1]).astype(BF)
        buf.ctx[r, at, 0:128] = both
        buf.ctx[r, at, 128:256] = parts[2].astype(BF)
        for part in range(2):
            first = part * 128
            buf.cs[r, h, part, 0:128] = both[first : first + 128]
            buf.cs[r, h, part, 128:192] = jnp.where(
                lane[0:64] < 64,
                parts[2][first : first + 64],
                pltpu.roll(parts[2][first + 64 : first + 128], 64, 1),
            ).astype(BF)

    def send_context(r, h):
        there = buf.cr.at[r, h, me]
        ctx_copies[r, h] = [
            send(buf.cs.at[r, h, core], there, over, (OVER, r, h)),
            send(buf.cs.at[r, h, 1 - core], there, over_mate, (CORNER, r, h)),
            send(buf.cs.at[r, h, 1 - core], there, mate, (PAIR, r, h)),
        ]
        buf.cr[r, h, me] = buf.cs[r, h, core]

    weight_copies = SimpleNamespace()

    def send_weight():
        weight_copies.over = send(wo_h, buf.wo.at[me, 0:192], over, 0)
        weight_copies.mate = send(wo_h, buf.wo.at[me, 0:192], mate, 1)

    def forward_weight():
        weight_copies.over.wait_recv()
        theirs = buf.wo.at[(1 - chip) * 2 + core, 0:192]
        weight_copies.far = send(theirs, theirs, mate, 2)

    def complete_weight():
        later.wo.wait()
        weight_copies.mate.wait_recv()
        weight_copies.far.wait_recv()
        for group in range(4):
            buf.wo[group, 192:256] = buf.wo[group, 128:192]

    flow_copies = {}

    def first_norm(r, h):
        for copy in ctx_copies[r, h]:
            copy.wait_recv()
        total = None
        for group in range(4):
            packed = buf.cr[r, h, group, 128:192]
            zero = jnp.zeros_like(packed)
            keep = lane[0:64] < 64
            left = jnp.concatenate(
                [
                    buf.cr[r, h, group, 0:128],
                    jnp.concatenate(
                        [jnp.where(keep, packed, zero), jnp.where(keep, zero, packed)], axis=0
                    ),
                ],
                axis=1,
            )
            term = dot(left, buf.wo[group], 1, 0).astype(BF).astype(F32)
            total = term if total is None else total + term
        at = pl.ds(h * 128, 128)
        first_in = buf.tok[r, h, core].astype(F32) + total + vec[1:2, :]
        center = first_in - mean_of(first_in)
        scale = lax.rsqrt(mean_of(center * center) + EPS)
        unit = center * scale
        buf.n1[r, at, :] = unit
        buf.r1[r, at, :] = scale
        first_out = unit * vec[2:3, :] + vec[3:4, :]
        buf.fo[r, at, :] = first_out
        buf.flow[r, h, core] = first_out.astype(BF)
        own = buf.flow.at[r, h, core]
        flow_copies[r, h] = send(own, own, mate, (ROWS, r, h))

    pair_copies = {}
    cross_copies = {}

    def ffn_forward(r, h):
        flow_copies[r, h].wait_recv()
        loaded(later.wu)
        loaded(later.wd)
        rows_in = buf.flow[r, h].reshape(256, 768)
        for part in range(3):
            at = pl.ds(part * 256, 256)
            hidden = dot(rows_in, buf.wu[:, at], 1, 0) + vec[4:5, at]
            phi = 0.5 * (1.0 + lax.erf(hidden * 0.7071067811865476))
            buf.act[r, h, :, at] = (hidden * phi).astype(BF)
            buf.gp[r, h, :, at] = (
                phi + hidden * jnp.exp(-0.5 * hidden * hidden) * 0.3989422804014327
            )
        terms = dot(buf.act[r, h], buf.wd[...], 1, 0).astype(BF)
        buf.pair[0][r, h] = terms.reshape(2, 128, 768)
        pair_copies[2, r, h] = send(
            buf.pair[0].at[r, h, 1 - core], buf.paired[0].at[r, h], mate, (PAIR, r, h)
        )

    def exchange(stage, r, h):
        pair_copies[stage, r, h].wait_recv()
        own = buf.pair[stage - 2][r, h, core].astype(F32)
        other = buf.paired[stage - 2][r, h].astype(F32)
        buf.cross[stage - 2][r, h] = (own + other).astype(BF)
        cross_copies[stage, r, h] = send(
            buf.cross[stage - 2].at[r, h],
            buf.crossed[stage - 2].at[r, h],
            over,
            (CROSS if stage == 2 else OVER, r, h),
        )

    def crossed(stage, r, h):
        cross_copies[stage, r, h].wait_recv()
        return buf.cross[stage - 2][r, h].astype(F32) + buf.crossed[stage - 2][r, h].astype(F32)

    dsl_copies = {}

    def second_norm(r, h):
        loaded(later.cot)
        total = crossed(2, r, h)
        at = pl.ds(h * 128, 128)
        second_in = buf.fo[r, at, :] + total + vec[5:6, :]
        center = second_in - mean_of(second_in)
        scale = lax.rsqrt(mean_of(center * center) + EPS)
        unit = center * scale

        @pl.when(chip == r)
        def _():
            layer = unit * vec[6:7, :] + vec[7:8, :]
            outs[0][at, :] = layer.astype(BF)

        grad = buf.cot[r, h].astype(F32)
        scaled = grad * vec[6:7, :]
        d_second = scale * (scaled - mean_of(scaled) - unit * mean_of(scaled * unit))
        buf.ds[r, at, :] = d_second
        buf.dsl[r, h, core] = d_second.astype(BF)
        own = buf.dsl.at[r, h, core]
        dsl_copies[r, h] = send(own, own, mate, (ROWS, r, h))
        buf.vs[0:1, :] += row_sum(grad * unit)
        buf.vs[1:2, :] += row_sum(grad)
        buf.vs[2:3, :] += row_sum(d_second)
        layer_rows.append((r, h))
        if len(layer_rows) == 2 * rows:
            emit(0)

    def ffn_backward(r, h):
        arrive(dsl_copies[r, h])
        rows_in = buf.dsl[r, h].reshape(256, 768)
        for part in range(3):
            at = pl.ds(part * 256, 256)
            d_hidden = dot(rows_in, buf.wd[at, :], 1, 1) * buf.gp[r, h, :, at]
            buf.vs[6:7, at] += row_sum(d_hidden)
            buf.dhl[r, h, :, at] = d_hidden.astype(BF)
        terms = dot(buf.dhl[r, h], buf.wu[...], 1, 1).astype(BF)
        buf.pair[1][r, h] = terms.reshape(2, 128, 768)
        pair_copies[3, r, h] = send(
            buf.pair[1].at[r, h, 1 - core], buf.paired[1].at[r, h], mate, (PAIR, r, h)
        )

    dal_copies = {}

    def first_norm_back(r, h):
        total = crossed(3, r, h)
        at = pl.ds(h * 128, 128)
        d_first = buf.ds[r, at, :] + total
        unit = buf.n1[r, at, :]
        scaled = d_first * vec[2:3, :]
        d_in = buf.r1[r, at, :] * (scaled - mean_of(scaled) - unit * mean_of(scaled * unit))
        buf.dfi[r, at, :] = d_in
        buf.dal[r, h, core] = d_in.astype(BF)
        own = buf.dal.at[r, h, core]
        dal_copies[r, h] = send(own, own, mate, (ROWS, r, h))
        buf.vs[3:4, :] += row_sum(d_first * unit)
        buf.vs[4:5, :] += row_sum(d_first)
        buf.vs[5:6, :] += row_sum(d_in)

    out_parts = []

    def attention_back(r):
        for h in range(2):
            arrive(dal_copies[r, h])
        buf.dctx[...] = dot(
            buf.dal[r].reshape(512, 768), buf.wo[me], 1, 1
        ).astype(BF)
        q_a = buf.mix[r, :, 0:128]
        k_a = buf.mix[r, :, 128:256]
        v_a = buf.mix[r, :, 256:384]
        qk_roll = buf.mixr[r]
        v_b = buf.mix[r, :, 512:640]
        d_q, d_k, d_v = [], [], []
        for head in range(3):
            tile = pl.ds((head // 2) * 128, 128)
            value = v_a if head < 2 else v_b
            for h in range(2):
                at = pl.ds(h * 256, 256)
                d_rows = buf.dctx[at, tile]
                if head == 0:
                    d_rows = jnp.where(low_half, d_rows, jnp.zeros_like(d_rows))
                if head == 1:
                    d_rows = jnp.where(low_half, jnp.zeros_like(d_rows), d_rows)
                probs = buf.prob[r, head, at, :]
                weighted = probs * dot(d_rows, value, 1, 1)
                inner = jnp.sum(weighted, axis=-1, keepdims=True)
                buf.dsc[head, at, :] = (weighted - probs * inner).astype(BF)
            d_scores = buf.dsc[head]
            d_q.append(dot(d_scores, k_a if head < 2 else qk_roll, 1, 0))
            d_k.append(dot(d_scores, q_a if head < 2 else qk_roll, 0, 0))
            d_v.append(dot(buf.prob[r, head].astype(BF), buf.dctx[:, tile], 0, 0))
        tiles = [
            jnp.where(lane_row, d_q[0], d_q[1]) * SCALE,
            jnp.where(lane_row, d_k[0], d_k[1]),
            jnp.where(lane_row, d_v[0], d_v[1]),
            jnp.where(lane_row, d_q[2] * SCALE, d_k[2]),
            jnp.where(lane_row, d_v[2], 0.0),
        ]
        for at, tile in enumerate(tiles):
            lanes = pl.ds(at * 128, 128)
            buf.dmx[r, :, lanes] = tile.astype(BF)
            if at != 1:
                buf.vs[7:8, lanes] += row_sum(tile)

    tok_copies = []

    def token_terms(r, h):
        terms = dot(
            buf.dmx[r, h * 256 : h * 256 + 256, :], buf.wq[...].reshape(640, 768), 1, 0
        )
        buf.pair[2][r, h] = terms.astype(BF).reshape(2, 128, 768)
        pair_copies[4, r, h] = send(
            buf.pair[2].at[r, h, 1 - core], buf.paired[2].at[r, h], mate, (PAIR, r, h)
        )

    cross4 = []

    def token_way():
        for h in range(2):
            cross4.append(remote(buf.x4.at[h], buf.x4r.at[h], over, (CROSS, 0, h)))

    def token_cross(r, h):
        if not cross4:
            token_way()
        pair_copies[4, r, h].wait_recv()

        @pl.when(chip != r)
        def _():
            own = buf.pair[2][r, h, core].astype(F32)
            other = buf.paired[2][r, h].astype(F32)
            buf.x4[h] = (own + other).astype(BF)
            cross4[h].start()

    def token_finish(h):
        cross4[h].wait_recv()
        own = buf.pair[2][chip, h, core].astype(F32)
        other = buf.paired[2][chip, h].astype(F32)
        pair = (own + other).astype(BF).astype(F32)
        total = pair + buf.x4r[h].astype(F32)
        result = buf.dfi[chip, pl.ds(h * 128, 128), :] + total
        outs[1][h * 128 : h * 128 + 128, :] = result.astype(BF)
        token_rows.append(h)
        if len(token_rows) == 2:
            emit(1)

    steps = {}
    starts = [sum(WIDTHS[:at]) for at in range(len(WIDTHS))]
    finished = []
    pieces = buf.pieces if fused else None

    def reduce_start(name):
        grad = gradient(name)
        width = WIDTHS[name]
        if not fused:
            outs[2][:, starts[name] : starts[name] + width] = grad
            finished.append(name)
            if len(finished) == len(WIDTHS):
                emit(2)
            return
        stage, came = pieces[name][:2]
        stage[...] = grad.astype(BF).reshape(stage.shape)
        if name in DEPTH_FIRST:
            steps[name] = send(stage.at[:, 1 - near], came, next_near, (-1, name))
        else:
            steps[name] = send(stage.at[:, :, 1 - why], came, side, (-1, name))

    def reduce_first(name):
        if not fused:
            return
        steps[name].wait_recv()
        stage, came, out, into = pieces[name][:4]
        for at in range(2):
            if name in DEPTH_FIRST:
                total = stage[1 - far, near, at].astype(F32) + came[1 - far, at].astype(F32)
            else:
                total = stage[at, 1 - near, why].astype(F32) + came[at, 1 - near].astype(F32)
            out[at] = total.astype(BF)
        steps[name] = send(
            out, into, next_far if name in DEPTH_FIRST else next_near, (-2, name)
        )

    def reduce_second(name):
        if not fused:
            return
        steps[name].wait_recv()
        stage, came, _, into, out, last = pieces[name]
        if name in DEPTH_FIRST:
            total = stage[far, near, 1 - why].astype(F32) + came[far, 1 - why].astype(F32)
            total = total + into[1 - why].astype(F32)
        else:
            total = stage[1 - far, near, why].astype(F32) + came[1 - far, near].astype(F32)
            total = total + into[1 - far].astype(F32)
        out[...] = total.astype(BF)
        steps[name] = send(out, last, side if name in DEPTH_FIRST else next_far, (-3, name))

    def emit(*which):
        for at in which:
            stored.append(fetch(outs[at], results[at], len(stored)))

    def reduce_finish(name):
        if not fused:
            return
        steps[name].wait_recv()
        stage, came, _, into, _, last = pieces[name]
        total = stage[far, near, why].astype(F32)
        if name in DEPTH_FIRST:
            total = total + came[far, why].astype(F32) + into[why].astype(F32)
        else:
            total = total + came[far, near].astype(F32) + into[far].astype(F32)
        total = total + last[...].astype(F32)
        flipped = None if name <= U2 else total.T
        if name <= D2:
            outs[10][:, starts[name] : starts[name] + 256] = total
        elif name <= U2:
            at = starts[name] - starts[U0]
            outs[8][:, at : at + 256] = total
        elif name == OUT:
            outs[4][0:128, :] = flipped
        elif name == QK:
            outs[2][0:128, :] = flipped[0:128]
            outs[2][192:320, :] = flipped[128:256]
        elif name == V:
            outs[2][384:512, :] = flipped
        elif name == QK2:
            outs[2][128:192, :] = flipped[0:64]
            outs[2][320:384, :] = flipped[64:128]
        else:
            outs[2][512:576, :] = flipped[0:64]
            outs[4][128:192, :] = flipped[64:128]
        before = set(finished)
        finished.append(name)
        after = set(finished)
        for group, at in (
            ({D0, D1, D2}, 10),
            ({U0, U1, U2}, 8),
            ({QK, V, QK2, V2}, 2),
            ({OUT, V2}, 4),
        ):
            if group <= after and not group <= before:
                emit(at)

    def down_grad(part):
        for r in range(rows):
            for h in range(2):
                arrive(dsl_copies[r, h])
        at = pl.ds(part * 256, 256)
        return dot(
            buf.dsl[...].reshape(rows * 512, 768),
            buf.act[:, :, :, at].reshape(rows * 512, 256),
            0,
            0,
        )

    def up_grad(part):
        at = pl.ds(part * 256, 256)
        return dot(
            buf.flow[...].reshape(rows * 512, 768),
            buf.dhl[:, :, :, at].reshape(rows * 512, 256),
            0,
            0,
        )

    def all_back():
        for r in range(rows):
            for h in range(2):
                arrive(dal_copies[r, h])

    def out_grad_first():
        all_back()
        return dot(
            buf.dal[...].reshape(rows * 512, 768),
            buf.ctx[:, :, 0:128].reshape(rows * 512, 128),
            0,
            0,
        )

    def out_grad_second():
        all_back()
        turned = dot(
            buf.dal[...].reshape(rows * 512, 768),
            buf.ctx[:, :, 128:256].reshape(rows * 512, 128),
            0,
            0,
        )
        return pltpu.roll(turned, 64, 1)

    def qkv_grad(low, high):
        return dot(
            buf.tok[...].reshape(rows * 512, 768),
            buf.dmx[:, :, low:high].reshape(rows * 512, high - low),
            0,
            0,
        )

    def gradient(name):
        if name <= D2:
            return down_grad(name)
        if name <= U2:
            return up_grad(name - U0)
        if name == OUT:
            return out_grad_first()
        if name == QK:
            return qkv_grad(0, 256)
        if name == V:
            return qkv_grad(256, 384)
        if name == QK2:
            return qkv_grad(384, 512)
        first = lax.broadcasted_iota(jnp.int32, (768, 128), 1) < 64
        return jnp.where(first, qkv_grad(512, 640), out_grad_second())

    small_copies = SimpleNamespace()

    def small_mate():
        small_copies.mate = send(buf.vs, buf.vm, mate, 3)

    def small_side():
        small_copies.mate.wait_recv()
        shared = lax.broadcasted_iota(jnp.int32, (8, 768), 0) < 6
        small = buf.vs[...] + jnp.where(shared, buf.vm[...], 0.0)
        if not fused:
            outs[3][...] = small
            emit(3)
            return
        buf.small[0][...] = small
        small_copies.side = send(buf.small[0], buf.small[1], side, 4)

    def small_near():
        if not fused:
            return
        small_copies.side.wait_recv()
        buf.small[2][...] = buf.small[0][...] + buf.small[1][...]
        small_copies.near = send(buf.small[2], buf.small[3], next_near, 5)

    def small_far():
        if not fused:
            return
        small_copies.near.wait_recv()
        buf.small[4][...] = buf.small[2][...] + buf.small[3][...]
        small_copies.far = send(buf.small[4], buf.small[5], next_far, 6)

    def small_finish():
        if not fused:
            return
        small_copies.far.wait_recv()
        small = buf.small[4][...] + buf.small[5][...]
        share = 768 // n_dp
        turned = pltpu.roll(small, 768 - dp * share, 1)
        for row, at in ((5, 5), (3, 6), (4, 7), (2, 11), (0, 12), (1, 13)):
            outs[at][...] = turned[row : row + 1, 0:share]
        wide = HEAD // n_dp
        lanes = lax.broadcasted_iota(jnp.int32, (8, 768), 1)
        depth = lax.broadcasted_iota(jnp.int32, (8, 768), 0)
        spread = jnp.where(lax.rem(lanes, HEAD) == depth + dp * wide, small[6:7, :], 0.0)
        group = lax.broadcasted_iota(jnp.int32, (768, 128), 0) // HEAD
        pick = (group == lax.broadcasted_iota(jnp.int32, (768, 128), 1)).astype(F32)
        outs[9][...] = jnp.dot(spread, pick, precision=lax.Precision.HIGHEST)[0:wide, 0:12]
        group = lanes // HEAD
        where = jnp.where(
            depth < 4,
            lax.rem(depth, 2) * 4 + depth // 2,
            jnp.where(depth == 4, 6, 8),
        )
        spread = jnp.where((group == where) & (depth < 6), small[7:8, :], 0.0)
        inside = lax.rem(lax.broadcasted_iota(jnp.int32, (768, 128), 0), HEAD)
        pick = (inside == lax.broadcasted_iota(jnp.int32, (768, 128), 1) + dp * wide).astype(F32)
        heads = jnp.dot(spread, pick, precision=lax.Precision.HIGHEST)
        for head in range(3):
            outs[3][head] = heads[head * 2 : head * 2 + 2, 0:wide]
        emit(3, 5, 6, 7, 9, 11, 12, 13)

    pl.semaphore_wait(barrier, len(partners))
    send_weight()
    prepare()
    project(0)
    attend(0, 1)
    send_context(0, 1)
    project(1)
    attend(1, 0)
    attend(1, 1)
    send_context(1, 1)
    forward_weight()
    attend(0, 0)
    send_context(0, 0)
    send_context(1, 0)
    complete_weight()
    first_norm(0, 1)
    ffn_forward(0, 1)
    first_norm(1, 1)
    exchange(2, 0, 1)
    first_norm(0, 0)
    ffn_forward(1, 1)
    ffn_forward(0, 0)
    first_norm(1, 0)
    exchange(2, 1, 1)
    exchange(2, 0, 0)
    ffn_forward(1, 0)
    second_norm(0, 1)
    exchange(2, 1, 0)
    ffn_backward(0, 1)
    exchange(3, 0, 1)
    second_norm(1, 1)
    ffn_backward(1, 1)
    second_norm(0, 0)
    exchange(3, 1, 1)
    ffn_backward(0, 0)
    exchange(3, 0, 0)
    second_norm(1, 0)
    reduce_start(D0)
    reduce_start(D1)
    reduce_start(D2)
    ffn_backward(1, 0)
    reduce_start(U2)
    first_norm_back(0, 1)
    reduce_start(U0)
    reduce_start(U1)
    exchange(3, 1, 0)
    first_norm_back(1, 1)
    reduce_first(D0)
    reduce_first(D1)
    first_norm_back(0, 0)
    reduce_first(U2)
    reduce_first(D2)
    attention_back(0)
    first_norm_back(1, 0)
    reduce_second(D1)
    token_terms(0, 1)
    reduce_second(D0)
    token_terms(0, 0)
    reduce_first(U0)
    reduce_start(OUT)
    attention_back(1)
    reduce_second(D2)
    reduce_start(V2)
    small_mate()
    token_cross(0, 1)
    token_cross(0, 0)
    reduce_start(QK)
    reduce_first(U1)
    reduce_finish(D0)
    reduce_start(V)
    reduce_finish(D1)
    reduce_second(U2)
    small_side()
    reduce_first(OUT)
    reduce_start(QK2)
    token_terms(1, 1)
    reduce_second(U0)
    token_terms(1, 0)
    reduce_first(V2)
    token_cross(1, 1)
    reduce_finish(D2)
    token_cross(1, 0)
    reduce_second(U1)
    reduce_second(OUT)
    reduce_first(QK)
    reduce_second(V2)
    reduce_finish(U0)
    reduce_first(V)
    token_finish(1)
    reduce_finish(U1)
    reduce_finish(U2)
    small_near()
    reduce_finish(OUT)
    reduce_second(QK)
    reduce_first(QK2)
    reduce_second(V)
    token_finish(0)
    small_far()
    reduce_finish(V2)
    reduce_second(QK2)
    reduce_finish(QK)
    reduce_finish(V)
    small_finish()
    reduce_finish(QK2)
    for copy in latest.values():
        copy.wait_send()
    for copy in stored:
        copy.wait()


def body(
    tokens,
    segment_ids,
    qkv_weight,
    qkv_bias,
    output_weight,
    output_bias,
    first_gain,
    first_shift,
    up_weight,
    up_bias,
    down_weight,
    down_bias,
    second_gain,
    second_shift,
    cotangent,
):
    rows = tokens.shape[0] // SEQ
    n_dp = lax.axis_size("dp")
    share = 768 // n_dp
    fused = n_dp == 8
    split = (rows, 2, 2, 128, 768)
    shape = jax.ShapeDtypeStruct
    outs = [shape((256, 768), BF), shape((256, 768), BF)]
    if fused:
        wide = HEAD // n_dp
        vector = shape((1, share), F32)
        outs += [
            shape((576, share), F32),
            shape((3, 2, wide), F32),
            shape((192, share), F32),
            vector,
            vector,
            vector,
            shape((share, 768), F32),
            shape((wide, 12), F32),
            shape((share, 768), F32),
            vector,
            vector,
            vector,
        ]
    else:
        outs += [shape((768, 2304), F32), shape((8, 768), F32)]
    plan = scratch_plan(rows, share, fused, outs)
    leaves, tree = jax.tree.flatten(plan, is_leaf=is_buffer)
    anywhere = pl.BlockSpec(memory_space=pl.ANY)

    def kernel(*refs):
        layer_kernel(rows, n_dp, fused, tree, *refs)

    got = pl.pallas_call(
        kernel,
        out_shape=outs,
        in_specs=[anywhere] * INPUTS,
        out_specs=[anywhere] * len(outs),
        scratch_shapes=[pltpu.VMEM(dims, kind) for dims, kind in leaves]
        + [
            pltpu.SemaphoreType.DMA((LOCAL_COPIES,)),
            pltpu.SemaphoreType.DMA((REMOTE_COPIES,)),
            pltpu.SemaphoreType.DMA((REMOTE_COPIES,)),
        ],
        compiler_params=pltpu.CompilerParams(
            collective_id=0, has_side_effects=True, vmem_limit_bytes=62 * 1024 * 1024
        ),
    )(
        tokens.reshape(split),
        cotangent.reshape(split),
        qkv_weight.transpose(1, 2, 3, 0).reshape(3, 192, 768),
        output_weight.reshape(192, 768),
        up_weight,
        down_weight,
        segment_ids,
        qkv_bias.transpose(1, 0, 2),
        up_bias,
        *(
            vector.reshape(6, 128)
            for vector in (
                output_bias,
                first_gain,
                first_shift,
                down_bias,
                second_gain,
                second_shift,
            )
        ),
    )
    if fused:
        got = hand_over(got)
    else:
        got = finish_plain(n_dp, *got)
    return (
        got[0],
        got[1],
        got[2].reshape(3, 3, HEAD, share).transpose(3, 0, 1, 2),
        got[3].transpose(1, 0, 2),
        got[4].reshape(3, HEAD, share),
        got[5].reshape(share),
        got[6].reshape(share),
        got[7].reshape(share),
        got[8],
        got[9].T,
        got[10].T,
        got[11].reshape(share),
        got[12].reshape(share),
        got[13].reshape(share),
    )


def hand_over(arrays):
    count = len(arrays)

    def kernel(*refs):
        source, result, held = (refs[at * count : at * count + count] for at in range(3))
        sem = refs[3 * count]
        inward = [
            pltpu.make_async_copy(source[at], held[at], sem.at[at]) for at in range(count)
        ]
        outward = [
            pltpu.make_async_copy(held[at], result[at], sem.at[count + at]) for at in range(count)
        ]
        for copy in inward:
            copy.start()
        for before, after in zip(inward, outward):
            before.wait()
            after.start()
        for copy in outward:
            copy.wait()

    anywhere = pl.BlockSpec(memory_space=pl.ANY)
    return pl.pallas_call(
        kernel,
        out_shape=[jax.ShapeDtypeStruct(a.shape, a.dtype) for a in arrays],
        in_specs=[anywhere] * count,
        out_specs=[anywhere] * count,
        scratch_shapes=[pltpu.VMEM(a.shape, a.dtype) for a in arrays]
        + [pltpu.SemaphoreType.DMA((2 * count,))],
    )(*arrays)


def finish_plain(n_dp, layer, tokens_grad, grads, small):
    share = 768 // n_dp
    grads = lax.psum_scatter(grads, "dp", scatter_dimension=0, tiled=True)
    small = lax.psum(small, "dp")
    dp = lax.axis_index("dp")
    wide = HEAD // n_dp
    turned = lax.dynamic_slice_in_dim(small, dp * share, share, 1)
    up_bias = lax.dynamic_slice_in_dim(small[6].reshape(12, HEAD), dp * wide, wide, 1)
    row = small[7]
    sums = jnp.stack(
        [row[0:64], row[256:320], row[64:128], row[320:384], row[384:448], row[512:576]]
    )
    sums = lax.dynamic_slice_in_dim(sums, dp * wide, wide, 1)
    down, up = grads[:, 0:768], grads[:, 768:1536]
    out_a, main, tail = grads[:, 1536:1664], grads[:, 1664:2048], grads[:, 2048:2304]
    qkv = jnp.concatenate(
        [
            main[:, 0:128],
            tail[:, 0:64],
            main[:, 128:256],
            tail[:, 64:128],
            main[:, 256:384],
            tail[:, 128:192],
        ],
        axis=1,
    )
    out = jnp.concatenate([out_a, tail[:, 192:256]], axis=1)
    return [
        layer,
        tokens_grad,
        qkv.T,
        sums.reshape(3, 2, wide),
        out.T,
        turned[5],
        turned[3],
        turned[4],
        up,
        up_bias.T,
        down,
        turned[2],
        turned[0],
        turned[1],
    ]


def solution(mesh):
    placed = (
        P("dp", None),
        P("dp", None),
        P(None, None, "tensor", None),
        P(None, "tensor", None),
        P("tensor", None, None),
        P(),
        P(),
        P(),
        P(None, "tensor"),
        P("tensor", None),
        P("tensor", None),
        P(),
        P(),
        P(),
        P("dp", None),
    )
    return jax.shard_map(
        body,
        mesh=mesh,
        in_specs=placed,
        out_specs=(
            P(("dp", "tensor"), None),
            P(("dp", "tensor"), None),
            P("dp", None, "tensor", None),
            P(None, "tensor", "dp"),
            P("tensor", None, "dp"),
            P("dp"),
            P("dp"),
            P("dp"),
            P("dp", "tensor"),
            P("tensor", "dp"),
            P("tensor", "dp"),
            P("dp"),
            P("dp"),
            P("dp"),
        ),
        check_vma=False,
    )
```

```python
from types import SimpleNamespace

import jax
import jax.numpy as jnp
from jax import lax
from jax.experimental import pallas as pl
from jax.experimental.pallas import tpu as pltpu
from jax.sharding import PartitionSpec as P

HEAD = 64
SEQ = 512
EPS = 1e-12
SCALE = HEAD ** (-0.5)
BF = jnp.bfloat16
F32 = jnp.float32
MESH_ID = pl.DeviceIdType.MESH
NAMES = ("dp", "tensor")
D0, D1, D2, U0, U1, U2, OUT, QK, V, QK2, V2 = range(11)
WIDTHS = (256, 256, 256, 256, 256, 256, 128, 256, 128, 128, 128)
DEPTH_FIRST = (D0, U2)
DIRECT = ()


def dot(left, right, left_dim, right_dim):
    return lax.dot_general(
        left, right, (((left_dim,), (right_dim,)), ((), ())), preferred_element_type=F32
    )


def mean_of(values):
    return jnp.mean(values, axis=-1, keepdims=True)


def row_sum(values):
    return jnp.sum(values, axis=0, keepdims=True)


def scratch_plan(rows, share, fused, results):
    plan = dict(
        seg=((rows, SEQ), jnp.int32),
        bqv=((3, 2, HEAD), BF),
        bup=((12, HEAD), BF),
        vec=((8, 768), F32),
        tok=((rows, 2, 2, 128, 768), BF),
        cot=((rows, 2, 128, 768), BF),
        wq=((5, 128, 768), BF),
        wo=((4, 256, 768), BF),
        wu=((768, 768), BF),
        wd=((768, 768), BF),
        mix=((rows, 512, 640), BF),
        bias=((rows, 512, 512), F32),
        mixr=((rows, 512, 128), BF),
        prob=((rows, 3, 512, 512), F32),
        ctx=((rows, 512, 256), BF),
        cs=((rows, 2, 2, 192, 128), BF),
        cr=((rows, 2, 4, 192, 128), BF),
        n1=((rows, 256, 768), F32),
        r1=((rows, 256, 1), F32),
        fo=((rows, 256, 768), F32),
        flow=((rows, 2, 2, 128, 768), BF),
        act=((rows, 2, 256, 768), BF),
        gp=((rows, 2, 256, 768), F32),
        ds=((rows, 256, 768), F32),
        dsl=((rows, 2, 2, 128, 768), BF),
        dhl=((rows, 2, 256, 768), BF),
        dfi=((rows, 256, 768), F32),
        dal=((rows, 2, 2, 128, 768), BF),
        dkv=((4, 512, 128), F32),
        dq2=((512, 128), F32),
        dmx=((rows, 512, 640), BF),
        x4=((2, 128, 768), BF),
        x4r=((2, 128, 768), BF),
        vs=((8, 768), F32),
        vm=((8, 768), F32),
    )
    plan.update(
        pair=[((rows, 2, 2, 128, 768), BF)] * 3,
        paired=[((rows, 2, 128, 768), BF)] * 3,
        cross=[((rows, 2, 128, 768), BF)] * 2,
        crossed=[((rows, 2, 128, 768), BF)] * 2,
        given=[((6, 128), BF)] * 6,
        outs=[(result.shape, result.dtype) for result in results],
    )
    if fused:
        plan.update(
            small=[((8, 768), F32)] * 6,
            pieces=[
                [
                    ((2, 2, 2, share, width), BF),
                    ((2, 2, share, width), BF),
                    ((3 if name in DIRECT else 2, share, width), BF),
                    ((3 if name in DIRECT else 2, share, width), BF),
                    ((share, width), BF),
                    ((share, width), BF),
                ]
                for name, width in enumerate(WIDTHS)
            ],
        )
    return plan


def is_buffer(node):
    return isinstance(node, tuple)


INPUTS = 15
OVER, CORNER, PAIR, ROWS, CROSS = range(5)
FIRST_ROW = 0
LOCAL_COPIES = 21
REMOTE_COPIES = 60 + len(DIRECT)


def layer_kernel(rows, n_dp, fused, tree, *refs):
    tok_h, cot_h, wq_h, wo_h, wu_h, wd_h, seg_h = refs[:7]
    small_h = refs[7:INPUTS]
    n_out = 14 if fused else 4
    results = refs[INPUTS : INPUTS + n_out]
    held = tree.num_leaves
    buf = SimpleNamespace(
        **jax.tree.unflatten(tree, refs[INPUTS + n_out : INPUTS + n_out + held])
    )
    outs, seg, vec = buf.outs, buf.seg, buf.vec
    local_sem, send_sem, recv_sem = refs[INPUTS + n_out + held :]

    dp = lax.axis_index("dp")
    me = lax.axis_index("tensor")
    chip = me // 2
    core = lax.rem(me, 2)
    mate = (dp, chip * 2 + (1 - core))
    over = (dp, (1 - chip) * 2 + core)
    over_mate = (dp, (1 - chip) * 2 + (1 - core))
    why = lax.rem(dp, 2)
    near = lax.rem(dp // 2, 2)
    far = dp // 4
    side = (dp + 1 - 2 * why, me)
    next_near = (dp + 2 - 4 * near, me)
    next_far = (dp + 4 - 8 * far, me)
    next_both = (dp + 6 - 4 * near - 8 * far, me)

    fetched = []
    stored, token_rows, layer_rows = [], [], []

    def fetch(src, dst, at=None):
        if at is None:
            at = len(fetched)
            fetched.append(at)
        copy = pltpu.make_async_copy(src, dst, local_sem.at[at])
        copy.start()
        return copy

    keys = {}
    latest = {}

    def remote(src, dst, device, key):
        at = keys.setdefault(key, len(keys))
        copy = pltpu.make_async_remote_copy(
            src_ref=src,
            dst_ref=dst,
            send_sem=send_sem.at[at],
            recv_sem=recv_sem.at[at],
            device_id=device,
            device_id_type=MESH_ID,
        )
        if key in latest:
            latest[key].wait_send()
        latest[key] = copy
        return copy

    arrived = []

    def once(copy):
        new = not any(copy is other for other in arrived)
        if new:
            arrived.append(copy)
        return new

    def arrive(copy):
        if once(copy):
            copy.wait_recv()

    def loaded(copy):
        if once(copy):
            copy.wait()

    def send(src, dst, device, key):
        copy = remote(src, dst, device, key)
        copy.start()
        return copy

    partners = [mate, over, over_mate]
    if fused:
        partners += [side, next_near, next_far] + [next_both] * bool(DIRECT)
    barrier = pltpu.get_barrier_semaphore()
    for device in partners:
        pl.semaphore_signal(barrier, inc=1, device_id=device, device_id_type=MESH_ID)
    got_tok = [None] * rows

    def fetch_row(r):
        got_tok[r] = [fetch(tok_h.at[r, :, h], buf.tok.at[r, h]) for h in range(2)]

    lane = lax.broadcasted_iota(jnp.int32, (256, 128), 1)
    low_half = lane < 64
    lane_row = lax.broadcasted_iota(jnp.int32, (512, 128), 1) < 64
    later = SimpleNamespace()

    def fetch_all():
        fetch_row(FIRST_ROW)
        later.wq = [
            fetch(wq_h.at[:, 0:128], buf.wq.at[0:3]),
            fetch(wq_h.at[0, 128:192], buf.wq.at[3, 0:64]),
            fetch(wq_h.at[1, 128:192], buf.wq.at[3, 64:128]),
            fetch(wq_h.at[2, 128:192], buf.wq.at[4, 0:64]),
        ]
        later.small = [fetch(seg_h, buf.seg), fetch(small_h[0], buf.bqv)]
        later.small.append(fetch(small_h[1], buf.bup))
        later.small += [fetch(small_h[2 + at], buf.given[at]) for at in range(6)]
        for r in range(rows):
            if r != FIRST_ROW:
                fetch_row(r)
        later.wo = fetch(wo_h, buf.wo.at[me, 0:192])
        later.wu = fetch(wu_h, buf.wu)
        later.wd = fetch(wd_h, buf.wd)
        later.cot = fetch(cot_h.at[:, core], buf.cot)

    def prepare():
        fetch_all()
        buf.wq[4, 64:128] = jnp.zeros((64, 768), BF)
        buf.vs[...] = jnp.zeros((8, 768), F32)
        for copy in later.small:
            copy.wait()
        bias = [[buf.bqv[head, kind : kind + 1, :].astype(F32) for kind in range(2)] for head in range(3)]
        none = jnp.zeros((1, HEAD), F32)
        none2 = jnp.zeros((1, 128), F32)
        for at, pair in enumerate(
            (
                (bias[0][0], bias[1][0]),
                (none, none),
                (bias[0][1], bias[1][1]),
                (bias[2][0], none),
                (bias[2][1], none),
            )
        ):
            vec[0:1, at * 128 : at * 128 + 128] = jnp.concatenate(pair, axis=1)
        vec[0:1, 640:768] = none2
        for at in range(6):
            pair = buf.bup[2 * at : 2 * at + 2, :].astype(F32)
            vec[4:5, at * 128 : at * 128 + 128] = jnp.concatenate([pair[0:1], pair[1:2]], axis=1)
        for at, row in enumerate((1, 2, 3, 5, 6, 7)):
            short = buf.given[at][...].astype(F32)
            for part in range(6):
                vec[row : row + 1, part * 128 : part * 128 + 128] = short[part : part + 1]

    ctx_copies = {}

    def project(r):
        for copy in got_tok[r]:
            copy.wait()
        for copy in later.wq:
            loaded(copy)
        mixed = dot(
            buf.tok[r].reshape(512, 768), buf.wq[...].reshape(640, 768), 1, 1
        ) + vec[0:1, 0:640]
        q_low = mixed[:, 0:128].astype(BF).astype(F32) * SCALE
        buf.mix[r, :, 0:128] = q_low.astype(BF)
        buf.mix[r, :, 128:384] = mixed[:, 128:384].astype(BF)
        tail = mixed[:, 384:512].astype(BF).astype(F32)
        tail = jnp.where(lane_row, tail * SCALE, tail)
        buf.mix[r, :, 384:512] = tail.astype(BF)
        buf.mixr[r] = pltpu.roll(tail, 64, 1).astype(BF)
        buf.mix[r, :, 512:640] = mixed[:, 512:640].astype(BF)

        ids = seg[r : r + 1, :].astype(F32)
        ids = jnp.concatenate(
            [ids[:, 0:128], ids[:, 256:384], ids[:, 128:256], ids[:, 384:512]], axis=1
        )
        column = jnp.broadcast_to(ids, (128, 512)).T
        buf.bias[r] = jnp.where(column[:, 0:1] == ids, 0.0, -1e30)

    def attend(r, h):
        at = pl.ds(h * 256, 256)
        q_a = buf.mix[r, at, 0:128]
        q_b = buf.mix[r, at, 384:512]
        zero = jnp.zeros_like(q_a)
        parts = []
        for head in range(3):
            if head == 1:
                query = jnp.where(low_half, zero, q_a)
            else:
                query = jnp.where(low_half, q_b if head == 2 else q_a, zero)
            key = buf.mixr[r] if head == 2 else buf.mix[r, :, 128:256]
            value = buf.mix[r, :, 512:640] if head == 2 else buf.mix[r, :, 256:384]
            scores = dot(query, key, 1, 1) + buf.bias[r, at, :]
            top = jnp.max(scores, axis=-1, keepdims=True)
            expo = jnp.exp(scores - top)
            probs = expo * (1.0 / jnp.sum(expo, axis=-1, keepdims=True))
            buf.prob[r, head, at, :] = probs
            parts.append(dot(probs.astype(BF), value, 1, 0))
        both = jnp.where(low_half, parts[0], parts[1]).astype(BF)
        buf.ctx[r, at, 0:128] = both
        buf.ctx[r, at, 128:256] = parts[2].astype(BF)
        for part in range(2):
            first = part * 128
            buf.cs[r, h, part, 0:128] = both[first : first + 128]
            buf.cs[r, h, part, 128:192] = jnp.where(
                lane[0:64] < 64,
                parts[2][first : first + 64],
                pltpu.roll(parts[2][first + 64 : first + 128], 64, 1),
            ).astype(BF)

    def send_context(r, h):
        there = buf.cr.at[r, h, me]
        ctx_copies[r, h] = [
            send(buf.cs.at[r, h, core], there, over, (OVER, r, h)),
            send(buf.cs.at[r, h, 1 - core], there, over_mate, (CORNER, r, h)),
            send(buf.cs.at[r, h, 1 - core], there, mate, (PAIR, r, h)),
        ]
        buf.cr[r, h, me] = buf.cs[r, h, core]

    weight_copies = SimpleNamespace()

    def send_weight():
        weight_copies.over = send(wo_h, buf.wo.at[me, 0:192], over, 0)
        weight_copies.mate = send(wo_h, buf.wo.at[me, 0:192], mate, 1)

    def forward_weight():
        weight_copies.over.wait_recv()
        theirs = buf.wo.at[(1 - chip) * 2 + core, 0:192]
        weight_copies.far = send(theirs, theirs, mate, 2)

    def complete_weight():
        later.wo.wait()
        weight_copies.mate.wait_recv()
        weight_copies.far.wait_recv()
        for group in range(4):
            buf.wo[group, 192:256] = buf.wo[group, 128:192]

    flow_copies = {}

    def first_norm(r, h):
        for copy in ctx_copies[r, h]:
            copy.wait_recv()
        total = None
        for group in range(4):
            packed = buf.cr[r, h, group, 128:192]
            zero = jnp.zeros_like(packed)
            keep = lane[0:64] < 64
            left = jnp.concatenate(
                [
                    buf.cr[r, h, group, 0:128],
                    jnp.concatenate(
                        [jnp.where(keep, packed, zero), jnp.where(keep, zero, packed)], axis=0
                    ),
                ],
                axis=1,
            )
            term = dot(left, buf.wo[group], 1, 0).astype(BF).astype(F32)
            total = term if total is None else total + term
        at = pl.ds(h * 128, 128)
        first_in = buf.tok[r, h, core].astype(F32) + total + vec[1:2, :]
        center = first_in - mean_of(first_in)
        scale = lax.rsqrt(mean_of(center * center) + EPS)
        unit = center * scale
        buf.n1[r, at, :] = unit
        buf.r1[r, at, :] = scale
        first_out = unit * vec[2:3, :] + vec[3:4, :]
        buf.fo[r, at, :] = first_out
        buf.flow[r, h, core] = first_out.astype(BF)
        own = buf.flow.at[r, h, core]
        flow_copies[r, h] = send(own, own, mate, (ROWS, r, h))

    pair_copies = {}
    cross_copies = {}

    def ffn_forward(r, h):
        flow_copies[r, h].wait_recv()
        loaded(later.wu)
        loaded(later.wd)
        rows_in = buf.flow[r, h].reshape(256, 768)
        for part in range(3):
            at = pl.ds(part * 256, 256)
            hidden = dot(rows_in, buf.wu[:, at], 1, 0) + vec[4:5, at]
            phi = 0.5 * (1.0 + lax.erf(hidden * 0.7071067811865476))
            buf.act[r, h, :, at] = (hidden * phi).astype(BF)
            buf.gp[r, h, :, at] = (
                phi + hidden * jnp.exp(-0.5 * hidden * hidden) * 0.3989422804014327
            )
        terms = dot(buf.act[r, h], buf.wd[...], 1, 0).astype(BF)
        buf.pair[0][r, h] = terms.reshape(2, 128, 768)
        pair_copies[2, r, h] = send(
            buf.pair[0].at[r, h, 1 - core], buf.paired[0].at[r, h], mate, (PAIR, r, h)
        )

    def exchange(stage, r, h):
        pair_copies[stage, r, h].wait_recv()
        own = buf.pair[stage - 2][r, h, core].astype(F32)
        other = buf.paired[stage - 2][r, h].astype(F32)
        buf.cross[stage - 2][r, h] = (own + other).astype(BF)
        cross_copies[stage, r, h] = send(
            buf.cross[stage - 2].at[r, h],
            buf.crossed[stage - 2].at[r, h],
            over,
            (CROSS if stage == 2 else OVER, r, h),
        )

    def crossed(stage, r, h):
        cross_copies[stage, r, h].wait_recv()
        return buf.cross[stage - 2][r, h].astype(F32) + buf.crossed[stage - 2][r, h].astype(F32)

    dsl_copies = {}

    def second_norm(r, h):
        loaded(later.cot)
        total = crossed(2, r, h)
        at = pl.ds(h * 128, 128)
        second_in = buf.fo[r, at, :] + total + vec[5:6, :]
        center = second_in - mean_of(second_in)
        scale = lax.rsqrt(mean_of(center * center) + EPS)
        unit = center * scale

        @pl.when(chip == r)
        def _():
            layer = unit * vec[6:7, :] + vec[7:8, :]
            outs[0][at, :] = layer.astype(BF)

        grad = buf.cot[r, h].astype(F32)
        scaled = grad * vec[6:7, :]
        d_second = scale * (scaled - mean_of(scaled) - unit * mean_of(scaled * unit))
        buf.ds[r, at, :] = d_second
        buf.dsl[r, h, core] = d_second.astype(BF)
        own = buf.dsl.at[r, h, core]
        dsl_copies[r, h] = send(own, own, mate, (ROWS, r, h))
        buf.vs[0:1, :] += row_sum(grad * unit)
        buf.vs[1:2, :] += row_sum(grad)
        buf.vs[2:3, :] += row_sum(d_second)
        layer_rows.append((r, h))
        if len(layer_rows) == 2 * rows:
            emit(0)

    def ffn_backward(r, h):
        arrive(dsl_copies[r, h])
        rows_in = buf.dsl[r, h].reshape(256, 768)
        for part in range(3):
            at = pl.ds(part * 256, 256)
            d_hidden = dot(rows_in, buf.wd[at, :], 1, 1) * buf.gp[r, h, :, at]
            buf.vs[6:7, at] += row_sum(d_hidden)
            buf.dhl[r, h, :, at] = d_hidden.astype(BF)
        terms = dot(buf.dhl[r, h], buf.wu[...], 1, 1).astype(BF)
        buf.pair[1][r, h] = terms.reshape(2, 128, 768)
        pair_copies[3, r, h] = send(
            buf.pair[1].at[r, h, 1 - core], buf.paired[1].at[r, h], mate, (PAIR, r, h)
        )

    dal_copies = {}

    def first_norm_back(r, h):
        total = crossed(3, r, h)
        at = pl.ds(h * 128, 128)
        d_first = buf.ds[r, at, :] + total
        unit = buf.n1[r, at, :]
        scaled = d_first * vec[2:3, :]
        d_in = buf.r1[r, at, :] * (scaled - mean_of(scaled) - unit * mean_of(scaled * unit))
        buf.dfi[r, at, :] = d_in
        buf.dal[r, h, core] = d_in.astype(BF)
        own = buf.dal.at[r, h, core]
        dal_copies[r, h] = send(own, own, mate, (ROWS, r, h))
        buf.vs[3:4, :] += row_sum(d_first * unit)
        buf.vs[4:5, :] += row_sum(d_first)
        buf.vs[5:6, :] += row_sum(d_in)

    out_parts = []

    halves = []

    def attend_back(r, h):
        arrive(dal_copies[r, h])
        at = pl.ds(h * 256, 256)
        d_ctx = dot(buf.dal[r, h].reshape(256, 768), buf.wo[me], 1, 1).astype(BF)
        turned = buf.mixr[r]
        d_q, d_k, d_v = [], [], []
        for head in range(3):
            tile = d_ctx[:, 0:128] if head < 2 else d_ctx[:, 128:256]
            zero = jnp.zeros_like(tile)
            rows_in = tile
            if head == 0:
                rows_in = jnp.where(low_half, tile, zero)
            if head == 1:
                rows_in = jnp.where(low_half, zero, tile)
            value = buf.mix[r, :, 256:384] if head < 2 else buf.mix[r, :, 512:640]
            probs = buf.prob[r, head, at, :]
            weighted = probs * dot(rows_in, value, 1, 1)
            inner = jnp.sum(weighted, axis=-1, keepdims=True)
            d_scores = (weighted - probs * inner).astype(BF)
            key = buf.mix[r, :, 128:256] if head < 2 else turned
            query = buf.mix[r, at, 0:128] if head < 2 else buf.mixr[r, at, :]
            d_q.append(dot(d_scores, key, 1, 0))
            d_k.append(dot(d_scores, query, 0, 0))
            d_v.append(dot(probs.astype(BF), tile, 0, 0))
        query_rows = jnp.where(low_half, d_q[0], d_q[1]) * SCALE
        buf.dmx[r, at, 0:128] = query_rows.astype(BF)
        vs = buf.vs
        vs[7:8, 0:128] += row_sum(query_rows)
        buf.dq2[at, :] = d_q[2] * SCALE
        sums = [
            jnp.where(lane_row, d_k[0], d_k[1]),
            jnp.where(lane_row, d_v[0], d_v[1]),
            d_k[2],
            d_v[2],
        ]
        halves.append(r)
        if halves.count(r) < 2:
            for part in range(4):
                buf.dkv[part] = sums[part]
            return
        sums = [buf.dkv[part] + sums[part] for part in range(4)]
        tiles = [
            sums[0],
            sums[1],
            jnp.where(lane_row, buf.dq2[...], sums[2]),
            jnp.where(lane_row, sums[3], 0.0),
        ]
        for part, tile in enumerate(tiles):
            lanes = pl.ds(part * 128 + 128, 128)
            buf.dmx[r, :, lanes] = tile.astype(BF)
            if part > 0:
                vs[7:8, lanes] += row_sum(tile)

    tok_copies = []

    def token_terms(r, h):
        terms = dot(
            buf.dmx[r, h * 256 : h * 256 + 256, :], buf.wq[...].reshape(640, 768), 1, 0
        )
        buf.pair[2][r, h] = terms.astype(BF).reshape(2, 128, 768)
        pair_copies[4, r, h] = send(
            buf.pair[2].at[r, h, 1 - core], buf.paired[2].at[r, h], mate, (PAIR, r, h)
        )

    cross4 = []

    def token_way():
        for h in range(2):
            cross4.append(remote(buf.x4.at[h], buf.x4r.at[h], over, (CROSS, 0, h)))

    def token_cross(r, h):
        if not cross4:
            token_way()
        pair_copies[4, r, h].wait_recv()

        @pl.when(chip != r)
        def _():
            own = buf.pair[2][r, h, core].astype(F32)
            other = buf.paired[2][r, h].astype(F32)
            buf.x4[h] = (own + other).astype(BF)
            cross4[h].start()

    def token_finish(h):
        cross4[h].wait_recv()
        own = buf.pair[2][chip, h, core].astype(F32)
        other = buf.paired[2][chip, h].astype(F32)
        pair = (own + other).astype(BF).astype(F32)
        total = pair + buf.x4r[h].astype(F32)
        result = buf.dfi[chip, pl.ds(h * 128, 128), :] + total
        outs[1][h * 128 : h * 128 + 128, :] = result.astype(BF)
        token_rows.append(h)
        if len(token_rows) == 2:
            emit(1)

    steps = {}
    starts = [sum(WIDTHS[:at]) for at in range(len(WIDTHS))]
    finished = []
    pieces = buf.pieces if fused else None

    def reduce_start(name):
        grad = gradient(name)
        width = WIDTHS[name]
        if not fused:
            outs[2][:, starts[name] : starts[name] + width] = grad
            finished.append(name)
            if len(finished) == len(WIDTHS):
                emit(2)
            return
        stage, came = pieces[name][:2]
        stage[...] = grad.astype(BF).reshape(stage.shape)
        if name in DEPTH_FIRST:
            steps[name] = send(stage.at[:, 1 - near], came, next_near, (-1, name))
        else:
            steps[name] = send(stage.at[:, :, 1 - why], came, side, (-1, name))

    def reduce_first(name):
        if not fused:
            return
        steps[name].wait_recv()
        stage, came, out, into = pieces[name][:4]
        if name in DIRECT:
            ways = (
                (far, 1 - near, next_near),
                (1 - far, near, next_far),
                (1 - far, 1 - near, next_both),
            )
            copies = []
            for at, (high, low, device) in enumerate(ways):
                total = stage[high, low, why].astype(F32) + came[high, low].astype(F32)
                out[at] = total.astype(BF)
                copies.append(send(out.at[at], into.at[at], device, (-2 - at, name)))
            steps[name] = copies
            return
        for at in range(2):
            if name in DEPTH_FIRST:
                total = stage[1 - far, near, at].astype(F32) + came[1 - far, at].astype(F32)
            else:
                total = stage[at, 1 - near, why].astype(F32) + came[at, 1 - near].astype(F32)
            out[at] = total.astype(BF)
        steps[name] = send(
            out, into, next_far if name in DEPTH_FIRST else next_near, (-2, name)
        )

    def reduce_second(name):
        if not fused:
            return
        steps[name].wait_recv()
        stage, came, _, into, out, last = pieces[name]
        if name in DEPTH_FIRST:
            total = stage[far, near, 1 - why].astype(F32) + came[far, 1 - why].astype(F32)
            total = total + into[1 - why].astype(F32)
        else:
            total = stage[1 - far, near, why].astype(F32) + came[1 - far, near].astype(F32)
            total = total + into[1 - far].astype(F32)
        out[...] = total.astype(BF)
        steps[name] = send(out, last, side if name in DEPTH_FIRST else next_far, (-3, name))

    def emit(*which):
        for at in which:
            stored.append(fetch(outs[at], results[at], len(stored)))

    def reduce_finish(name):
        if not fused:
            return
        copies = steps[name] if name in DIRECT else [steps[name]]
        for copy in copies:
            copy.wait_recv()
        stage, came, _, into, _, last = pieces[name]
        total = stage[far, near, why].astype(F32)
        if name in DEPTH_FIRST:
            total = total + came[far, why].astype(F32) + into[why].astype(F32)
        elif name in DIRECT:
            total = total + came[far, near].astype(F32)
            for at in range(3):
                total = total + into[at].astype(F32)
        else:
            total = total + came[far, near].astype(F32) + into[far].astype(F32)
        if name not in DIRECT:
            total = total + last[...].astype(F32)
        flipped = None if name <= U2 else total.T
        if name <= D2:
            outs[10][:, starts[name] : starts[name] + 256] = total
        elif name <= U2:
            at = starts[name] - starts[U0]
            outs[8][:, at : at + 256] = total
        elif name == OUT:
            outs[4][0:128, :] = flipped
        elif name == QK:
            outs[2][0:128, :] = flipped[0:128]
            outs[2][192:320, :] = flipped[128:256]
        elif name == V:
            outs[2][384:512, :] = flipped
        elif name == QK2:
            outs[2][128:192, :] = flipped[0:64]
            outs[2][320:384, :] = flipped[64:128]
        else:
            outs[2][512:576, :] = flipped[0:64]
            outs[4][128:192, :] = flipped[64:128]
        before = set(finished)
        finished.append(name)
        after = set(finished)
        for group, at in (
            ({D0, D1, D2}, 10),
            ({U0, U1, U2}, 8),
            ({QK, V, QK2, V2}, 2),
            ({OUT, V2}, 4),
        ):
            if group <= after and not group <= before:
                emit(at)

    def down_grad(part):
        for r in range(rows):
            for h in range(2):
                arrive(dsl_copies[r, h])
        at = pl.ds(part * 256, 256)
        return dot(
            buf.dsl[...].reshape(rows * 512, 768),
            buf.act[:, :, :, at].reshape(rows * 512, 256),
            0,
            0,
        )

    def up_grad(part):
        at = pl.ds(part * 256, 256)
        return dot(
            buf.flow[...].reshape(rows * 512, 768),
            buf.dhl[:, :, :, at].reshape(rows * 512, 256),
            0,
            0,
        )

    def all_back():
        for r in range(rows):
            for h in range(2):
                arrive(dal_copies[r, h])

    def out_grad_first():
        all_back()
        return dot(
            buf.dal[...].reshape(rows * 512, 768),
            buf.ctx[:, :, 0:128].reshape(rows * 512, 128),
            0,
            0,
        )

    def out_grad_second():
        all_back()
        turned = dot(
            buf.dal[...].reshape(rows * 512, 768),
            buf.ctx[:, :, 128:256].reshape(rows * 512, 128),
            0,
            0,
        )
        return pltpu.roll(turned, 64, 1)

    def qkv_grad(low, high):
        return dot(
            buf.tok[...].reshape(rows * 512, 768),
            buf.dmx[:, :, low:high].reshape(rows * 512, high - low),
            0,
            0,
        )

    def gradient(name):
        if name <= D2:
            return down_grad(name)
        if name <= U2:
            return up_grad(name - U0)
        if name == OUT:
            return out_grad_first()
        if name == QK:
            return qkv_grad(0, 256)
        if name == V:
            return qkv_grad(256, 384)
        if name == QK2:
            return qkv_grad(384, 512)
        first = lax.broadcasted_iota(jnp.int32, (768, 128), 1) < 64
        return jnp.where(first, qkv_grad(512, 640), out_grad_second())

    small_copies = SimpleNamespace()

    def small_mate():
        small_copies.mate = send(buf.vs, buf.vm, mate, 3)

    def small_side():
        small_copies.mate.wait_recv()
        shared = lax.broadcasted_iota(jnp.int32, (8, 768), 0) < 6
        small = buf.vs[...] + jnp.where(shared, buf.vm[...], 0.0)
        if not fused:
            outs[3][...] = small
            emit(3)
            return
        buf.small[0][...] = small
        small_copies.side = send(buf.small[0], buf.small[1], side, 4)

    def small_near():
        if not fused:
            return
        small_copies.side.wait_recv()
        buf.small[2][...] = buf.small[0][...] + buf.small[1][...]
        small_copies.near = send(buf.small[2], buf.small[3], next_near, 5)

    def small_far():
        if not fused:
            return
        small_copies.near.wait_recv()
        buf.small[4][...] = buf.small[2][...] + buf.small[3][...]
        small_copies.far = send(buf.small[4], buf.small[5], next_far, 6)

    def small_finish():
        if not fused:
            return
        small_copies.far.wait_recv()
        small = buf.small[4][...] + buf.small[5][...]
        share = 768 // n_dp
        turned = pltpu.roll(small, 768 - dp * share, 1)
        for row, at in ((5, 5), (3, 6), (4, 7), (2, 11), (0, 12), (1, 13)):
            outs[at][...] = turned[row : row + 1, 0:share]
        wide = HEAD // n_dp
        lanes = lax.broadcasted_iota(jnp.int32, (8, 768), 1)
        depth = lax.broadcasted_iota(jnp.int32, (8, 768), 0)
        spread = jnp.where(lax.rem(lanes, HEAD) == depth + dp * wide, small[6:7, :], 0.0)
        group = lax.broadcasted_iota(jnp.int32, (768, 128), 0) // HEAD
        pick = (group == lax.broadcasted_iota(jnp.int32, (768, 128), 1)).astype(F32)
        outs[9][...] = jnp.dot(spread, pick, precision=lax.Precision.HIGHEST)[0:wide, 0:12]
        group = lanes // HEAD
        where = jnp.where(
            depth < 4,
            lax.rem(depth, 2) * 4 + depth // 2,
            jnp.where(depth == 4, 6, 8),
        )
        spread = jnp.where((group == where) & (depth < 6), small[7:8, :], 0.0)
        inside = lax.rem(lax.broadcasted_iota(jnp.int32, (768, 128), 0), HEAD)
        pick = (inside == lax.broadcasted_iota(jnp.int32, (768, 128), 1) + dp * wide).astype(F32)
        heads = jnp.dot(spread, pick, precision=lax.Precision.HIGHEST)
        for head in range(3):
            outs[3][head] = heads[head * 2 : head * 2 + 2, 0:wide]
        emit(3, 5, 6, 7, 9, 11, 12, 13)

    pl.semaphore_wait(barrier, len(partners))
    send_weight()
    prepare()
    project(0)
    attend(0, 1)
    send_context(0, 1)
    project(1)
    attend(1, 0)
    attend(1, 1)
    send_context(1, 1)
    forward_weight()
    attend(0, 0)
    send_context(0, 0)
    send_context(1, 0)
    complete_weight()
    first_norm(0, 1)
    ffn_forward(0, 1)
    first_norm(1, 1)
    exchange(2, 0, 1)
    first_norm(0, 0)
    ffn_forward(1, 1)
    ffn_forward(0, 0)
    first_norm(1, 0)
    exchange(2, 1, 1)
    exchange(2, 0, 0)
    ffn_forward(1, 0)
    second_norm(0, 1)
    exchange(2, 1, 0)
    ffn_backward(0, 1)
    exchange(3, 0, 1)
    second_norm(1, 1)
    ffn_backward(1, 1)
    second_norm(0, 0)
    exchange(3, 1, 1)
    ffn_backward(0, 0)
    exchange(3, 0, 0)
    second_norm(1, 0)
    reduce_start(D0)
    reduce_start(D1)
    reduce_start(D2)
    ffn_backward(1, 0)
    reduce_start(U2)
    first_norm_back(0, 1)
    reduce_start(U0)
    reduce_start(U1)
    exchange(3, 1, 0)
    first_norm_back(1, 1)
    reduce_first(D0)
    reduce_first(D1)
    attend_back(0, 1)
    first_norm_back(0, 0)
    reduce_first(U2)
    reduce_first(D2)
    attend_back(0, 0)
    attend_back(1, 1)
    first_norm_back(1, 0)
    reduce_second(D1)
    token_terms(0, 1)
    reduce_second(D0)
    token_terms(0, 0)
    reduce_first(U0)
    reduce_start(OUT)
    attend_back(1, 0)
    reduce_second(D2)
    reduce_start(V2)
    small_mate()
    token_cross(0, 1)
    token_cross(0, 0)
    reduce_start(QK)
    reduce_first(U1)
    reduce_finish(D0)
    reduce_start(V)
    reduce_finish(D1)
    reduce_second(U2)
    small_side()
    reduce_first(OUT)
    reduce_start(QK2)
    token_terms(1, 1)
    reduce_second(U0)
    token_terms(1, 0)
    reduce_first(V2)
    token_cross(1, 1)
    reduce_finish(D2)
    token_cross(1, 0)
    reduce_second(U1)
    reduce_second(OUT)
    reduce_first(QK)
    reduce_second(V2)
    reduce_finish(U0)
    reduce_first(V)
    token_finish(1)
    reduce_finish(U1)
    reduce_finish(U2)
    small_near()
    reduce_finish(OUT)
    reduce_second(QK)
    reduce_first(QK2)
    reduce_second(V)
    token_finish(0)
    small_far()
    reduce_finish(V2)
    reduce_second(QK2)
    reduce_finish(QK)
    reduce_finish(V)
    small_finish()
    reduce_finish(QK2)
    for copy in latest.values():
        copy.wait_send()
    for copy in stored:
        copy.wait()


def body(
    tokens,
    segment_ids,
    qkv_weight,
    qkv_bias,
    output_weight,
    output_bias,
    first_gain,
    first_shift,
    up_weight,
    up_bias,
    down_weight,
    down_bias,
    second_gain,
    second_shift,
    cotangent,
):
    rows = tokens.shape[0] // SEQ
    n_dp = lax.axis_size("dp")
    share = 768 // n_dp
    fused = n_dp == 8
    split = (rows, 2, 2, 128, 768)
    shape = jax.ShapeDtypeStruct
    outs = [shape((256, 768), BF), shape((256, 768), BF)]
    if fused:
        wide = HEAD // n_dp
        vector = shape((1, share), F32)
        outs += [
            shape((576, share), F32),
            shape((3, 2, wide), F32),
            shape((192, share), F32),
            vector,
            vector,
            vector,
            shape((share, 768), F32),
            shape((wide, 12), F32),
            shape((share, 768), F32),
            vector,
            vector,
            vector,
        ]
    else:
        outs += [shape((768, 2304), F32), shape((8, 768), F32)]
    plan = scratch_plan(rows, share, fused, outs)
    leaves, tree = jax.tree.flatten(plan, is_leaf=is_buffer)
    anywhere = pl.BlockSpec(memory_space=pl.ANY)

    def kernel(*refs):
        layer_kernel(rows, n_dp, fused, tree, *refs)

    got = pl.pallas_call(
        kernel,
        out_shape=outs,
        in_specs=[anywhere] * INPUTS,
        out_specs=[anywhere] * len(outs),
        scratch_shapes=[pltpu.VMEM(dims, kind) for dims, kind in leaves]
        + [
            pltpu.SemaphoreType.DMA((LOCAL_COPIES,)),
            pltpu.SemaphoreType.DMA((REMOTE_COPIES,)),
            pltpu.SemaphoreType.DMA((REMOTE_COPIES,)),
        ],
        compiler_params=pltpu.CompilerParams(
            collective_id=0, has_side_effects=True, vmem_limit_bytes=62 * 1024 * 1024
        ),
    )(
        tokens.reshape(split),
        cotangent.reshape(split),
        qkv_weight.transpose(1, 2, 3, 0).reshape(3, 192, 768),
        output_weight.reshape(192, 768),
        up_weight,
        down_weight,
        segment_ids,
        qkv_bias.transpose(1, 0, 2),
        up_bias,
        *(
            vector.reshape(6, 128)
            for vector in (
                output_bias,
                first_gain,
                first_shift,
                down_bias,
                second_gain,
                second_shift,
            )
        ),
    )
    if fused:
        got = hand_over(got)
    else:
        got = finish_plain(n_dp, *got)
    return (
        got[0],
        got[1],
        got[2].reshape(3, 3, HEAD, share).transpose(3, 0, 1, 2),
        got[3].transpose(1, 0, 2),
        got[4].reshape(3, HEAD, share),
        got[5].reshape(share),
        got[6].reshape(share),
        got[7].reshape(share),
        got[8],
        got[9].T,
        got[10].T,
        got[11].reshape(share),
        got[12].reshape(share),
        got[13].reshape(share),
    )


def hand_over(arrays):
    count = len(arrays)

    def kernel(*refs):
        source, result, held = (refs[at * count : at * count + count] for at in range(3))
        sem = refs[3 * count]
        inward = [
            pltpu.make_async_copy(source[at], held[at], sem.at[at]) for at in range(count)
        ]
        outward = [
            pltpu.make_async_copy(held[at], result[at], sem.at[count + at]) for at in range(count)
        ]
        for copy in inward:
            copy.start()
        for before, after in zip(inward, outward):
            before.wait()
            after.start()
        for copy in outward:
            copy.wait()

    anywhere = pl.BlockSpec(memory_space=pl.ANY)
    return pl.pallas_call(
        kernel,
        out_shape=[jax.ShapeDtypeStruct(a.shape, a.dtype) for a in arrays],
        in_specs=[anywhere] * count,
        out_specs=[anywhere] * count,
        scratch_shapes=[pltpu.VMEM(a.shape, a.dtype) for a in arrays]
        + [pltpu.SemaphoreType.DMA((2 * count,))],
    )(*arrays)


def finish_plain(n_dp, layer, tokens_grad, grads, small):
    share = 768 // n_dp
    grads = lax.psum_scatter(grads, "dp", scatter_dimension=0, tiled=True)
    small = lax.psum(small, "dp")
    dp = lax.axis_index("dp")
    wide = HEAD // n_dp
    turned = lax.dynamic_slice_in_dim(small, dp * share, share, 1)
    up_bias = lax.dynamic_slice_in_dim(small[6].reshape(12, HEAD), dp * wide, wide, 1)
    row = small[7]
    sums = jnp.stack(
        [row[0:64], row[256:320], row[64:128], row[320:384], row[384:448], row[512:576]]
    )
    sums = lax.dynamic_slice_in_dim(sums, dp * wide, wide, 1)
    down, up = grads[:, 0:768], grads[:, 768:1536]
    out_a, main, tail = grads[:, 1536:1664], grads[:, 1664:2048], grads[:, 2048:2304]
    qkv = jnp.concatenate(
        [
            main[:, 0:128],
            tail[:, 0:64],
            main[:, 128:256],
            tail[:, 64:128],
            main[:, 256:384],
            tail[:, 128:192],
        ],
        axis=1,
    )
    out = jnp.concatenate([out_a, tail[:, 192:256]], axis=1)
    return [
        layer,
        tokens_grad,
        qkv.T,
        sums.reshape(3, 2, wide),
        out.T,
        turned[5],
        turned[3],
        turned[4],
        up,
        up_bias.T,
        down,
        turned[2],
        turned[0],
        turned[1],
    ]


def solution(mesh):
    placed = (
        P("dp", None),
        P("dp", None),
        P(None, None, "tensor", None),
        P(None, "tensor", None),
        P("tensor", None, None),
        P(),
        P(),
        P(),
        P(None, "tensor"),
        P("tensor", None),
        P("tensor", None),
        P(),
        P(),
        P(),
        P("dp", None),
    )
    return jax.shard_map(
        body,
        mesh=mesh,
        in_specs=placed,
        out_specs=(
            P(("dp", "tensor"), None),
            P(("dp", "tensor"), None),
            P("dp", None, "tensor", None),
            P(None, "tensor", "dp"),
            P("tensor", None, "dp"),
            P("dp"),
            P("dp"),
            P("dp"),
            P("dp", "tensor"),
            P("tensor", "dp"),
            P("tensor", "dp"),
            P("dp"),
            P("dp"),
            P("dp"),
        ),
        check_vma=False,
    )
```

```python
from types import SimpleNamespace

import jax
import jax.numpy as jnp
from jax import lax
from jax.experimental import pallas as pl
from jax.experimental.pallas import tpu as pltpu
from jax.sharding import PartitionSpec as P

HEAD = 64
SEQ = 512
EPS = 1e-12
SCALE = HEAD ** (-0.5)
BF = jnp.bfloat16
F32 = jnp.float32
MESH_ID = pl.DeviceIdType.MESH
NAMES = ("dp", "tensor")
D0, D1, D2, U0, U1, U2, OUT, QK, V, QK2, V2 = range(11)
WIDTHS = (256, 256, 256, 256, 256, 256, 128, 256, 128, 128, 128)
DEPTH_FIRST = (D0, U2)
DIRECT = ()


def dot(left, right, left_dim, right_dim):
    return lax.dot_general(
        left, right, (((left_dim,), (right_dim,)), ((), ())), preferred_element_type=F32
    )


def mean_of(values):
    return jnp.mean(values, axis=-1, keepdims=True)


def row_sum(values):
    return jnp.sum(values, axis=0, keepdims=True)


def scratch_plan(rows, share, fused, results):
    plan = dict(
        seg=((rows, SEQ), jnp.int32),
        bqv=((3, 2, HEAD), BF),
        bup=((12, HEAD), BF),
        vec=((8, 768), F32),
        tok=((rows, 2, 2, 128, 768), BF),
        cot=((rows, 2, 128, 768), BF),
        wq=((5, 128, 768), BF),
        wo=((4, 256, 768), BF),
        wu=((768, 768), BF),
        wd=((768, 768), BF),
        mix=((rows, 512, 640), BF),
        bias=((rows, 512, 512), F32),
        mixr=((rows, 512, 128), BF),
        prob=((rows, 3, 512, 512), F32),
        ctx=((rows, 512, 256), BF),
        cs=((rows, 2, 2, 192, 128), BF),
        cr=((rows, 2, 4, 192, 128), BF),
        n1=((rows, 256, 768), F32),
        r1=((rows, 256, 1), F32),
        fo=((rows, 256, 768), F32),
        flow=((rows, 2, 2, 128, 768), BF),
        act=((rows, 2, 256, 768), BF),
        gp=((rows, 2, 256, 768), F32),
        ds=((rows, 256, 768), F32),
        dsl=((rows, 2, 2, 128, 768), BF),
        dhl=((rows, 2, 256, 768), BF),
        dfi=((rows, 256, 768), F32),
        dal=((rows, 2, 2, 128, 768), BF),
        dkv=((4, 512, 128), F32),
        dq2=((512, 128), F32),
        dmx=((rows, 512, 640), BF),
        x4=((2, 128, 768), BF),
        x4r=((2, 128, 768), BF),
        vs=((8, 768), F32),
        vm=((8, 768), F32),
    )
    plan.update(
        pair=[((rows, 2, 2, 128, 768), BF)] * 3,
        paired=[((rows, 2, 128, 768), BF)] * 3,
        cross=[((rows, 2, 128, 768), BF)] * 2,
        crossed=[((rows, 2, 128, 768), BF)] * 2,
        given=[((6, 128), BF)] * 6,
        outs=[(result.shape, result.dtype) for result in results],
    )
    if fused:
        plan.update(
            small=[((8, 768), F32)] * 6,
            pieces=[
                [
                    ((2, 2, 2, share, width), BF),
                    ((2, 2, share, width), BF),
                    ((3 if name in DIRECT else 2, share, width), BF),
                    ((3 if name in DIRECT else 2, share, width), BF),
                    ((share, width), BF),
                    ((share, width), BF),
                ]
                for name, width in enumerate(WIDTHS)
            ],
        )
    return plan


def is_buffer(node):
    return isinstance(node, tuple)


INPUTS = 15
OVER, CORNER, PAIR, ROWS, CROSS = range(5)
FIRST_ROW = 0
LOCAL_COPIES = 21
REMOTE_COPIES = 60 + len(DIRECT)


def layer_kernel(rows, n_dp, fused, tree, *refs):
    tok_h, cot_h, wq_h, wo_h, wu_h, wd_h, seg_h = refs[:7]
    small_h = refs[7:INPUTS]
    n_out = 14 if fused else 4
    results = refs[INPUTS : INPUTS + n_out]
    held = tree.num_leaves
    buf = SimpleNamespace(
        **jax.tree.unflatten(tree, refs[INPUTS + n_out : INPUTS + n_out + held])
    )
    outs, seg, vec = buf.outs, buf.seg, buf.vec
    local_sem, send_sem, recv_sem = refs[INPUTS + n_out + held :]

    dp = lax.axis_index("dp")
    me = lax.axis_index("tensor")
    chip = me // 2
    core = lax.rem(me, 2)
    mate = (dp, chip * 2 + (1 - core))
    over = (dp, (1 - chip) * 2 + core)
    over_mate = (dp, (1 - chip) * 2 + (1 - core))
    why = lax.rem(dp, 2)
    near = lax.rem(dp // 2, 2)
    far = dp // 4
    side = (dp + 1 - 2 * why, me)
    next_near = (dp + 2 - 4 * near, me)
    next_far = (dp + 4 - 8 * far, me)
    next_both = (dp + 6 - 4 * near - 8 * far, me)

    fetched = []
    stored, token_rows, layer_rows = [], [], []

    def fetch(src, dst, at=None):
        if at is None:
            at = len(fetched)
            fetched.append(at)
        copy = pltpu.make_async_copy(src, dst, local_sem.at[at])
        copy.start()
        return copy

    keys = {}
    latest = {}

    def remote(src, dst, device, key):
        at = keys.setdefault(key, len(keys))
        copy = pltpu.make_async_remote_copy(
            src_ref=src,
            dst_ref=dst,
            send_sem=send_sem.at[at],
            recv_sem=recv_sem.at[at],
            device_id=device,
            device_id_type=MESH_ID,
        )
        if key in latest:
            latest[key].wait_send()
        latest[key] = copy
        return copy

    arrived = []

    def once(copy):
        new = not any(copy is other for other in arrived)
        if new:
            arrived.append(copy)
        return new

    def arrive(copy):
        if once(copy):
            copy.wait_recv()

    def loaded(copy):
        if once(copy):
            copy.wait()

    def send(src, dst, device, key):
        copy = remote(src, dst, device, key)
        copy.start()
        return copy

    partners = [mate, over, over_mate]
    if fused:
        partners += [side, next_near, next_far] + [next_both] * bool(DIRECT)
    barrier = pltpu.get_barrier_semaphore()
    for device in partners:
        pl.semaphore_signal(barrier, inc=1, device_id=device, device_id_type=MESH_ID)
    got_tok = [None] * rows

    def fetch_row(r):
        got_tok[r] = [fetch(tok_h.at[r, :, h], buf.tok.at[r, h]) for h in range(2)]

    lane = lax.broadcasted_iota(jnp.int32, (256, 128), 1)
    low_half = lane < 64
    lane_row = lax.broadcasted_iota(jnp.int32, (512, 128), 1) < 64
    later = SimpleNamespace()

    def fetch_all():
        fetch_row(FIRST_ROW)
        later.wq = [
            fetch(wq_h.at[:, 0:128], buf.wq.at[0:3]),
            fetch(wq_h.at[0, 128:192], buf.wq.at[3, 0:64]),
            fetch(wq_h.at[1, 128:192], buf.wq.at[3, 64:128]),
            fetch(wq_h.at[2, 128:192], buf.wq.at[4, 0:64]),
        ]
        later.small = [fetch(seg_h, buf.seg), fetch(small_h[0], buf.bqv)]
        later.small.append(fetch(small_h[1], buf.bup))
        later.small += [fetch(small_h[2 + at], buf.given[at]) for at in range(6)]
        for r in range(rows):
            if r != FIRST_ROW:
                fetch_row(r)
        later.wo = fetch(wo_h, buf.wo.at[me, 0:192])
        later.wu = fetch(wu_h, buf.wu)
        later.wd = fetch(wd_h, buf.wd)
        later.cot = fetch(cot_h.at[:, core], buf.cot)

    def prepare():
        fetch_all()
        buf.wq[4, 64:128] = jnp.zeros((64, 768), BF)
        buf.vs[...] = jnp.zeros((8, 768), F32)
        for copy in later.small:
            copy.wait()
        bias = [[buf.bqv[head, kind : kind + 1, :].astype(F32) for kind in range(2)] for head in range(3)]
        none = jnp.zeros((1, HEAD), F32)
        none2 = jnp.zeros((1, 128), F32)
        for at, pair in enumerate(
            (
                (bias[0][0], bias[1][0]),
                (none, none),
                (bias[0][1], bias[1][1]),
                (bias[2][0], none),
                (bias[2][1], none),
            )
        ):
            vec[0:1, at * 128 : at * 128 + 128] = jnp.concatenate(pair, axis=1)
        vec[0:1, 640:768] = none2
        for at in range(6):
            pair = buf.bup[2 * at : 2 * at + 2, :].astype(F32)
            vec[4:5, at * 128 : at * 128 + 128] = jnp.concatenate([pair[0:1], pair[1:2]], axis=1)
        for at, row in enumerate((1, 2, 3, 5, 6, 7)):
            short = buf.given[at][...].astype(F32)
            for part in range(6):
                vec[row : row + 1, part * 128 : part * 128 + 128] = short[part : part + 1]

    ctx_copies = {}

    def project(r):
        for copy in got_tok[r]:
            copy.wait()
        for copy in later.wq:
            loaded(copy)
        mixed = dot(
            buf.tok[r].reshape(512, 768), buf.wq[...].reshape(640, 768), 1, 1
        ) + vec[0:1, 0:640]
        q_low = mixed[:, 0:128].astype(BF).astype(F32) * SCALE
        buf.mix[r, :, 0:128] = q_low.astype(BF)
        buf.mix[r, :, 128:384] = mixed[:, 128:384].astype(BF)
        tail = mixed[:, 384:512].astype(BF).astype(F32)
        tail = jnp.where(lane_row, tail * SCALE, tail)
        buf.mix[r, :, 384:512] = tail.astype(BF)
        buf.mixr[r] = pltpu.roll(tail, 64, 1).astype(BF)
        buf.mix[r, :, 512:640] = mixed[:, 512:640].astype(BF)

        ids = seg[r : r + 1, :].astype(F32)
        ids = jnp.concatenate(
            [ids[:, 0:128], ids[:, 256:384], ids[:, 128:256], ids[:, 384:512]], axis=1
        )
        column = jnp.broadcast_to(ids, (128, 512)).T
        buf.bias[r] = jnp.where(column[:, 0:1] == ids, 0.0, -1e30)

    def attend(r, h):
        at = pl.ds(h * 256, 256)
        q_a = buf.mix[r, at, 0:128]
        q_b = buf.mix[r, at, 384:512]
        zero = jnp.zeros_like(q_a)
        parts = []
        for head in range(3):
            if head == 1:
                query = jnp.where(low_half, zero, q_a)
            else:
                query = jnp.where(low_half, q_b if head == 2 else q_a, zero)
            key = buf.mixr[r] if head == 2 else buf.mix[r, :, 128:256]
            value = buf.mix[r, :, 512:640] if head == 2 else buf.mix[r, :, 256:384]
            scores = dot(query, key, 1, 1) + buf.bias[r, at, :]
            top = jnp.max(scores, axis=-1, keepdims=True)
            expo = jnp.exp(scores - top)
            probs = expo * (1.0 / jnp.sum(expo, axis=-1, keepdims=True))
            buf.prob[r, head, at, :] = probs
            parts.append(dot(probs.astype(BF), value, 1, 0))
        both = jnp.where(low_half, parts[0], parts[1]).astype(BF)
        buf.ctx[r, at, 0:128] = both
        buf.ctx[r, at, 128:256] = parts[2].astype(BF)
        for part in range(2):
            first = part * 128
            buf.cs[r, h, part, 0:128] = both[first : first + 128]
            buf.cs[r, h, part, 128:192] = jnp.where(
                lane[0:64] < 64,
                parts[2][first : first + 64],
                pltpu.roll(parts[2][first + 64 : first + 128], 64, 1),
            ).astype(BF)

    def send_context(r, h):
        there = buf.cr.at[r, h, me]
        ctx_copies[r, h] = [
            send(buf.cs.at[r, h, core], there, over, (OVER, r, h)),
            send(buf.cs.at[r, h, 1 - core], there, over_mate, (CORNER, r, h)),
            send(buf.cs.at[r, h, 1 - core], there, mate, (PAIR, r, h)),
        ]
        buf.cr[r, h, me] = buf.cs[r, h, core]

    weight_copies = SimpleNamespace()

    def send_weight():
        weight_copies.over = send(wo_h, buf.wo.at[me, 0:192], over, 0)
        weight_copies.mate = send(wo_h, buf.wo.at[me, 0:192], mate, 1)

    def forward_weight():
        weight_copies.over.wait_recv()
        theirs = buf.wo.at[(1 - chip) * 2 + core, 0:192]
        weight_copies.far = send(theirs, theirs, mate, 2)

    def complete_weight():
        later.wo.wait()
        weight_copies.mate.wait_recv()
        weight_copies.far.wait_recv()
        for group in range(4):
            buf.wo[group, 192:256] = buf.wo[group, 128:192]

    flow_copies = {}

    def first_norm(r, h):
        for copy in ctx_copies[r, h]:
            copy.wait_recv()
        total = None
        for group in range(4):
            packed = buf.cr[r, h, group, 128:192]
            zero = jnp.zeros_like(packed)
            keep = lane[0:64] < 64
            left = jnp.concatenate(
                [
                    buf.cr[r, h, group, 0:128],
                    jnp.concatenate(
                        [jnp.where(keep, packed, zero), jnp.where(keep, zero, packed)], axis=0
                    ),
                ],
                axis=1,
            )
            term = dot(left, buf.wo[group], 1, 0).astype(BF).astype(F32)
            total = term if total is None else total + term
        at = pl.ds(h * 128, 128)
        first_in = buf.tok[r, h, core].astype(F32) + total + vec[1:2, :]
        center = first_in - mean_of(first_in)
        scale = lax.rsqrt(mean_of(center * center) + EPS)
        unit = center * scale
        buf.n1[r, at, :] = unit
        buf.r1[r, at, :] = scale
        first_out = unit * vec[2:3, :] + vec[3:4, :]
        buf.fo[r, at, :] = first_out
        buf.flow[r, h, core] = first_out.astype(BF)
        own = buf.flow.at[r, h, core]
        flow_copies[r, h] = send(own, own, mate, (ROWS, r, h))

    pair_copies = {}
    cross_copies = {}

    def ffn_forward(r, h):
        flow_copies[r, h].wait_recv()
        loaded(later.wu)
        loaded(later.wd)
        rows_in = buf.flow[r, h].reshape(256, 768)
        for part in range(3):
            at = pl.ds(part * 256, 256)
            hidden = dot(rows_in, buf.wu[:, at], 1, 0) + vec[4:5, at]
            phi = 0.5 * (1.0 + lax.erf(hidden * 0.7071067811865476))
            buf.act[r, h, :, at] = (hidden * phi).astype(BF)
            buf.gp[r, h, :, at] = (
                phi + hidden * jnp.exp(-0.5 * hidden * hidden) * 0.3989422804014327
            )
        terms = dot(buf.act[r, h], buf.wd[...], 1, 0).astype(BF)
        buf.pair[0][r, h] = terms.reshape(2, 128, 768)
        pair_copies[2, r, h] = send(
            buf.pair[0].at[r, h, 1 - core], buf.paired[0].at[r, h], mate, (PAIR, r, h)
        )

    def exchange(stage, r, h):
        pair_copies[stage, r, h].wait_recv()
        own = buf.pair[stage - 2][r, h, core].astype(F32)
        other = buf.paired[stage - 2][r, h].astype(F32)
        buf.cross[stage - 2][r, h] = (own + other).astype(BF)
        cross_copies[stage, r, h] = send(
            buf.cross[stage - 2].at[r, h],
            buf.crossed[stage - 2].at[r, h],
            over,
            (CROSS if stage == 2 else OVER, r, h),
        )

    def crossed(stage, r, h):
        cross_copies[stage, r, h].wait_recv()
        return buf.cross[stage - 2][r, h].astype(F32) + buf.crossed[stage - 2][r, h].astype(F32)

    dsl_copies = {}

    def second_norm(r, h):
        loaded(later.cot)
        total = crossed(2, r, h)
        at = pl.ds(h * 128, 128)
        second_in = buf.fo[r, at, :] + total + vec[5:6, :]
        center = second_in - mean_of(second_in)
        scale = lax.rsqrt(mean_of(center * center) + EPS)
        unit = center * scale

        @pl.when(chip == r)
        def _():
            layer = unit * vec[6:7, :] + vec[7:8, :]
            outs[0][at, :] = layer.astype(BF)

        grad = buf.cot[r, h].astype(F32)
        scaled = grad * vec[6:7, :]
        d_second = scale * (scaled - mean_of(scaled) - unit * mean_of(scaled * unit))
        buf.ds[r, at, :] = d_second
        buf.dsl[r, h, core] = d_second.astype(BF)
        own = buf.dsl.at[r, h, core]
        dsl_copies[r, h] = send(own, own, mate, (ROWS, r, h))
        buf.vs[0:1, :] += row_sum(grad * unit)
        buf.vs[1:2, :] += row_sum(grad)
        buf.vs[2:3, :] += row_sum(d_second)
        layer_rows.append((r, h))
        if len(layer_rows) == 2 * rows:
            emit(0)

    def ffn_backward(r, h):
        arrive(dsl_copies[r, h])
        rows_in = buf.dsl[r, h].reshape(256, 768)
        for part in range(3):
            at = pl.ds(part * 256, 256)
            d_hidden = dot(rows_in, buf.wd[at, :], 1, 1) * buf.gp[r, h, :, at]
            buf.vs[6:7, at] += row_sum(d_hidden)
            buf.dhl[r, h, :, at] = d_hidden.astype(BF)
        terms = dot(buf.dhl[r, h], buf.wu[...], 1, 1).astype(BF)
        buf.pair[1][r, h] = terms.reshape(2, 128, 768)
        pair_copies[3, r, h] = send(
            buf.pair[1].at[r, h, 1 - core], buf.paired[1].at[r, h], mate, (PAIR, r, h)
        )

    dal_copies = {}

    def first_norm_back(r, h):
        total = crossed(3, r, h)
        at = pl.ds(h * 128, 128)
        d_first = buf.ds[r, at, :] + total
        unit = buf.n1[r, at, :]
        scaled = d_first * vec[2:3, :]
        d_in = buf.r1[r, at, :] * (scaled - mean_of(scaled) - unit * mean_of(scaled * unit))
        buf.dfi[r, at, :] = d_in
        buf.dal[r, h, core] = d_in.astype(BF)
        own = buf.dal.at[r, h, core]
        dal_copies[r, h] = send(own, own, mate, (ROWS, r, h))
        buf.vs[3:4, :] += row_sum(d_first * unit)
        buf.vs[4:5, :] += row_sum(d_first)
        buf.vs[5:6, :] += row_sum(d_in)

    out_parts = []

    halves = []

    def attend_back(r, h):
        arrive(dal_copies[r, h])
        at = pl.ds(h * 256, 256)
        d_ctx = dot(buf.dal[r, h].reshape(256, 768), buf.wo[me], 1, 1).astype(BF)
        turned = buf.mixr[r]
        d_q, d_k, d_v = [], [], []
        for head in range(3):
            tile = d_ctx[:, 0:128] if head < 2 else d_ctx[:, 128:256]
            zero = jnp.zeros_like(tile)
            rows_in = tile
            if head == 0:
                rows_in = jnp.where(low_half, tile, zero)
            if head == 1:
                rows_in = jnp.where(low_half, zero, tile)
            value = buf.mix[r, :, 256:384] if head < 2 else buf.mix[r, :, 512:640]
            probs = buf.prob[r, head, at, :]
            weighted = probs * dot(rows_in, value, 1, 1)
            inner = jnp.sum(weighted, axis=-1, keepdims=True)
            d_scores = (weighted - probs * inner).astype(BF)
            key = buf.mix[r, :, 128:256] if head < 2 else turned
            query = buf.mix[r, at, 0:128] if head < 2 else buf.mixr[r, at, :]
            d_q.append(dot(d_scores, key, 1, 0))
            d_k.append(dot(d_scores, query, 0, 0))
            d_v.append(dot(probs.astype(BF), tile, 0, 0))
        query_rows = jnp.where(low_half, d_q[0], d_q[1]) * SCALE
        buf.dmx[r, at, 0:128] = query_rows.astype(BF)
        vs = buf.vs
        vs[7:8, 0:128] += row_sum(query_rows)
        buf.dq2[at, :] = d_q[2] * SCALE
        sums = [
            jnp.where(lane_row, d_k[0], d_k[1]),
            jnp.where(lane_row, d_v[0], d_v[1]),
            d_k[2],
            d_v[2],
        ]
        halves.append(r)
        if halves.count(r) < 2:
            for part in range(4):
                buf.dkv[part] = sums[part]
            return
        sums = [buf.dkv[part] + sums[part] for part in range(4)]
        tiles = [
            sums[0],
            sums[1],
            jnp.where(lane_row, buf.dq2[...], sums[2]),
            jnp.where(lane_row, sums[3], 0.0),
        ]
        for part, tile in enumerate(tiles):
            lanes = pl.ds(part * 128 + 128, 128)
            buf.dmx[r, :, lanes] = tile.astype(BF)
            if part > 0:
                vs[7:8, lanes] += row_sum(tile)

    tok_copies = []

    def token_terms(r, h):
        terms = dot(
            buf.dmx[r, h * 256 : h * 256 + 256, :], buf.wq[...].reshape(640, 768), 1, 0
        )
        buf.pair[2][r, h] = terms.astype(BF).reshape(2, 128, 768)
        pair_copies[4, r, h] = send(
            buf.pair[2].at[r, h, 1 - core], buf.paired[2].at[r, h], mate, (PAIR, r, h)
        )

    cross4 = []

    def token_way():
        for h in range(2):
            cross4.append(remote(buf.x4.at[h], buf.x4r.at[h], over, (CROSS, 0, h)))

    def token_cross(r, h):
        if not cross4:
            token_way()
        pair_copies[4, r, h].wait_recv()

        @pl.when(chip != r)
        def _():
            own = buf.pair[2][r, h, core].astype(F32)
            other = buf.paired[2][r, h].astype(F32)
            buf.x4[h] = (own + other).astype(BF)
            cross4[h].start()

    def token_finish(h):
        cross4[h].wait_recv()
        own = buf.pair[2][chip, h, core].astype(F32)
        other = buf.paired[2][chip, h].astype(F32)
        pair = (own + other).astype(BF).astype(F32)
        total = pair + buf.x4r[h].astype(F32)
        result = buf.dfi[chip, pl.ds(h * 128, 128), :] + total
        outs[1][h * 128 : h * 128 + 128, :] = result.astype(BF)
        token_rows.append(h)
        if len(token_rows) == 2:
            emit(1)

    steps = {}
    starts = [sum(WIDTHS[:at]) for at in range(len(WIDTHS))]
    finished = []
    pieces = buf.pieces if fused else None

    def reduce_start(name):
        grad = gradient(name)
        width = WIDTHS[name]
        if not fused:
            outs[2][:, starts[name] : starts[name] + width] = grad
            finished.append(name)
            if len(finished) == len(WIDTHS):
                emit(2)
            return
        stage, came = pieces[name][:2]
        stage[...] = grad.astype(BF).reshape(stage.shape)
        if name in DEPTH_FIRST:
            steps[name] = send(stage.at[:, 1 - near], came, next_near, (-1, name))
        else:
            steps[name] = send(stage.at[:, :, 1 - why], came, side, (-1, name))

    def reduce_first(name):
        if not fused:
            return
        steps[name].wait_recv()
        stage, came, out, into = pieces[name][:4]
        if name in DIRECT:
            ways = (
                (far, 1 - near, next_near),
                (1 - far, near, next_far),
                (1 - far, 1 - near, next_both),
            )
            copies = []
            for at, (high, low, device) in enumerate(ways):
                total = stage[high, low, why].astype(F32) + came[high, low].astype(F32)
                out[at] = total.astype(BF)
                copies.append(send(out.at[at], into.at[at], device, (-2 - at, name)))
            steps[name] = copies
            return
        for at in range(2):
            if name in DEPTH_FIRST:
                total = stage[1 - far, near, at].astype(F32) + came[1 - far, at].astype(F32)
            else:
                total = stage[at, 1 - near, why].astype(F32) + came[at, 1 - near].astype(F32)
            out[at] = total.astype(BF)
        steps[name] = send(
            out, into, next_far if name in DEPTH_FIRST else next_near, (-2, name)
        )

    def reduce_second(name):
        if not fused:
            return
        steps[name].wait_recv()
        stage, came, _, into, out, last = pieces[name]
        if name in DEPTH_FIRST:
            total = stage[far, near, 1 - why].astype(F32) + came[far, 1 - why].astype(F32)
            total = total + into[1 - why].astype(F32)
        else:
            total = stage[1 - far, near, why].astype(F32) + came[1 - far, near].astype(F32)
            total = total + into[1 - far].astype(F32)
        out[...] = total.astype(BF)
        steps[name] = send(out, last, side if name in DEPTH_FIRST else next_far, (-3, name))

    def emit(*which):
        for at in which:
            stored.append(fetch(outs[at], results[at], len(stored)))

    def reduce_finish(name):
        if not fused:
            return
        copies = steps[name] if name in DIRECT else [steps[name]]
        for copy in copies:
            copy.wait_recv()
        stage, came, _, into, _, last = pieces[name]
        total = stage[far, near, why].astype(F32)
        if name in DEPTH_FIRST:
            total = total + came[far, why].astype(F32) + into[why].astype(F32)
        elif name in DIRECT:
            total = total + came[far, near].astype(F32)
            for at in range(3):
                total = total + into[at].astype(F32)
        else:
            total = total + came[far, near].astype(F32) + into[far].astype(F32)
        if name not in DIRECT:
            total = total + last[...].astype(F32)
        flipped = None if name <= U2 else total.T
        if name <= D2:
            outs[10][:, starts[name] : starts[name] + 256] = total
        elif name <= U2:
            at = starts[name] - starts[U0]
            outs[8][:, at : at + 256] = total
        elif name == OUT:
            outs[4][0:128, :] = flipped
        elif name == QK:
            outs[2][0:128, :] = flipped[0:128]
            outs[2][192:320, :] = flipped[128:256]
        elif name == V:
            outs[2][384:512, :] = flipped
        elif name == QK2:
            outs[2][128:192, :] = flipped[0:64]
            outs[2][320:384, :] = flipped[64:128]
        else:
            outs[2][512:576, :] = flipped[0:64]
            outs[4][128:192, :] = flipped[64:128]
        before = set(finished)
        finished.append(name)
        after = set(finished)
        for group, at in (
            ({D0, D1, D2}, 10),
            ({U0, U1, U2}, 8),
            ({QK, V, QK2, V2}, 2),
            ({OUT, V2}, 4),
        ):
            if group <= after and not group <= before:
                emit(at)

    def down_grad(part):
        for r in range(rows):
            for h in range(2):
                arrive(dsl_copies[r, h])
        at = pl.ds(part * 256, 256)
        return dot(
            buf.dsl[...].reshape(rows * 512, 768),
            buf.act[:, :, :, at].reshape(rows * 512, 256),
            0,
            0,
        )

    def up_grad(part):
        at = pl.ds(part * 256, 256)
        return dot(
            buf.flow[...].reshape(rows * 512, 768),
            buf.dhl[:, :, :, at].reshape(rows * 512, 256),
            0,
            0,
        )

    def all_back():
        for r in range(rows):
            for h in range(2):
                arrive(dal_copies[r, h])

    def out_grad_first():
        all_back()
        return dot(
            buf.dal[...].reshape(rows * 512, 768),
            buf.ctx[:, :, 0:128].reshape(rows * 512, 128),
            0,
            0,
        )

    def out_grad_second():
        all_back()
        turned = dot(
            buf.dal[...].reshape(rows * 512, 768),
            buf.ctx[:, :, 128:256].reshape(rows * 512, 128),
            0,
            0,
        )
        return pltpu.roll(turned, 64, 1)

    def qkv_grad(low, high):
        return dot(
            buf.tok[...].reshape(rows * 512, 768),
            buf.dmx[:, :, low:high].reshape(rows * 512, high - low),
            0,
            0,
        )

    def gradient(name):
        if name <= D2:
            return down_grad(name)
        if name <= U2:
            return up_grad(name - U0)
        if name == OUT:
            return out_grad_first()
        if name == QK:
            return qkv_grad(0, 256)
        if name == V:
            return qkv_grad(256, 384)
        if name == QK2:
            return qkv_grad(384, 512)
        first = lax.broadcasted_iota(jnp.int32, (768, 128), 1) < 64
        return jnp.where(first, qkv_grad(512, 640), out_grad_second())

    small_copies = SimpleNamespace()

    def small_mate():
        small_copies.mate = send(buf.vs, buf.vm, mate, 3)

    def small_side():
        small_copies.mate.wait_recv()
        shared = lax.broadcasted_iota(jnp.int32, (8, 768), 0) < 6
        small = buf.vs[...] + jnp.where(shared, buf.vm[...], 0.0)
        if not fused:
            outs[3][...] = small
            emit(3)
            return
        buf.small[0][...] = small
        small_copies.side = send(buf.small[0], buf.small[1], side, 4)

    def small_near():
        if not fused:
            return
        small_copies.side.wait_recv()
        buf.small[2][...] = buf.small[0][...] + buf.small[1][...]
        small_copies.near = send(buf.small[2], buf.small[3], next_near, 5)

    def small_far():
        if not fused:
            return
        small_copies.near.wait_recv()
        buf.small[4][...] = buf.small[2][...] + buf.small[3][...]
        small_copies.far = send(buf.small[4], buf.small[5], next_far, 6)

    def small_finish():
        if not fused:
            return
        small_copies.far.wait_recv()
        small = buf.small[4][...] + buf.small[5][...]
        share = 768 // n_dp
        turned = pltpu.roll(small, 768 - dp * share, 1)
        for row, at in ((5, 5), (3, 6), (4, 7), (2, 11), (0, 12), (1, 13)):
            outs[at][...] = turned[row : row + 1, 0:share]
        wide = HEAD // n_dp
        lanes = lax.broadcasted_iota(jnp.int32, (8, 768), 1)
        depth = lax.broadcasted_iota(jnp.int32, (8, 768), 0)
        spread = jnp.where(lax.rem(lanes, HEAD) == depth + dp * wide, small[6:7, :], 0.0)
        group = lax.broadcasted_iota(jnp.int32, (768, 128), 0) // HEAD
        pick = (group == lax.broadcasted_iota(jnp.int32, (768, 128), 1)).astype(F32)
        outs[9][...] = jnp.dot(spread, pick, precision=lax.Precision.HIGHEST)[0:wide, 0:12]
        group = lanes // HEAD
        where = jnp.where(
            depth < 4,
            lax.rem(depth, 2) * 4 + depth // 2,
            jnp.where(depth == 4, 6, 8),
        )
        spread = jnp.where((group == where) & (depth < 6), small[7:8, :], 0.0)
        inside = lax.rem(lax.broadcasted_iota(jnp.int32, (768, 128), 0), HEAD)
        pick = (inside == lax.broadcasted_iota(jnp.int32, (768, 128), 1) + dp * wide).astype(F32)
        heads = jnp.dot(spread, pick, precision=lax.Precision.HIGHEST)
        for head in range(3):
            outs[3][head] = heads[head * 2 : head * 2 + 2, 0:wide]
        emit(3, 5, 6, 7, 9, 11, 12, 13)

    pl.semaphore_wait(barrier, len(partners))
    send_weight()
    prepare()
    project(0)
    attend(0, 1)
    send_context(0, 1)
    project(1)
    attend(1, 0)
    attend(1, 1)
    send_context(1, 1)
    forward_weight()
    attend(0, 0)
    send_context(0, 0)
    send_context(1, 0)
    complete_weight()
    first_norm(0, 1)
    ffn_forward(0, 1)
    first_norm(1, 1)
    exchange(2, 0, 1)
    first_norm(0, 0)
    ffn_forward(1, 1)
    ffn_forward(0, 0)
    first_norm(1, 0)
    exchange(2, 1, 1)
    exchange(2, 0, 0)
    ffn_forward(1, 0)
    second_norm(0, 1)
    exchange(2, 1, 0)
    ffn_backward(0, 1)
    exchange(3, 0, 1)
    second_norm(1, 1)
    ffn_backward(1, 1)
    second_norm(0, 0)
    exchange(3, 1, 1)
    ffn_backward(0, 0)
    exchange(3, 0, 0)
    second_norm(1, 0)
    reduce_start(D0)
    reduce_start(D1)
    reduce_start(D2)
    ffn_backward(1, 0)
    reduce_start(U2)
    first_norm_back(0, 1)
    reduce_start(U0)
    reduce_start(U1)
    exchange(3, 1, 0)
    first_norm_back(1, 1)
    reduce_first(D0)
    reduce_first(D1)
    attend_back(0, 1)
    first_norm_back(0, 0)
    reduce_first(U2)
    reduce_first(D2)
    attend_back(0, 0)
    attend_back(1, 1)
    first_norm_back(1, 0)
    reduce_second(D1)
    token_terms(0, 1)
    reduce_second(D0)
    token_terms(0, 0)
    reduce_first(U0)
    reduce_start(OUT)
    attend_back(1, 0)
    reduce_second(D2)
    reduce_start(V2)
    small_mate()
    token_cross(0, 1)
    token_cross(0, 0)
    small_side()
    reduce_start(QK)
    reduce_first(U1)
    reduce_finish(D0)
    reduce_start(V)
    reduce_finish(D1)
    reduce_second(U2)
    reduce_first(OUT)
    reduce_start(QK2)
    token_terms(1, 1)
    reduce_second(U0)
    token_terms(1, 0)
    reduce_first(V2)
    small_near()
    token_cross(1, 1)
    reduce_finish(D2)
    token_cross(1, 0)
    reduce_second(U1)
    reduce_second(OUT)
    reduce_first(QK)
    reduce_second(V2)
    small_far()
    reduce_finish(U0)
    reduce_first(V)
    token_finish(1)
    reduce_finish(U1)
    reduce_finish(U2)
    reduce_finish(OUT)
    reduce_second(QK)
    reduce_first(QK2)
    reduce_second(V)
    token_finish(0)
    reduce_finish(V2)
    small_finish()
    reduce_second(QK2)
    reduce_finish(QK)
    reduce_finish(V)
    reduce_finish(QK2)
    for copy in latest.values():
        copy.wait_send()
    for copy in stored:
        copy.wait()


def body(
    tokens,
    segment_ids,
    qkv_weight,
    qkv_bias,
    output_weight,
    output_bias,
    first_gain,
    first_shift,
    up_weight,
    up_bias,
    down_weight,
    down_bias,
    second_gain,
    second_shift,
    cotangent,
):
    rows = tokens.shape[0] // SEQ
    n_dp = lax.axis_size("dp")
    share = 768 // n_dp
    fused = n_dp == 8
    split = (rows, 2, 2, 128, 768)
    shape = jax.ShapeDtypeStruct
    outs = [shape((256, 768), BF), shape((256, 768), BF)]
    if fused:
        wide = HEAD // n_dp
        vector = shape((1, share), F32)
        outs += [
            shape((576, share), F32),
            shape((3, 2, wide), F32),
            shape((192, share), F32),
            vector,
            vector,
            vector,
            shape((share, 768), F32),
            shape((wide, 12), F32),
            shape((share, 768), F32),
            vector,
            vector,
            vector,
        ]
    else:
        outs += [shape((768, 2304), F32), shape((8, 768), F32)]
    plan = scratch_plan(rows, share, fused, outs)
    leaves, tree = jax.tree.flatten(plan, is_leaf=is_buffer)
    anywhere = pl.BlockSpec(memory_space=pl.ANY)

    def kernel(*refs):
        layer_kernel(rows, n_dp, fused, tree, *refs)

    got = pl.pallas_call(
        kernel,
        out_shape=outs,
        in_specs=[anywhere] * INPUTS,
        out_specs=[anywhere] * len(outs),
        scratch_shapes=[pltpu.VMEM(dims, kind) for dims, kind in leaves]
        + [
            pltpu.SemaphoreType.DMA((LOCAL_COPIES,)),
            pltpu.SemaphoreType.DMA((REMOTE_COPIES,)),
            pltpu.SemaphoreType.DMA((REMOTE_COPIES,)),
        ],
        compiler_params=pltpu.CompilerParams(
            collective_id=0, has_side_effects=True, vmem_limit_bytes=62 * 1024 * 1024
        ),
    )(
        tokens.reshape(split),
        cotangent.reshape(split),
        qkv_weight.transpose(1, 2, 3, 0).reshape(3, 192, 768),
        output_weight.reshape(192, 768),
        up_weight,
        down_weight,
        segment_ids,
        qkv_bias.transpose(1, 0, 2),
        up_bias,
        *(
            vector.reshape(6, 128)
            for vector in (
                output_bias,
                first_gain,
                first_shift,
                down_bias,
                second_gain,
                second_shift,
            )
        ),
    )
    if fused:
        got = hand_over(got)
    else:
        got = finish_plain(n_dp, *got)
    return (
        got[0],
        got[1],
        got[2].reshape(3, 3, HEAD, share).transpose(3, 0, 1, 2),
        got[3].transpose(1, 0, 2),
        got[4].reshape(3, HEAD, share),
        got[5].reshape(share),
        got[6].reshape(share),
        got[7].reshape(share),
        got[8],
        got[9].T,
        got[10].T,
        got[11].reshape(share),
        got[12].reshape(share),
        got[13].reshape(share),
    )


def hand_over(arrays):
    count = len(arrays)

    def kernel(*refs):
        source, result, held = (refs[at * count : at * count + count] for at in range(3))
        sem = refs[3 * count]
        inward = [
            pltpu.make_async_copy(source[at], held[at], sem.at[at]) for at in range(count)
        ]
        outward = [
            pltpu.make_async_copy(held[at], result[at], sem.at[count + at]) for at in range(count)
        ]
        for copy in inward:
            copy.start()
        for before, after in zip(inward, outward):
            before.wait()
            after.start()
        for copy in outward:
            copy.wait()

    anywhere = pl.BlockSpec(memory_space=pl.ANY)
    return pl.pallas_call(
        kernel,
        out_shape=[jax.ShapeDtypeStruct(a.shape, a.dtype) for a in arrays],
        in_specs=[anywhere] * count,
        out_specs=[anywhere] * count,
        scratch_shapes=[pltpu.VMEM(a.shape, a.dtype) for a in arrays]
        + [pltpu.SemaphoreType.DMA((2 * count,))],
    )(*arrays)


def finish_plain(n_dp, layer, tokens_grad, grads, small):
    share = 768 // n_dp
    grads = lax.psum_scatter(grads, "dp", scatter_dimension=0, tiled=True)
    small = lax.psum(small, "dp")
    dp = lax.axis_index("dp")
    wide = HEAD // n_dp
    turned = lax.dynamic_slice_in_dim(small, dp * share, share, 1)
    up_bias = lax.dynamic_slice_in_dim(small[6].reshape(12, HEAD), dp * wide, wide, 1)
    row = small[7]
    sums = jnp.stack(
        [row[0:64], row[256:320], row[64:128], row[320:384], row[384:448], row[512:576]]
    )
    sums = lax.dynamic_slice_in_dim(sums, dp * wide, wide, 1)
    down, up = grads[:, 0:768], grads[:, 768:1536]
    out_a, main, tail = grads[:, 1536:1664], grads[:, 1664:2048], grads[:, 2048:2304]
    qkv = jnp.concatenate(
        [
            main[:, 0:128],
            tail[:, 0:64],
            main[:, 128:256],
            tail[:, 64:128],
            main[:, 256:384],
            tail[:, 128:192],
        ],
        axis=1,
    )
    out = jnp.concatenate([out_a, tail[:, 192:256]], axis=1)
    return [
        layer,
        tokens_grad,
        qkv.T,
        sums.reshape(3, 2, wide),
        out.T,
        turned[5],
        turned[3],
        turned[4],
        up,
        up_bias.T,
        down,
        turned[2],
        turned[0],
        turned[1],
    ]


def solution(mesh):
    placed = (
        P("dp", None),
        P("dp", None),
        P(None, None, "tensor", None),
        P(None, "tensor", None),
        P("tensor", None, None),
        P(),
        P(),
        P(),
        P(None, "tensor"),
        P("tensor", None),
        P("tensor", None),
        P(),
        P(),
        P(),
        P("dp", None),
    )
    return jax.shard_map(
        body,
        mesh=mesh,
        in_specs=placed,
        out_specs=(
            P(("dp", "tensor"), None),
            P(("dp", "tensor"), None),
            P("dp", None, "tensor", None),
            P(None, "tensor", "dp"),
            P("tensor", None, "dp"),
            P("dp"),
            P("dp"),
            P("dp"),
            P("dp", "tensor"),
            P("tensor", "dp"),
            P("tensor", "dp"),
            P("dp"),
            P("dp"),
            P("dp"),
        ),
        check_vma=False,
    )
```
